32 devices in a mesh: items: 8 (over y, x, core), mem: 4 (over z).
Axes of the slice: x: 2, y: 2, z: 4, core: 2. Of those that a mesh axis runs over, the one named last changes fastest.
Arguments:
- tokens: bfloat16 [8192, 1024], P(('items', 'mem')), may hold values from -6 to 6
- memory: bfloat16 [64, 1024, 1024], P('items', 'mem'), may hold values from -6 to 6
- cotangent: bfloat16 [8192, 1024], P(('items', 'mem')), may hold values from -6 to 6
- mem_len: int32 [64], P('items'), may hold values from 128 to 1024, as said below
- dec_len: int32 [64], P('items'), may hold values from 32 to 128, as said below
- self_query: bfloat16 [1024, 1024], P('items', 'mem'), may hold values from -0.1875 to 0.1875
- self_key: bfloat16 [1024, 1024], P('items', 'mem'), may hold values from -0.1875 to 0.1875
- self_value: bfloat16 [1024, 1024], P('items', 'mem'), may hold values from -0.1875 to 0.1875
- self_out: bfloat16 [1024, 1024], P('items', 'mem'), may hold values from -0.875 to 0.875
- cross_query: bfloat16 [1024, 1024], P('items', 'mem'), may hold values from -0.1875 to 0.1875
- cross_key: bfloat16 [1024, 1024], P('items', 'mem'), may hold values from -0.1875 to 0.1875
- cross_value: bfloat16 [1024, 1024], P('items', 'mem'), may hold values from -0.1875 to 0.1875
- cross_out: bfloat16 [1024, 1024], P('items', 'mem'), may hold values from -3.5 to 3.5
- feed_in: bfloat16 [1024, 4096], P('items', 'mem'), may hold values from -0.1875 to 0.1875
- feed_out: bfloat16 [4096, 1024], P('items', 'mem'), may hold values from -0.09375 to 0.09375
- shifts: bfloat16 [10, 1024], P(None, 'items'), may hold values from -3 to 3
- gains: bfloat16 [3, 1024], P(None, 'items'), may hold values from 0.5 to 1.5
- inner_bias: bfloat16 [4096], P('items'), may hold values from -3 to 3
Outputs:
- layer_out: float32 [8192, 1024], P(('items', 'mem'))
- tokens_grad: float32 [8192, 1024], P(('items', 'mem'))
- memory_grad: float32 [64, 1024, 1024], P('items', 'mem')
- self_query_grad: float32 [1024, 1024], P('items', 'mem')
- self_key_grad: float32 [1024, 1024], P('items', 'mem')
- self_value_grad: float32 [1024, 1024], P('items', 'mem')
- self_out_grad: float32 [1024, 1024], P('items', 'mem')
- cross_query_grad: float32 [1024, 1024], P('items', 'mem')
- cross_key_grad: float32 [1024, 1024], P('items', 'mem')
- cross_value_grad: float32 [1024, 1024], P('items', 'mem')
- cross_out_grad: float32 [1024, 1024], P('items', 'mem')
- feed_in_grad: float32 [1024, 4096], P('items', 'mem')
- feed_out_grad: float32 [4096, 1024], P('items', 'mem')
- shifts_grad: float32 [10, 1024], P(None, 'items')
- gains_grad: float32 [3, 1024], P(None, 'items')
- inner_bias_grad: float32 [4096], P('items')
The draws below stay inside these ranges and needn't reach their ends.
Inputs may be any that keep to these rules, and one draw needn't show every extreme that they name: Memory slots below mem_len[i] hold item i's encoded table and question; the rest are padding. Decoder positions at or above dec_len[i] are padding that no query attends to.
All inputs are finite; a program needn't handle non-finite values.
Results may differ from the reference program's by a relative error of at most 0.03.
Values may be sent and summed in bfloat16 or wider, within the bound.
A program may use at most 256 MiB of HBM per device.

```python
import jax
import jax.numpy as jnp
from jax import lax

D = 1024
HEADS = 16
HEAD_DIM = 64
FF = 4096
DEC = 128
MEM = 1024
ITEMS_G = 8
SHIFT_ROWS = 10
GAIN_ROWS = 3
ITEMS = 64
TOKENS = 8192
N_ITEMS = 8


def ragged_lengths(key, total_items, low_end, high_end):
    key_base, key_top, key_step = jax.random.split(key, 3)
    lengths = jax.random.randint(key_base, (total_items,), low_end, high_end + 1)
    top_spot = jax.random.randint(key_top, (), 0, total_items)
    step_size = jax.random.randint(key_step, (), 1, total_items)
    bottom_spot = (top_spot + step_size) % total_items
    lengths = lengths.at[top_spot].set(high_end)
    lengths = lengths.at[bottom_spot].set(low_end)
    return lengths.astype(jnp.int32)


def draw_mem_len(key, part):
    return ragged_lengths(jax.random.fold_in(key, 17), ITEMS, MEM // 8, MEM)


def draw_dec_len(key, part):
    return ragged_lengths(jax.random.fold_in(key, 29), ITEMS, DEC // 4, DEC)


def level_of(rng, shape, shards, low, largest):
    level, own = 1.0, jax.random.fold_in(rng, 6)
    for dim, shards_of in shards:
        heights = jnp.exp(jax.random.uniform(jax.random.fold_in(own, dim), (shards_of,), jnp.float32, low / len(shards), largest / len(shards)))
        level = level * jnp.repeat(heights, shape[dim] // shards_of).reshape([-1 if axis == dim else 1 for axis in range(len(shape))])
    return level


def centred(key, dims, width, reach, shards=(), dtype=jnp.bfloat16):
    loudness = level_of(key, dims, shards, -0.22, 0.18) if shards else 1.0
    values = jax.random.normal(key, dims, jnp.float32) * width * loudness
    return jnp.minimum(jnp.maximum(values, -reach), reach).astype(dtype)


def setup_inputs(seed: int = 0) -> dict:
    splits = jax.random.split(jax.random.key(seed), 19)
    tokens = centred(splits[0], (TOKENS, D), 1.0, 6.0, ((0, 32),))
    memory = centred(splits[1], (ITEMS, MEM, D), 1.0, 6.0, ((0, 8), (1, 4)))
    cotangent = centred(splits[2], (TOKENS, D), 1.0, 6.0, ((0, 32),))
    mem_len = draw_mem_len(jax.random.fold_in(splits[18], 71), 0)
    dec_len = draw_dec_len(jax.random.fold_in(splits[18], 71), 0)
    self_query = centred(splits[5], (D, D), D ** -0.5, 0.1875, ((0, 8), (1, 4)))
    self_key = centred(splits[6], (D, D), D ** -0.5, 0.1875, ((0, 8), (1, 4)))
    self_value = centred(splits[7], (D, D), D ** -0.5, 0.1875, ((0, 8), (1, 4)))
    self_out = centred(splits[8], (D, D), (max(6 * D // DEC, 1)) ** -0.5, 0.875, ((0, 8), (1, 4)))
    cross_query = centred(splits[9], (D, D), D ** -0.5, 0.1875, ((0, 8), (1, 4)))
    cross_key = centred(splits[10], (D, D), D ** -0.5, 0.1875, ((0, 8), (1, 4)))
    cross_value = centred(splits[11], (D, D), D ** -0.5, 0.1875, ((0, 8), (1, 4)))
    cross_out = centred(splits[12], (D, D), (max(3 * D // MEM, 1)) ** -0.5, 3.5, ((0, 8), (1, 4)))
    feed_in = centred(splits[13], (D, FF), D ** -0.5, 0.1875, ((0, 8), (1, 4)))
    feed_out = centred(splits[14], (FF, D), FF ** -0.5, 0.09375, ((0, 8), (1, 4)))
    shifts = centred(splits[15], (SHIFT_ROWS, D), 0.5, 3.0, ((1, 8),))
    gains = jnp.clip(1.0 + 0.1 * jax.random.normal(splits[16], (GAIN_ROWS, D), jnp.float32), 0.5, 1.5).astype(jnp.bfloat16)
    inner_bias = centred(splits[17], (FF,), 0.5, 3.0, ((0, 8),))
    return dict(tokens=tokens, memory=memory, cotangent=cotangent, mem_len=mem_len, dec_len=dec_len, self_query=self_query, self_key=self_key, self_value=self_value, self_out=self_out, cross_query=cross_query, cross_key=cross_key, cross_value=cross_value, cross_out=cross_out, feed_in=feed_in, feed_out=feed_out, shifts=shifts, gains=gains, inner_bias=inner_bias)


precise = lax.Precision.HIGHEST

@jax.custom_vjp
def low(v):
    return lax.optimization_barrier(v.astype(jnp.bfloat16)).astype(jnp.float32)

@jax.custom_vjp
def low_back(v):
    return v

def low_keep(v):
    return (low(v), None)

def low_pass(kept, grad):
    return (grad,)

def back_keep(v):
    return (v, None)

def back_low(kept, grad):
    return (low(grad),)
low.defvjp(low_keep, low_pass)
low_back.defvjp(back_keep, back_low)

def matmul(first_op, second_op):
    return jnp.dot(first_op, second_op, precision=precise)

def layer_norm(values, gain, shift):
    center = values - lax.optimization_barrier(jnp.mean(values, -1, keepdims=True))
    spread = lax.optimization_barrier(jnp.mean(center * center, -1, keepdims=True))
    return center * lax.rsqrt(spread + 1e-05) * gain + shift

def gelu_exact(values):
    return 0.5 * values * (1.0 + jax.scipy.special.erf(values * 0.7071067811865476))

def rounded_both(values):
    return low(low_back(values))

def heads_of(values, item_count):
    return values.reshape(item_count, -1, HEADS, HEAD_DIM)

def forward_block(params, tokens_in, memory_in, mem_valid, dec_valid):
    query_self, key_self, value_self, output_self, query_cross, key_cross, value_cross, output_cross, feed_up, feed_down, shift_rows, gain_rows, inner_shift = params
    item_count = memory_in.shape[0]
    row_count = tokens_in.shape[0]
    queries_one = rounded_both((matmul(tokens_in, query_self) + shift_rows[0]) * 0.125)
    keys_one = rounded_both(matmul(tokens_in, key_self))
    values_one = rounded_both(matmul(tokens_in, value_self) + shift_rows[1])
    position = jnp.arange(DEC)
    allowed_one = (position[None, None, :] <= position[None, :, None]) & (position[None, None, :] < dec_valid[:, None, None])
    scores_one = low_back(jnp.einsum('iqhd,ikhd->ihqk', heads_of(queries_one, item_count), heads_of(keys_one, item_count), precision=precise))
    exp_one = jnp.where(allowed_one[:, None], jnp.exp(scores_one), 0.0)
    total_one = jnp.transpose(lax.optimization_barrier(jnp.sum(exp_one, -1)), (0, 2, 1))
    numer_one = low_back(jnp.einsum('ihqk,ikhd->iqhd', low(exp_one), heads_of(values_one, item_count), precision=precise))
    mixed_one = low((numer_one / total_one[..., None]).reshape(row_count, D))
    branch_one = low_back(matmul(mixed_one, output_self) + shift_rows[2])
    hidden_one = layer_norm(tokens_in + branch_one, gain_rows[0], shift_rows[7])
    queries_two = rounded_both((matmul(low(hidden_one), query_cross) + shift_rows[3]) * 0.125)
    memory_rows = memory_in.reshape(-1, D)
    keys_two = rounded_both(matmul(memory_rows, key_cross))
    values_two = rounded_both(matmul(memory_rows, value_cross) + shift_rows[4])
    allowed_two = (jnp.arange(MEM)[None, :] < mem_valid[:, None])[:, None, :]
    scores_two = low_back(jnp.einsum('iqhd,ikhd->ihqk', heads_of(queries_two, item_count), heads_of(keys_two, item_count), precision=precise))
    exp_two = jnp.where(allowed_two[:, None], jnp.exp(scores_two), 0.0)
    total_two = low_back(jnp.transpose(lax.optimization_barrier(jnp.sum(exp_two, -1)), (0, 2, 1)))
    numer_two = low_back(jnp.einsum('ihqk,ikhd->iqhd', low(exp_two), heads_of(values_two, item_count), precision=precise))
    mixed_two = low((numer_two / total_two[..., None]).reshape(row_count, D))
    branch_two = low_back(matmul(mixed_two, output_cross) + shift_rows[5])
    hidden_two = layer_norm(hidden_one + branch_two, gain_rows[1], shift_rows[8])
    inner_pre = low_back(matmul(low(hidden_two), feed_up) + inner_shift)
    branch_three = low_back(matmul(low(gelu_exact(inner_pre)), feed_down) + shift_rows[6])
    return layer_norm(hidden_two + branch_three, gain_rows[2], shift_rows[9])

def reference(tokens, memory, cotangent, mem_len, dec_len, self_query, self_key, self_value, self_out, cross_query, cross_key, cross_value, cross_out, feed_in, feed_out, shifts, gains, inner_bias):
    weights = tuple((weight_arr.astype(jnp.float32) for weight_arr in (self_query, self_key, self_value, self_out, cross_query, cross_key, cross_value, cross_out, feed_in, feed_out, shifts, gains, inner_bias)))
    token_blocks = tokens.reshape(N_ITEMS, ITEMS_G * DEC, D)
    memory_blocks = memory.reshape(N_ITEMS, ITEMS_G, MEM, D)
    cot_blocks = cotangent.reshape(N_ITEMS, ITEMS_G * DEC, D)
    mem_blocks_len = mem_len.reshape(N_ITEMS, ITEMS_G)
    dec_blocks_len = dec_len.reshape(N_ITEMS, ITEMS_G)

    def one_block(grad_total, pieces):
        token_piece, memory_piece, cot_piece, mem_piece_len, dec_piece_len = pieces

        def closed(weight_set, token_float, memory_float):
            return forward_block(weight_set, token_float, memory_float, mem_piece_len, dec_piece_len)
        result, pullback = jax.vjp(closed, weights, token_piece.astype(jnp.float32), memory_piece.astype(jnp.float32))
        weight_grads, token_grad, memory_grad = pullback(cot_piece.astype(jnp.float32))
        return (jax.tree.map(jnp.add, grad_total, weight_grads), (result, token_grad, memory_grad))
    initial = jax.tree.map(jnp.zeros_like, weights)
    totals, (outputs, token_grads, memory_grads) = lax.scan(one_block, initial, (token_blocks, memory_blocks, cot_blocks, mem_blocks_len, dec_blocks_len))
    grad_sq, grad_sk, grad_sv, grad_so, grad_cq, grad_ck, grad_cv, grad_co, grad_fi, grad_fo, grad_sh, grad_ga, grad_ib = totals
    return (outputs.reshape(TOKENS, D), token_grads.reshape(TOKENS, D), memory_grads.reshape(ITEMS, MEM, D), grad_sq, grad_sk, grad_sv, grad_so, grad_cq, grad_ck, grad_cv, grad_co, grad_fi, grad_fo, grad_sh, grad_ga, grad_ib)
```

```python
import functools

import jax
import jax.numpy as jnp
from jax import lax
from jax.experimental import pallas as pl
from jax.experimental.pallas import tpu as pltpu
from jax.sharding import PartitionSpec as P

D = 1024
HEADS = 16
HEAD_DIM = 64
PAIR = 2 * HEAD_DIM
PAIRS = HEADS // 2
DEC = 128
half_root = 0.7071067811865476
normal_peak = 0.3989422804014327
MESH = pl.DeviceIdType.MESH
F32 = jnp.float32
BF16 = jnp.bfloat16
ANY = pl.BlockSpec(memory_space=pl.ANY)


def product(first_op, second_op):
    return jnp.dot(first_op, second_op, preferred_element_type=F32)


def left_product(first_op, second_op):
    return lax.dot_general(
        first_op, second_op, (((0,), (0,)), ((), ())), preferred_element_type=F32
    )


def right_product(first_op, second_op):
    return lax.dot_general(
        first_op, second_op, (((1,), (1,)), ((), ())), preferred_element_type=F32
    )


def column_sums(values):
    return jnp.sum(values.astype(F32), 0)


def norm_forward(values, gain, shift):
    center = values - jnp.mean(values, -1, keepdims=True)
    inverse = lax.rsqrt(jnp.mean(center * center, -1, keepdims=True) + 1e-05)
    normed = center * inverse
    return (normed * gain + shift, normed, inverse)


def norm_backward(grad_out, normed, inverse, gain):
    scaled = grad_out * gain
    grad_in = inverse * (
        scaled
        - jnp.mean(scaled, -1, keepdims=True)
        - normed * jnp.mean(scaled * normed, -1, keepdims=True)
    )
    return (grad_in, jnp.sum(grad_out * normed, 0), jnp.sum(grad_out, 0))


def gather_kernel(members, items_here, units, *refs):
    count = len(units)
    weights = 1 + max(unit[0] for unit in units)
    shard_refs, memory_ref = refs[:weights], refs[weights]
    whole_refs, items_ref = refs[weights + 1 : 2 * weights + 1], refs[2 * weights + 1]
    send_sem, recv_sem, copy_sem, mem_send, mem_recv, mem_copy = refs[2 * weights + 2 :]
    row = lax.axis_index("items")
    member = lax.axis_index("mem")
    hops = members - 1
    core_peer, first_peer, second_peer = row ^ 1, row ^ 2, row ^ 4
    UP, DOWN = 0, hops
    ALONG_X, ALONG_Y, HALF_A, HALF_B, CORE = 2 * hops, 2 * hops + 1, 2 * hops + 2, 2 * hops + 3, 2 * hops + 4

    barrier = pltpu.get_barrier_semaphore()
    partners = [(core_peer, member), (first_peer, member), (second_peer, member)]
    partners += [(row, lax.rem(member + step, members)) for step in range(1, members)]
    for partner in partners:
        pl.semaphore_signal(barrier, inc=1, device_id=partner, device_id_type=MESH)
    pl.semaphore_wait(barrier, len(partners))

    def place(unit, owner):
        weight, start, depth, height = units[unit]
        return pl.ds(pl.multiple_of(owner * height + start, depth), depth)

    def cols(unit, who):
        width = shard_refs[units[unit][0]].shape[1]
        return pl.ds(pl.multiple_of(who * width, width), width)

    def shard(unit):
        weight, start, depth, height = units[unit]
        return shard_refs[weight].at[pl.ds(start, depth)]

    def remote(unit, kind, src, dst, device):
        return pltpu.make_async_remote_copy(
            src_ref=src,
            dst_ref=dst,
            send_sem=send_sem.at[unit, kind],
            recv_sem=recv_sem.at[unit, kind],
            device_id=device,
            device_id_type=MESH,
        )

    def along(unit, hop, upward):
        whole = whole_refs[units[unit][0]]
        origin = member - hop if upward else member + hop
        origin = jnp.clip(origin, 0, members - 1)
        piece = whole.at[place(unit, row), cols(unit, origin)]
        target = jnp.clip(member + 1 if upward else member - 1, 0, members - 1)
        return remote(
            unit, (UP if upward else DOWN) + hop, shard(unit) if hop == 0 else piece, piece, (row, target)
        )

    def along_start(unit, hop):
        @pl.when((member >= hop) & (member < members - 1))
        def _():
            along(unit, hop, True).start()

        @pl.when((member <= members - 1 - hop) & (member > 0))
        def _():
            along(unit, hop, False).start()

    def along_arrive(unit, hop):
        @pl.when(member >= hop + 1)
        def _():
            along(unit, hop, True).wait_recv()

        @pl.when(member <= members - 2 - hop)
        def _():
            along(unit, hop, False).wait_recv()

    def along_sent(unit, hop):
        @pl.when((member >= hop) & (member < members - 1))
        def _():
            along(unit, hop, True).wait_send()

        @pl.when((member <= members - 1 - hop) & (member > 0))
        def _():
            along(unit, hop, False).wait_send()

    def own_copy(unit):
        return pltpu.make_async_copy(
            shard(unit), whole_refs[units[unit][0]].at[place(unit, row), cols(unit, member)], copy_sem.at[unit]
        )

    def block(unit, kind, owner, device, half=None):
        weight, start, depth, height = units[unit]
        if half is None:
            rows = place(unit, owner)
        else:
            part = depth // 2
            rows = pl.ds(pl.multiple_of(owner * height + start + half * part, part), part)
        ref = whole_refs[weight].at[rows]
        return remote(unit, kind, ref, ref, (device, member))

    def to_x(unit):
        return block(unit, ALONG_X, row, first_peer)

    def to_y(unit):
        return block(unit, ALONG_Y, row, second_peer)

    def half_a(unit):
        return block(unit, HALF_A, first_peer, second_peer, 0)

    def half_b(unit):
        return block(unit, HALF_B, second_peer, first_peer, 1)

    def to_core(unit, which):
        owner = (row, first_peer, second_peer, row ^ 6)[which]
        return block(unit, CORE + which, owner, core_peer)

    pieces = memory_ref.shape[1] // 32 * items_here

    def memory_send(piece, step):
        which, start = piece // (pieces // items_here), piece % (pieces // items_here) * 32
        target = lax.rem(member + step, members)
        return pltpu.make_async_remote_copy(
            src_ref=memory_ref.at[target * items_here + which, pl.ds(start, 32)],
            dst_ref=items_ref.at[which, step, pl.ds(start, 32)],
            send_sem=mem_send.at[piece, step],
            recv_sem=mem_recv.at[piece, step],
            device_id=(row, target),
            device_id_type=MESH,
        )

    local = pltpu.make_async_copy(
        memory_ref.at[pl.ds(member * items_here, items_here)], items_ref.at[:, 0], mem_copy
    )
    local.start()

    depth_ticks = hops + 3
    for tick in range(max(count + depth_ticks, pieces)):
        unit = tick
        if unit < count:
            along_start(unit, 0)
            own_copy(unit).start()
        if tick < pieces:
            for step in range(1, members):
                memory_send(tick, step).start()
        for hop in range(1, hops):
            unit = tick - hop
            if 0 <= unit < count:
                along_arrive(unit, hop - 1)
                along_start(unit, hop)
        unit = tick - hops
        if 0 <= unit < count:
            along_arrive(unit, hops - 1)
            own_copy(unit).wait()
            to_x(unit).start()
            to_y(unit).start()
            to_core(unit, 0).start()
        unit = tick - hops - 1
        if 0 <= unit < count:
            to_x(unit).wait_recv()
            half_a(unit).start()
            to_core(unit, 1).start()
            to_y(unit).wait_recv()
            half_b(unit).start()
            to_core(unit, 2).start()
        unit = tick - hops - 2
        if 0 <= unit < count:
            half_a(unit).wait_recv()
            half_b(unit).wait_recv()
            to_core(unit, 3).start()
    for unit in range(count):
        for hop in range(hops):
            along_sent(unit, hop)
        to_x(unit).wait_send()
        to_y(unit).wait_send()
        half_a(unit).wait_send()
        half_b(unit).wait_send()
        for which in range(4):
            to_core(unit, which).wait()
    for piece in range(pieces):
        for step in range(1, members):
            memory_send(piece, step).wait()
    local.wait()


def gather_by_kernel(shards, memory, items_count, members):
    items_here = memory.shape[0] // members
    units = []
    for weight, shard in enumerate(shards):
        height, width = shard.shape
        depth = height * 256 // max(height * width // 128, 256)
        for start in range(0, height, depth):
            units.append((weight, start, depth, height))
    pieces = memory.shape[1] // 32 * items_here
    hops = members - 1
    kinds = 2 * hops + 8
    out_shape = [jax.ShapeDtypeStruct((s.shape[0] * items_count, s.shape[1] * members), s.dtype) for s in shards]
    out_shape.append(
        jax.ShapeDtypeStruct((items_here, members, memory.shape[1], memory.shape[2]), memory.dtype)
    )
    outs = pl.pallas_call(
        functools.partial(gather_kernel, members, items_here, tuple(units)),
        out_shape=out_shape,
        in_specs=[ANY] * (len(shards) + 1),
        out_specs=[ANY] * len(out_shape),
        scratch_shapes=[
            pltpu.SemaphoreType.DMA((len(units), kinds)),
            pltpu.SemaphoreType.DMA((len(units), kinds)),
            pltpu.SemaphoreType.DMA((len(units),)),
            pltpu.SemaphoreType.DMA((pieces, members)),
            pltpu.SemaphoreType.DMA((pieces, members)),
            pltpu.SemaphoreType.DMA,
        ],
        compiler_params=pltpu.CompilerParams(collective_id=0, has_side_effects=True),
        name="gather_all",
    )(*shards, memory)
    return outs[:-1], outs[-1]


def gather_by_collectives(shards, memory, items_count, members):
    whole = []
    for shard in shards:
        cols = lax.all_gather(shard, "mem", axis=1, tiled=True)
        whole.append(lax.all_gather(cols, "items", axis=0, tiled=True))
    items_here = memory.shape[0] // members
    member = lax.axis_index("mem")
    parts = []
    for step in range(members):
        target = lax.rem(member + step, members)
        part = lax.dynamic_slice_in_dim(memory, target * items_here, items_here)
        if step:
            part = lax.ppermute(part, "mem", [(a, (a + step) % members) for a in range(members)])
        parts.append(part)
    return whole, jnp.stack(parts, 1)


def stack_pair(values, lane_low):
    zero = jnp.zeros_like(values)
    return jnp.concatenate([jnp.where(lane_low, values, zero), jnp.where(lane_low, zero, values)], 0)


def low_lanes(rows):
    return lax.broadcasted_iota(jnp.int32, (rows, PAIR), 1) < HEAD_DIM


def allowed_slots(causal, chunk, lens_ref, bases_ref, which, step, key_dim):
    shape = (2 * DEC, chunk) if key_dim == 1 else (chunk, 2 * DEC)
    slot = lax.broadcasted_iota(jnp.int32, shape, key_dim)
    if causal:
        query = lax.broadcasted_iota(jnp.int32, shape, 1 - key_dim) % DEC
        return (slot <= query) & (slot < lens_ref[which])
    return slot < lens_ref[which] - bases_ref[step]


def attend_forward_kernel(causal, chunk, lens_ref, bases_ref, q_ref, k_ref, v_ref, mixed_ref, exact_ref, scale_ref):
    which = pl.program_id(0)
    lane_low = low_lanes(DEC)
    q2 = stack_pair(q_ref[...], lane_low)
    numer = jnp.zeros((2 * DEC, PAIR), F32)
    total = jnp.zeros((2 * DEC, 1), F32)
    for step in range(k_ref.shape[0] // chunk):
        rows = pl.ds(step * chunk, chunk)
        scores = right_product(q2, k_ref[rows, :])
        allowed = allowed_slots(causal, chunk, lens_ref, bases_ref, which, step, 1)
        exp_scores = jnp.where(allowed, jnp.exp(scores), 0.0)
        total += jnp.sum(exp_scores, -1, keepdims=True)
        numer += product(exp_scores.astype(BF16), v_ref[rows, :])
    numer = jnp.where(lane_low, numer[:DEC], numer[DEC:])
    scale = 1.0 / jnp.where(lane_low, total[:DEC], total[DEC:])
    exact = numer * scale
    mixed_ref[...] = exact.astype(BF16)
    exact_ref[...] = exact
    scale_ref[...] = scale


def attend_backward_kernel(
    causal, chunk, lens_ref, bases_ref, q_ref, k_ref, v_ref, grad_ref, exact_ref, scale_ref, gq_ref, gk_ref, gv_ref
):
    which = pl.program_id(0)
    lane_low = low_lanes(DEC)
    q2 = stack_pair(q_ref[...], lane_low)
    grad_numer = grad_ref[...] * scale_ref[...]
    gn2 = stack_pair(grad_numer.astype(BF16), lane_low)
    weighted = jnp.transpose(grad_numer * exact_ref[...])
    grad_total = -jnp.concatenate(
        [
            jnp.sum(weighted[:HEAD_DIM], 0, keepdims=True),
            jnp.sum(weighted[HEAD_DIM:], 0, keepdims=True),
        ],
        1,
    )
    gq2 = jnp.zeros((2 * DEC, PAIR), F32)
    for step in range(k_ref.shape[0] // chunk):
        rows = pl.ds(step * chunk, chunk)
        keys = k_ref[rows, :]
        scores = right_product(keys, q2)
        allowed = allowed_slots(causal, chunk, lens_ref, bases_ref, which, step, 0)
        exp_scores = jnp.where(allowed, jnp.exp(scores), 0.0)
        grad_exp = right_product(v_ref[rows, :], gn2) + grad_total
        grad_scores = (exp_scores * grad_exp).astype(BF16)
        gk_ref[rows, :] = product(grad_scores, q2).astype(BF16)
        gv_ref[rows, :] = product(exp_scores.astype(BF16), gn2).astype(BF16)
        gq2 += left_product(grad_scores, keys)
    gq_ref[...] = jnp.where(lane_low, gq2[:DEC], gq2[DEC:]).astype(BF16)


def attention_call(kernel, causal, chunk, lens, bases, queries, keys, values, more, outs):
    item_count = lens.shape[0]
    slots = keys.shape[0] // item_count
    q_spec = pl.BlockSpec((DEC, PAIR), lambda a, p, *_: (a, p))
    k_spec = pl.BlockSpec((slots, PAIR), lambda a, p, *_: (a, p))
    spec = {"q": q_spec, "k": k_spec}
    rows = {"q": queries.shape[0], "k": keys.shape[0]}
    return pl.pallas_call(
        functools.partial(kernel, causal, chunk),
        grid_spec=pltpu.PrefetchScalarGridSpec(
            num_scalar_prefetch=2,
            grid=(item_count, PAIRS),
            in_specs=[q_spec, k_spec, k_spec] + [q_spec] * len(more),
            out_specs=[spec[kind] for kind, _ in outs],
        ),
        out_shape=[jax.ShapeDtypeStruct((rows[kind], D), dtype) for kind, dtype in outs],
        cost_estimate=pl.CostEstimate(
            flops=4 * item_count * HEADS * DEC * slots * 256, bytes_accessed=16 * D * slots, transcendentals=0
        ),
        name="self_attention" if causal else "cross_attention",
    )(lens, bases, queries, keys, values, *more)


def attend_forward(causal, chunk, lens, bases, queries, keys, values):
    return attention_call(
        attend_forward_kernel, causal, chunk, lens, bases, queries, keys, values, (),
        (("q", BF16), ("q", F32), ("q", F32)),
    )


def attend_backward(causal, chunk, lens, bases, queries, keys, values, grad_mixed, exact, scale):
    return attention_call(
        attend_backward_kernel, causal, chunk, lens, bases, queries, keys, values, (grad_mixed, exact, scale),
        (("q", BF16), ("k", BF16), ("k", BF16)),
    )


def halving_order(items_count, flipped):
    bits = [1 << b for b in range(1, items_count.bit_length() - 1)]
    return [1] + (bits if flipped else bits[::-1])


def block_order(items_count, flipped):
    bits = halving_order(items_count, flipped)
    order = []
    for spot in range(items_count):
        distance = 0
        for place, bit in enumerate(bits):
            if spot >> (len(bits) - 1 - place) & 1:
                distance |= bit
        order.append(distance)
    return order


def order_columns(values, row, items_count, flipped):
    width = values.shape[1] // items_count
    return jnp.concatenate(
        [
            lax.dynamic_slice_in_dim(values, (row ^ distance) * width, width, 1)
            for distance in block_order(items_count, flipped)
        ],
        1,
    )


def reduce_rows(partial, items_count, flipped):
    for bit in halving_order(items_count, flipped):
        half = partial.shape[0] // 2
        arrived = lax.ppermute(partial[half:], "items", [(a, a ^ bit) for a in range(items_count)])
        partial = (partial[:half].astype(F32) + arrived.astype(F32)).astype(BF16)
    return partial


def reduce_columns(partial, member, members):
    bit = members // 2
    while bit:
        half = partial.shape[1] // 2
        high = (member & bit) != 0
        left, right = partial[:, :half], partial[:, half:]
        arrived = lax.ppermute(
            jnp.where(high, left, right), "mem", [(a, a ^ bit) for a in range(members)]
        )
        partial = jnp.where(high, right, left).astype(F32) + arrived.astype(F32)
        if bit > 1:
            partial = partial.astype(BF16)
        bit //= 2
    return partial


def weight_gradients(left_ordered, grads, items_count, member, members, flipped):
    width = grads[0].shape[1]
    joined = grads[0] if len(grads) == 1 else jnp.concatenate(grads, 1)
    partial = left_product(left_ordered, joined).astype(BF16)
    partial = reduce_rows(partial, items_count, flipped)
    return [
        reduce_columns(partial[:, k * width : (k + 1) * width], member, members) for k in range(len(grads))
    ]


def body(
    items_count,
    members,
    tokens,
    memory,
    cotangent,
    mem_len,
    dec_len,
    self_query,
    self_key,
    self_value,
    self_out,
    cross_query,
    cross_key,
    cross_value,
    cross_out,
    feed_in,
    feed_out,
    shifts,
    gains,
    inner_bias,
):
    row = lax.axis_index("items")
    member = lax.axis_index("mem")
    rows_here = tokens.shape[0]
    item_count = rows_here // DEC
    group_items = memory.shape[0]
    mem_local = memory.shape[1]
    shards = (
        self_query, self_key, self_value, self_out, cross_query, cross_key, cross_value, cross_out, feed_in, feed_out,
    )
    gather = gather_by_kernel if (items_count, members) == (8, 4) else gather_by_collectives
    whole, item_memory = gather(shards, memory, items_count, members)
    (
        query_self, key_self, value_self, output_self, query_cross, key_cross, value_cross, output_cross,
        feed_up, feed_down,
    ) = whole
    memory_flat = item_memory.reshape(-1, D)
    shift_rows = lax.all_gather(shifts, "items", axis=1, tiled=True).astype(F32)
    gain_rows = lax.all_gather(gains, "items", axis=1, tiled=True).astype(F32)
    inner_shift = lax.all_gather(inner_bias, "items", axis=0, tiled=True).astype(F32)

    own_dec = lax.dynamic_slice_in_dim(dec_len, member * item_count, item_count)
    own_mem = lax.dynamic_slice_in_dim(mem_len, member * item_count, item_count)
    bases = lax.rem(member - jnp.arange(members, dtype=jnp.int32) + members, members) * mem_local

    tokens_float = tokens.astype(F32)
    queries_one = ((product(tokens, query_self) + shift_rows[0]) * 0.125).astype(BF16)
    keys_one = product(tokens, key_self).astype(BF16)
    values_one = (product(tokens, value_self) + shift_rows[1]).astype(BF16)
    mixed_one, exact_one, scale_one = attend_forward(
        True, DEC, own_dec, bases, queries_one, keys_one, values_one
    )
    resid_one = tokens_float + product(mixed_one, output_self) + shift_rows[2]
    hidden_one, normed_one, inverse_one = norm_forward(resid_one, gain_rows[0], shift_rows[7])
    hidden_one_low = hidden_one.astype(BF16)
    queries_two = ((product(hidden_one_low, query_cross) + shift_rows[3]) * 0.125).astype(BF16)
    keys_two = product(memory_flat, key_cross).astype(BF16)
    values_two = (product(memory_flat, value_cross) + shift_rows[4]).astype(BF16)
    mixed_two, exact_two, scale_two = attend_forward(
        False, mem_local, own_mem, bases, queries_two, keys_two, values_two
    )
    resid_two = hidden_one + product(mixed_two, output_cross) + shift_rows[5]
    hidden_two, normed_two, inverse_two = norm_forward(resid_two, gain_rows[1], shift_rows[8])
    hidden_two_low = hidden_two.astype(BF16)
    inner_pre = product(hidden_two_low, feed_up) + inner_shift
    cdf_part = 0.5 * (1.0 + jax.scipy.special.erf(inner_pre * half_root))
    active_low = (inner_pre * cdf_part).astype(BF16)
    resid_three = hidden_two + product(active_low, feed_down) + shift_rows[6]
    layer_out, normed_three, inverse_three = norm_forward(resid_three, gain_rows[2], shift_rows[9])

    grad_three, gain_grad_three, shift_grad_three = norm_backward(
        cotangent.astype(F32), normed_three, inverse_three, gain_rows[2]
    )
    grad_down = grad_three.astype(BF16)

    def summed(values, grads, flipped):
        ordered = order_columns(values, row, items_count, flipped)
        return weight_gradients(ordered, grads, items_count, member, members, flipped)

    (feed_down_grad,) = summed(active_low, [grad_down], False)
    out_bias_grad = column_sums(grad_down)
    grad_active = right_product(grad_down, feed_down)
    slope = cdf_part + inner_pre * jnp.exp(-0.5 * inner_pre * inner_pre) * normal_peak
    grad_inner = (grad_active * slope).astype(BF16)
    (feed_up_grad,) = summed(hidden_two_low, [grad_inner], True)
    inner_bias_grad = column_sums(grad_inner)
    grad_hidden_two = grad_three + right_product(grad_inner, feed_up)
    grad_two, gain_grad_two, shift_grad_two = norm_backward(
        grad_hidden_two, normed_two, inverse_two, gain_rows[1]
    )
    grad_cross_branch = grad_two.astype(BF16)
    (output_cross_grad,) = summed(mixed_two, [grad_cross_branch], False)
    cross_out_bias_grad = column_sums(grad_cross_branch)
    grad_mixed_two = right_product(grad_cross_branch, output_cross)
    query_grad_two, key_grad_two, value_grad_two = attend_backward(
        False, mem_local, own_mem, bases, queries_two, keys_two, values_two, grad_mixed_two, exact_two, scale_two
    )
    query_grad_two = query_grad_two * jnp.asarray(0.125, BF16)

    memory_part = (
        right_product(key_grad_two, key_cross) + right_product(value_grad_two, value_cross)
    ).astype(BF16).reshape(item_count, members, mem_local, D)
    memory_grad = jnp.zeros((group_items, mem_local, D), F32)
    for step in range(members):
        part = memory_part[:, step]
        if step:
            part = lax.ppermute(part, "mem", [(a, (a - step) % members) for a in range(members)])
        owner = lax.rem(member + step, members)
        memory_grad = lax.dynamic_update_slice_in_dim(memory_grad, part.astype(F32), owner * item_count, 0)

    key_cross_grad, value_cross_grad = summed(memory_flat, [key_grad_two, value_grad_two], True)
    cross_value_bias_grad = column_sums(value_grad_two)
    (query_cross_grad,) = summed(hidden_one_low, [query_grad_two], False)
    cross_query_bias_grad = column_sums(query_grad_two)
    grad_hidden_one = grad_two + right_product(query_grad_two, query_cross)
    grad_one, gain_grad_one, shift_grad_one = norm_backward(
        grad_hidden_one, normed_one, inverse_one, gain_rows[0]
    )
    grad_self_branch = grad_one.astype(BF16)
    (output_self_grad,) = summed(mixed_one, [grad_self_branch], True)
    self_out_bias_grad = column_sums(grad_self_branch)
    grad_mixed_one = right_product(grad_self_branch, output_self)
    query_grad_one, key_grad_one, value_grad_one = attend_backward(
        True, DEC, own_dec, bases, queries_one, keys_one, values_one, grad_mixed_one, exact_one, scale_one
    )
    query_grad_one = query_grad_one * jnp.asarray(0.125, BF16)
    query_self_grad, key_self_grad, value_self_grad = summed(
        tokens, [query_grad_one, key_grad_one, value_grad_one], False
    )
    tokens_grad = (
        grad_one
        + right_product(query_grad_one, query_self)
        + right_product(key_grad_one, key_self)
        + right_product(value_grad_one, value_self)
    )
    vectors = jnp.concatenate(
        [
            column_sums(query_grad_one),
            column_sums(value_grad_one),
            self_out_bias_grad,
            cross_query_bias_grad,
            cross_value_bias_grad,
            cross_out_bias_grad,
            out_bias_grad,
            shift_grad_one,
            shift_grad_two,
            shift_grad_three,
            gain_grad_one,
            gain_grad_two,
            gain_grad_three,
            inner_bias_grad,
        ]
    )
    vectors = lax.psum(vectors.reshape(-1, 128), ("items", "mem")).reshape(-1)
    shift_count = shifts.shape[0] * D
    gain_count = gains.shape[0] * D
    shift_width, gain_width, bias_width = shifts.shape[1], gains.shape[1], inner_bias.shape[0]
    shifts_grad = lax.dynamic_slice_in_dim(
        vectors[:shift_count].reshape(-1, D), row * shift_width, shift_width, 1
    )
    gains_grad = lax.dynamic_slice_in_dim(
        vectors[shift_count : shift_count + gain_count].reshape(-1, D), row * gain_width, gain_width, 1
    )
    bias_grad = lax.dynamic_slice_in_dim(vectors[shift_count + gain_count :], row * bias_width, bias_width)
    return (
        layer_out,
        tokens_grad,
        memory_grad,
        query_self_grad,
        key_self_grad,
        value_self_grad,
        output_self_grad,
        query_cross_grad,
        key_cross_grad,
        value_cross_grad,
        output_cross_grad,
        feed_up_grad,
        feed_down_grad,
        shifts_grad,
        gains_grad,
        bias_grad,
    )


def solution(mesh):
    tiles = P("items", "mem")
    rows = P(("items", "mem"), None)
    blocks = P("items", "mem", None)
    return jax.shard_map(
        functools.partial(body, mesh.shape["items"], mesh.shape["mem"]),
        mesh=mesh,
        in_specs=(rows, blocks, rows, P("items"), P("items"))
        + (tiles,) * 10
        + (P(None, "items"), P(None, "items"), P("items")),
        out_specs=(rows, rows, blocks) + (tiles,) * 10 + (P(None, "items"), P(None, "items"), P("items")),
        check_vma=False,
    )
```

```python
import functools

import jax
import jax.numpy as jnp
from jax import lax
from jax.experimental import pallas as pl
from jax.experimental.pallas import tpu as pltpu
from jax.sharding import PartitionSpec as P

D = 1024
HEADS = 16
HEAD_DIM = 64
PAIR = 2 * HEAD_DIM
PAIRS = HEADS // 2
DEC = 128
half_root = 0.7071067811865476
normal_peak = 0.3989422804014327
MESH = pl.DeviceIdType.MESH
F32 = jnp.float32
BF16 = jnp.bfloat16
Z_LAG, X_LAG, FIRST_PIECE, SPREAD = 1, 1, 3, 17
ANY = pl.BlockSpec(memory_space=pl.ANY)
VMEM = pl.BlockSpec(memory_space=pltpu.VMEM)


def product(first_op, second_op):
    return jnp.dot(first_op, second_op, preferred_element_type=F32)


def left_product(first_op, second_op):
    return lax.dot_general(
        first_op, second_op, (((0,), (0,)), ((), ())), preferred_element_type=F32
    )


def right_product(first_op, second_op):
    return lax.dot_general(
        first_op, second_op, (((1,), (1,)), ((), ())), preferred_element_type=F32
    )


def column_sums(values):
    return jnp.sum(values.astype(F32), 0)


def norm_forward(values, gain, shift):
    center = values - jnp.mean(values, -1, keepdims=True)
    inverse = lax.rsqrt(jnp.mean(center * center, -1, keepdims=True) + 1e-05)
    normed = center * inverse
    return (normed * gain + shift, normed, inverse)


def norm_backward(grad_out, normed, inverse, gain):
    scaled = grad_out * gain
    grad_in = inverse * (
        scaled
        - jnp.mean(scaled, -1, keepdims=True)
        - normed * jnp.mean(scaled * normed, -1, keepdims=True)
    )
    return (grad_in, jnp.sum(grad_out * normed, 0), jnp.sum(grad_out, 0))


def gather_kernel(members, items_here, units, *refs):
    count = len(units)
    weights = 1 + max(unit[0] for unit in units)
    shard_refs, memory_ref, vector_ref = refs[:weights], refs[weights], refs[weights + 1]
    whole_refs, items_ref, vectors_ref = refs[weights + 2 : 2 * weights + 2], refs[2 * weights + 2], refs[2 * weights + 3]
    send_sem, recv_sem, copy_sem, mem_send, mem_recv, mem_copy, vec_send, vec_recv, bounce = refs[2 * weights + 4 :]
    row = lax.axis_index("items")
    member = lax.axis_index("mem")
    hops = members - 1
    core_peer, first_peer, second_peer = row ^ 1, row ^ 2, row ^ 4
    UP, DOWN = 0, hops
    ALONG_X, ALONG_Y, HALF_A, HALF_B, CORE = 2 * hops, 2 * hops + 1, 2 * hops + 2, 2 * hops + 3, 2 * hops + 4

    barrier = pltpu.get_barrier_semaphore()
    partners = [(row ^ distance, member) for distance in range(1, 8)]
    partners += [(row, lax.rem(member + step, members)) for step in range(1, members)]
    for partner in partners:
        pl.semaphore_signal(barrier, inc=1, device_id=partner, device_id_type=MESH)
    pl.semaphore_wait(barrier, len(partners))

    def place(unit, owner):
        weight, start, depth, height = units[unit]
        return pl.ds(pl.multiple_of(owner * height + start, depth), depth)

    def cols(unit, who):
        width = shard_refs[units[unit][0]].shape[1]
        return pl.ds(pl.multiple_of(who * width, width), width)

    def shard(unit):
        weight, start, depth, height = units[unit]
        return shard_refs[weight].at[pl.ds(start, depth)]

    def remote(unit, kind, src, dst, device):
        return pltpu.make_async_remote_copy(
            src_ref=src,
            dst_ref=dst,
            send_sem=send_sem.at[unit, kind],
            recv_sem=recv_sem.at[unit, kind],
            device_id=device,
            device_id_type=MESH,
        )

    def along(unit, hop, upward):
        whole = whole_refs[units[unit][0]]
        origin = member - hop if upward else member + hop
        origin = jnp.clip(origin, 0, members - 1)
        piece = whole.at[place(unit, row), cols(unit, origin)]
        target = jnp.clip(member + 1 if upward else member - 1, 0, members - 1)
        return remote(
            unit, (UP if upward else DOWN) + hop, shard(unit) if hop == 0 else piece, piece, (row, target)
        )

    def along_start(unit, hop):
        @pl.when((member >= hop) & (member < members - 1))
        def _():
            along(unit, hop, True).start()

        @pl.when((member <= members - 1 - hop) & (member > 0))
        def _():
            along(unit, hop, False).start()

    def along_arrive(unit, hop):
        @pl.when(member >= hop + 1)
        def _():
            along(unit, hop, True).wait_recv()

        @pl.when(member <= members - 2 - hop)
        def _():
            along(unit, hop, False).wait_recv()

    def along_sent(unit, hop):
        @pl.when((member >= hop) & (member < members - 1))
        def _():
            along(unit, hop, True).wait_send()

        @pl.when((member <= members - 1 - hop) & (member > 0))
        def _():
            along(unit, hop, False).wait_send()

    def own_copy(unit):
        return pltpu.make_async_copy(
            shard(unit), whole_refs[units[unit][0]].at[place(unit, row), cols(unit, member)], copy_sem.at[unit]
        )

    def block(unit, kind, owner, device, half=None):
        weight, start, depth, height = units[unit]
        if half is None:
            rows = place(unit, owner)
        else:
            part = depth // 2
            rows = pl.ds(pl.multiple_of(owner * height + start + half * part, part), part)
        ref = whole_refs[weight].at[rows]
        return remote(unit, kind, ref, ref, (device, member))

    def to_x(unit):
        return block(unit, ALONG_X, row, first_peer)

    def to_y(unit):
        return block(unit, ALONG_Y, row, second_peer)

    def half_a(unit):
        return block(unit, HALF_A, first_peer, second_peer, 0)

    def half_b(unit):
        return block(unit, HALF_B, second_peer, first_peer, 1)

    def to_core(unit, which):
        owner = (row, first_peer, second_peer, row ^ 6)[which]
        return block(unit, CORE + which, owner, core_peer)

    pieces = memory_ref.shape[1] // 32 * items_here

    def memory_send(piece, step):
        which, start = piece // (pieces // items_here), piece % (pieces // items_here) * 32
        target = lax.rem(member + step, members)
        return pltpu.make_async_remote_copy(
            src_ref=memory_ref.at[target * items_here + which, pl.ds(start, 32)],
            dst_ref=items_ref.at[which, step, pl.ds(start, 32)],
            send_sem=mem_send.at[piece, step],
            recv_sem=mem_recv.at[piece, step],
            device_id=(row, target),
            device_id_type=MESH,
        )

    fetch = pltpu.make_async_copy(memory_ref.at[pl.ds(member * items_here, items_here)], bounce, mem_copy.at[0])
    local = pltpu.make_async_copy(bounce, items_ref.at[:, 0], mem_copy.at[1])
    fetch.start()
    spot = vectors_ref.at[:, pl.ds(pl.multiple_of(row * 128, 128), 128)]
    vector_copies = [
        pltpu.make_async_remote_copy(
            src_ref=vector_ref,
            dst_ref=spot,
            send_sem=vec_send.at[distance],
            recv_sem=vec_recv.at[distance],
            device_id=(row ^ distance, member),
            device_id_type=MESH,
        )
        for distance in range(1, 8)
    ]
    vector_copies.append(pltpu.make_async_copy(vector_ref, spot, vec_send.at[0]))
    for copy in vector_copies:
        copy.start()

    depth_ticks = Z_LAG * hops + 2 * X_LAG
    due = [FIRST_PIECE + piece * SPREAD // pieces for piece in range(pieces)]
    for tick in range(max(count + depth_ticks, due[-1] + 1)):
        unit = tick
        if unit < count:
            along_start(unit, 0)
            own_copy(unit).start()
        for piece in range(pieces):
            if due[piece] == tick:
                for step in range(1, members):
                    memory_send(piece, step).start()
        for hop in range(1, hops):
            unit = tick - Z_LAG * hop
            if 0 <= unit < count:
                along_arrive(unit, hop - 1)
                along_start(unit, hop)
        unit = tick - Z_LAG * hops
        if 0 <= unit < count:
            along_arrive(unit, hops - 1)
            own_copy(unit).wait()
            to_x(unit).start()
            to_y(unit).start()
            to_core(unit, 0).start()
        unit = tick - Z_LAG * hops - X_LAG
        if 0 <= unit < count:
            to_x(unit).wait_recv()
            half_a(unit).start()
            to_core(unit, 1).start()
            to_y(unit).wait_recv()
            half_b(unit).start()
            to_core(unit, 2).start()
        unit = tick - Z_LAG * hops - 2 * X_LAG
        if 0 <= unit < count:
            half_a(unit).wait_recv()
            half_b(unit).wait_recv()
            to_core(unit, 3).start()
    for unit in range(count):
        for hop in range(hops):
            along_sent(unit, hop)
        to_x(unit).wait_send()
        to_y(unit).wait_send()
        half_a(unit).wait_send()
        half_b(unit).wait_send()
        for which in range(4):
            to_core(unit, which).wait()
    for piece in range(pieces):
        for step in range(1, members):
            memory_send(piece, step).wait()
    fetch.wait()
    local.start()
    local.wait()
    for copy in vector_copies:
        copy.wait()


def gather_by_kernel(shards, memory, vector, items_count, members):
    items_here = memory.shape[0] // members
    units = []
    for weight, shard in enumerate(shards):
        height, width = shard.shape
        depth = height * 256 // max(height * width // 128, 256)
        for start in range(0, height, depth):
            units.append((weight, start, depth, height))
    pieces = memory.shape[1] // 32 * items_here
    hops = members - 1
    kinds = 2 * hops + 8
    out_shape = [jax.ShapeDtypeStruct((s.shape[0] * items_count, s.shape[1] * members), s.dtype) for s in shards]
    out_shape.append(
        jax.ShapeDtypeStruct((items_here, members, memory.shape[1], memory.shape[2]), memory.dtype)
    )
    out_shape.append(jax.ShapeDtypeStruct((vector.shape[0], vector.shape[1] * items_count), vector.dtype))
    outs = pl.pallas_call(
        functools.partial(gather_kernel, members, items_here, tuple(units)),
        out_shape=out_shape,
        in_specs=[VMEM] * len(shards) + [ANY, VMEM],
        out_specs=[ANY] * len(out_shape),
        scratch_shapes=[
            pltpu.SemaphoreType.DMA((len(units), kinds)),
            pltpu.SemaphoreType.DMA((len(units), kinds)),
            pltpu.SemaphoreType.DMA((len(units),)),
            pltpu.SemaphoreType.DMA((pieces, members)),
            pltpu.SemaphoreType.DMA((pieces, members)),
            pltpu.SemaphoreType.DMA((2,)),
            pltpu.SemaphoreType.DMA((items_count,)),
            pltpu.SemaphoreType.DMA((items_count,)),
            pltpu.VMEM((items_here,) + memory.shape[1:], memory.dtype),
        ],
        compiler_params=pltpu.CompilerParams(collective_id=0, has_side_effects=True),
        name="gather_all",
    )(*shards, memory, vector)
    return outs[:-2], outs[-2], outs[-1]


def gather_by_collectives(shards, memory, vector, items_count, members):
    whole = []
    for shard in shards:
        cols = lax.all_gather(shard, "mem", axis=1, tiled=True)
        whole.append(lax.all_gather(cols, "items", axis=0, tiled=True))
    items_here = memory.shape[0] // members
    member = lax.axis_index("mem")
    parts = []
    for step in range(members):
        target = lax.rem(member + step, members)
        part = lax.dynamic_slice_in_dim(memory, target * items_here, items_here)
        if step:
            part = lax.ppermute(part, "mem", [(a, (a + step) % members) for a in range(members)])
        parts.append(part)
    return whole, jnp.stack(parts, 1), lax.all_gather(vector, "items", axis=1, tiled=True)


def stack_pair(values, lane_low):
    zero = jnp.zeros_like(values)
    return jnp.concatenate([jnp.where(lane_low, values, zero), jnp.where(lane_low, zero, values)], 0)


def low_lanes(rows):
    return lax.broadcasted_iota(jnp.int32, (rows, PAIR), 1) < HEAD_DIM


def allowed_slots(causal, chunk, lens_ref, bases_ref, which, step, key_dim):
    shape = (2 * DEC, chunk) if key_dim == 1 else (chunk, 2 * DEC)
    slot = lax.broadcasted_iota(jnp.int32, shape, key_dim)
    if causal:
        query = lax.broadcasted_iota(jnp.int32, shape, 1 - key_dim) % DEC
        return (slot <= query) & (slot < lens_ref[which])
    return slot < lens_ref[which] - bases_ref[step]


def attend_forward_kernel(causal, chunk, lens_ref, bases_ref, q_ref, k_ref, v_ref, mixed_ref, exact_ref, scale_ref):
    which = pl.program_id(0)
    lane_low = low_lanes(DEC)
    q2 = stack_pair(q_ref[...], lane_low)
    numer = jnp.zeros((2 * DEC, PAIR), F32)
    total = jnp.zeros((2 * DEC, 1), F32)
    for step in range(k_ref.shape[0] // chunk):
        rows = pl.ds(step * chunk, chunk)
        scores = right_product(q2, k_ref[rows, :])
        allowed = allowed_slots(causal, chunk, lens_ref, bases_ref, which, step, 1)
        exp_scores = jnp.where(allowed, jnp.exp(scores), 0.0)
        total += jnp.sum(exp_scores, -1, keepdims=True)
        numer += product(exp_scores.astype(BF16), v_ref[rows, :])
    numer = jnp.where(lane_low, numer[:DEC], numer[DEC:])
    scale = 1.0 / jnp.where(lane_low, total[:DEC], total[DEC:])
    exact = numer * scale
    mixed_ref[...] = exact.astype(BF16)
    exact_ref[...] = exact
    scale_ref[...] = scale


def attend_backward_kernel(
    causal, chunk, lens_ref, bases_ref, q_ref, k_ref, v_ref, grad_ref, exact_ref, scale_ref, gq_ref, gk_ref, gv_ref
):
    which = pl.program_id(0)
    lane_low = low_lanes(DEC)
    q2 = stack_pair(q_ref[...], lane_low)
    grad_numer = grad_ref[...] * scale_ref[...]
    gn2 = stack_pair(grad_numer.astype(BF16), lane_low)
    weighted = jnp.transpose(grad_numer * exact_ref[...])
    grad_total = -jnp.concatenate(
        [
            jnp.sum(weighted[:HEAD_DIM], 0, keepdims=True),
            jnp.sum(weighted[HEAD_DIM:], 0, keepdims=True),
        ],
        1,
    )
    gq2 = jnp.zeros((2 * DEC, PAIR), F32)
    for step in range(k_ref.shape[0] // chunk):
        rows = pl.ds(step * chunk, chunk)
        keys = k_ref[rows, :]
        scores = right_product(keys, q2)
        allowed = allowed_slots(causal, chunk, lens_ref, bases_ref, which, step, 0)
        exp_scores = jnp.where(allowed, jnp.exp(scores), 0.0)
        grad_exp = right_product(v_ref[rows, :], gn2) + grad_total
        grad_scores = (exp_scores * grad_exp).astype(BF16)
        gk_ref[rows, :] = product(grad_scores, q2).astype(BF16)
        gv_ref[rows, :] = product(exp_scores.astype(BF16), gn2).astype(BF16)
        gq2 += left_product(grad_scores, keys)
    gq_ref[...] = jnp.where(lane_low, gq2[:DEC], gq2[DEC:]).astype(BF16)


def attention_call(kernel, causal, chunk, lens, bases, queries, keys, values, more, outs):
    item_count = lens.shape[0]
    slots = keys.shape[0] // item_count
    q_spec = pl.BlockSpec((DEC, PAIR), lambda a, p, *_: (a, p))
    k_spec = pl.BlockSpec((slots, PAIR), lambda a, p, *_: (a, p))
    spec = {"q": q_spec, "k": k_spec}
    rows = {"q": queries.shape[0], "k": keys.shape[0]}
    return pl.pallas_call(
        functools.partial(kernel, causal, chunk),
        grid_spec=pltpu.PrefetchScalarGridSpec(
            num_scalar_prefetch=2,
            grid=(item_count, PAIRS),
            in_specs=[q_spec, k_spec, k_spec] + [q_spec] * len(more),
            out_specs=[spec[kind] for kind, _ in outs],
        ),
        out_shape=[jax.ShapeDtypeStruct((rows[kind], D), dtype) for kind, dtype in outs],
        cost_estimate=pl.CostEstimate(
            flops=4 * item_count * HEADS * DEC * slots * 256, bytes_accessed=16 * D * slots, transcendentals=0
        ),
        name="self_attention" if causal else "cross_attention",
    )(lens, bases, queries, keys, values, *more)


def attend_forward(causal, chunk, lens, bases, queries, keys, values):
    return attention_call(
        attend_forward_kernel, causal, chunk, lens, bases, queries, keys, values, (),
        (("q", BF16), ("q", F32), ("q", F32)),
    )


def attend_backward(causal, chunk, lens, bases, queries, keys, values, grad_mixed, exact, scale):
    return attention_call(
        attend_backward_kernel, causal, chunk, lens, bases, queries, keys, values, (grad_mixed, exact, scale),
        (("q", BF16), ("k", BF16), ("k", BF16)),
    )


def halving_order(items_count, flipped):
    bits = [1 << b for b in range(1, items_count.bit_length() - 1)]
    return [1] + (bits if flipped else bits[::-1])


def block_order(items_count, flipped):
    bits = halving_order(items_count, flipped)
    order = []
    for spot in range(items_count):
        distance = 0
        for place, bit in enumerate(bits):
            if spot >> (len(bits) - 1 - place) & 1:
                distance |= bit
        order.append(distance)
    return order


def order_columns(values, row, items_count, flipped):
    width = values.shape[1] // items_count
    return jnp.concatenate(
        [
            lax.dynamic_slice_in_dim(values, (row ^ distance) * width, width, 1)
            for distance in block_order(items_count, flipped)
        ],
        1,
    )


def reduce_rows(partial, items_count, flipped):
    for bit in halving_order(items_count, flipped):
        half = partial.shape[0] // 2
        arrived = lax.ppermute(partial[half:], "items", [(a, a ^ bit) for a in range(items_count)])
        partial = (partial[:half].astype(F32) + arrived.astype(F32)).astype(BF16)
    return partial


def reduce_columns(partial, member, members):
    bit = members // 2
    while bit:
        half = partial.shape[1] // 2
        high = (member & bit) != 0
        left, right = partial[:, :half], partial[:, half:]
        arrived = lax.ppermute(
            jnp.where(high, left, right), "mem", [(a, a ^ bit) for a in range(members)]
        )
        partial = jnp.where(high, right, left).astype(F32) + arrived.astype(F32)
        if bit > 1:
            partial = partial.astype(BF16)
        bit //= 2
    return partial


def weight_gradients(left_ordered, grads, items_count, member, members, flipped):
    width = grads[0].shape[1]
    joined = grads[0] if len(grads) == 1 else jnp.concatenate(grads, 1)
    partial = left_product(left_ordered, joined).astype(BF16)
    partial = reduce_rows(partial, items_count, flipped)
    return [
        reduce_columns(partial[:, k * width : (k + 1) * width], member, members) for k in range(len(grads))
    ]

RING, KEPT, ROUND = 4, 6, 8
S_LAG = 2


def scatter_kernel(members, units, back_rows, *refs):
    lefts = 1 + max(unit[0] for unit in units)
    rights = 1 + max(unit[1] for unit in units)
    outs = 1 + max(unit[2] for unit in units)
    count = len(units)
    left_refs, right_refs, part_ref = refs[:lefts], refs[lefts : lefts + rights], refs[lefts + rights]
    refs = refs[lefts + rights + 1 :]
    out_refs, back_ref = refs[:outs], refs[outs]
    (
        core_out, core_in, near_out, near_in, near_kept, far_out, far_in, own, hop_out, hop_in,
        send_sem, recv_sem, back_send, back_recv, credit,
    ) = refs[outs + 1 :]
    row = lax.axis_index("items")
    member = lax.axis_index("mem")
    hops = members - 1
    core_peer = row ^ 1

    barrier = pltpu.get_barrier_semaphore()
    partners = [(core_peer, member), (row ^ 2, member), (row ^ 4, member)]
    partners += [(row, lax.rem(member + step, members)) for step in range(1, members)]
    for partner in partners:
        pl.semaphore_signal(barrier, inc=1, device_id=partner, device_id_type=MESH)
    pl.semaphore_wait(barrier, len(partners))

    def bits(unit):
        return (2, 4) if unit % 2 == 0 else (4, 2)

    def owners(unit, who):
        near, far = bits(unit)
        return (who ^ near, who ^ near ^ far, who ^ far, who)

    def partial(unit, owner):
        left, right, _, left_start, left_step, right_start, right_step = units[unit]
        left_ref, right_ref = left_refs[left], right_refs[right]
        cols = pl.ds(pl.multiple_of(owner * left_step + left_start, 128), 128)
        depth = left_ref.shape[0]
        chunk = min(depth, 512)

        def term(start):
            rows = pl.ds(start, chunk)
            if right_step == 256:
                right_value = right_ref[rows, :]
            else:
                right_value = jnp.concatenate(
                    [
                        right_ref[rows, pl.ds(right_start + k * right_step, 256)]
                        for k in range(members)
                    ],
                    1,
                )
            return left_product(left_ref[rows, cols], right_value)

        total = term(0)
        if depth > chunk:
            total = lax.fori_loop(
                1, depth // chunk, lambda k, sums: sums + term(pl.multiple_of(k * chunk, chunk)), total
            )
        return total

    def remote(unit, kind, src, dst, device):
        return pltpu.make_async_remote_copy(
            src_ref=src,
            dst_ref=dst,
            send_sem=send_sem.at[unit, kind],
            recv_sem=recv_sem.at[unit, kind],
            device_id=device,
            device_id_type=MESH,
        )

    def core_copy(unit):
        return remote(unit, 0, core_out.at[unit % 2], core_in.at[unit % RING], (core_peer, member))

    def near_copy(unit):
        return remote(unit, 1, near_out.at[unit % RING], near_in.at[unit % ROUND], (row ^ bits(unit)[0], member))

    def far_copy(unit):
        return remote(unit, 2, far_out.at[unit % RING], far_in.at[unit % ROUND], (row ^ bits(unit)[1], member))

    def hop_copy(unit, hop, upward):
        target = jnp.clip(member + 1 if upward else member - 1, 0, members - 1)
        place = hop if upward else hops + hop
        return remote(unit, 3 + place, hop_out.at[unit % RING, place], hop_in.at[unit, place], (row, target))

    def hop_sends(hop, upward):
        distance = members - 1 - hop
        return (member + distance <= members - 1) if upward else (member - distance >= 0)

    def hop_gets(hop, upward):
        distance = members - 1 - hop
        return (
            ((member >= 1) & (member - 1 + distance <= members - 1))
            if upward
            else ((member <= members - 2) & (member + 1 - distance >= 0))
        )

    def core_stage(unit):
        if unit >= 2:
            core_copy(unit - 2).wait_send()
        targets = owners(unit, core_peer)

        def fill(spot, _):
            owner = targets[3]
            for k in range(3):
                owner = jnp.where(spot == k, targets[k], owner)
            core_out[unit % 2, spot] = partial(unit, owner).astype(BF16)
            return 0

        lax.fori_loop(0, 4, fill, 0)
        if unit >= RING:
            pl.semaphore_wait(credit, 1)
        core_copy(unit).start()

    def near_stage(unit):
        core_copy(unit).wait_recv()
        if unit >= RING:
            near_copy(unit - RING).wait_send()
        mine = owners(unit, row)

        def give(spot, _):
            total = partial(unit, jnp.where(spot == 0, mine[0], mine[1])) + core_in[unit % RING, spot].astype(F32)
            near_out[unit % RING, spot] = total.astype(BF16)
            return 0

        lax.fori_loop(0, 2, give, 0)
        near_copy(unit).start()

        def keep(spot, _):
            near_kept[unit % KEPT, spot] = partial(unit, jnp.where(spot == 0, mine[2], mine[3])) + core_in[
                unit % RING, 2 + spot
            ].astype(F32)
            return 0

        lax.fori_loop(0, 2, keep, 0)
        if unit + RING < count:
            pl.semaphore_signal(credit, inc=1, device_id=(core_peer, member), device_id_type=MESH)

    def far_stage(unit):
        near_copy(unit).wait_recv()
        if unit >= RING:
            far_copy(unit - RING).wait_send()
        far_out[unit % RING] = (near_kept[unit % KEPT, 0] + near_in[unit % ROUND, 1].astype(F32)).astype(BF16)
        far_copy(unit).start()

    def hop_stage(unit, hop):
        if hop == 0:
            far_copy(unit).wait_recv()
            own[unit % RING] = (
                near_kept[unit % KEPT, 1] + near_in[unit % ROUND, 0].astype(F32) + far_in[unit % ROUND].astype(F32)
            )
        for upward in (True, False):
            distance = members - 1 - hop
            owner = jnp.clip(member + distance if upward else member - distance, 0, members - 1)
            place = hop if upward else hops + hop
            block = pl.ds(pl.multiple_of(owner * 256, 256), 256)
            if unit >= RING:
                @pl.when(hop_sends(hop, upward))
                def _():
                    hop_copy(unit - RING, hop, upward).wait_send()

            if hop > 0:
                @pl.when(hop_gets(hop - 1, upward))
                def _():
                    hop_copy(unit, hop - 1, upward).wait_recv()
                    hop_out[unit % RING, place] = (
                        own[unit % RING, :, block] + hop_in[unit, place - 1].astype(F32)
                    ).astype(BF16)

                @pl.when(hop_sends(hop, upward) & jnp.logical_not(hop_gets(hop - 1, upward)))
                def _():
                    hop_out[unit % RING, place] = own[unit % RING, :, block].astype(BF16)

            else:
                @pl.when(hop_sends(hop, upward))
                def _():
                    hop_out[unit % RING, place] = own[unit % RING, :, block].astype(BF16)

            @pl.when(hop_sends(hop, upward))
            def _():
                hop_copy(unit, hop, upward).start()

    def last_stage(unit):
        _, _, out, left_start, left_step, right_start, right_step = units[unit]
        rows, cols = pl.ds(left_start, 128), pl.ds(right_start, 256)
        block = pl.ds(pl.multiple_of(member * 256, 256), 256)
        out_refs[out][rows, cols] = own[unit % RING, :, block]
        for upward in (True, False):
            place = hops - 1 if upward else 2 * hops - 1

            @pl.when(hop_gets(hops - 1, upward))
            def _():
                hop_copy(unit, hops - 1, upward).wait_recv()
                out_refs[out][rows, cols] += hop_in[unit, place].astype(F32)

    pieces = part_ref.shape[2] // back_rows * part_ref.shape[0]
    items_here = part_ref.shape[0]

    def back_copy(piece, step):
        which, start = piece // (pieces // items_here), piece % (pieces // items_here) * back_rows
        target = lax.rem(member - step + members, members)
        return pltpu.make_async_remote_copy(
            src_ref=part_ref.at[which, step, pl.ds(start, back_rows)],
            dst_ref=back_ref.at[member * items_here + which, pl.ds(start, back_rows)],
            send_sem=back_send.at[piece, step],
            recv_sem=back_recv.at[piece, step],
            device_id=(row, target),
            device_id_type=MESH,
        )

    far_tick, hop_tick = 1 + S_LAG, 1 + 2 * S_LAG
    last_tick = hop_tick + hops
    for tick in range(max(count + last_tick, pieces)):
        if tick < pieces:
            for step in range(1, members):
                back_copy(tick, step).start()
        if 0 <= tick - far_tick < count:
            far_stage(tick - far_tick)
        for hop in range(hops):
            if 0 <= tick - hop_tick - hop < count:
                hop_stage(tick - hop_tick - hop, hop)
        if 0 <= tick - last_tick < count:
            last_stage(tick - last_tick)
        if 0 <= tick < count:
            core_stage(tick)
        if 0 <= tick - 1 < count:
            near_stage(tick - 1)
    for unit in range(count - 2, count):
        core_copy(unit).wait_send()
    for unit in range(count - RING, count):
        near_copy(unit).wait_send()
        far_copy(unit).wait_send()
        for hop in range(hops):
            for upward in (True, False):
                @pl.when(hop_sends(hop, upward))
                def _():
                    hop_copy(unit, hop, upward).wait_send()
    for piece in range(pieces):
        for step in range(1, members):
            back_copy(piece, step).wait()


def scatter_by_kernel(pairs, blocks, memory_part, members):
    lefts, rights, units = [], [], []
    for out, ((left, right), (height, width)) in enumerate(zip(pairs, blocks)):
        spots = []
        for value, found in ((left, lefts), (right, rights)):
            for place, other in enumerate(found):
                if other is value:
                    spots.append(place)
                    break
            else:
                spots.append(len(found))
                found.append(value)
        for left_start in range(0, height, 128):
            for right_start in range(0, width, 256):
                units.append((spots[0], spots[1], out, left_start, height, right_start, width))
    count, hops = len(units), members - 1
    items_here, _, mem_local, width = memory_part.shape
    back_rows = 32
    pieces = mem_local // back_rows * items_here
    outs = pl.pallas_call(
        functools.partial(scatter_kernel, members, tuple(units), back_rows),
        out_shape=[jax.ShapeDtypeStruct(block, F32) for block in blocks]
        + [jax.ShapeDtypeStruct((items_here * members, mem_local, width), BF16)],
        in_specs=[VMEM] * (len(lefts) + len(rights)) + [ANY],
        out_specs=[VMEM] * len(blocks) + [ANY],
        scratch_shapes=[
            pltpu.VMEM((2, 4, 128, 1024), BF16),
            pltpu.VMEM((RING, 4, 128, 1024), BF16),
            pltpu.VMEM((RING, 2, 128, 1024), BF16),
            pltpu.VMEM((ROUND, 2, 128, 1024), BF16),
            pltpu.VMEM((KEPT, 2, 128, 1024), F32),
            pltpu.VMEM((RING, 128, 1024), BF16),
            pltpu.VMEM((ROUND, 128, 1024), BF16),
            pltpu.VMEM((RING, 128, 1024), F32),
            pltpu.VMEM((RING, 2 * hops, 128, 256), BF16),
            pltpu.VMEM((count, 2 * hops, 128, 256), BF16),
            pltpu.SemaphoreType.DMA((count, 3 + 2 * hops)),
            pltpu.SemaphoreType.DMA((count, 3 + 2 * hops)),
            pltpu.SemaphoreType.DMA((pieces, members)),
            pltpu.SemaphoreType.DMA((pieces, members)),
            pltpu.SemaphoreType.REGULAR,
        ],
        compiler_params=pltpu.CompilerParams(
            collective_id=1, has_side_effects=True, vmem_limit_bytes=60 * 1024 * 1024
        ),
        name="scatter_all",
    )(*lefts, *rights, memory_part)
    return outs[:-1], outs[-1]


def scatter_by_collectives(pairs, blocks, memory_part, row, member, items_count, members):
    grads = []
    for place, (left, right) in enumerate(pairs):
        ordered = order_columns(left, row, items_count, place % 2 == 1)
        grads += weight_gradients(ordered, [right], items_count, member, members, place % 2 == 1)
    items_here = memory_part.shape[0]
    back = jnp.zeros((items_here * members,) + memory_part.shape[2:], BF16)
    for step in range(1, members):
        part = lax.ppermute(memory_part[:, step], "mem", [(a, (a - step) % members) for a in range(members)])
        owner = lax.rem(member + step, members)
        back = lax.dynamic_update_slice_in_dim(back, part, owner * items_here, 0)
    return grads, back


def body(
    items_count,
    members,
    tokens,
    memory,
    cotangent,
    mem_len,
    dec_len,
    self_query,
    self_key,
    self_value,
    self_out,
    cross_query,
    cross_key,
    cross_value,
    cross_out,
    feed_in,
    feed_out,
    shifts,
    gains,
    inner_bias,
):
    row = lax.axis_index("items")
    member = lax.axis_index("mem")
    rows_here = tokens.shape[0]
    item_count = rows_here // DEC
    group_items = memory.shape[0]
    mem_local = memory.shape[1]
    shards = (
        self_query, self_key, self_value, self_out, cross_query, cross_key, cross_value, cross_out, feed_in, feed_out,
    )
    by_kernel = (items_count, members) == (8, 4)
    shift_width, bias_rows = shifts.shape[1], inner_bias.shape[0] // shifts.shape[1]
    vector = jnp.concatenate([shifts, gains, inner_bias.reshape(bias_rows, shift_width)], 0)
    gather = gather_by_kernel if by_kernel else gather_by_collectives
    whole, item_memory, vectors = gather(shards, memory, vector, items_count, members)
    (
        query_self, key_self, value_self, output_self, query_cross, key_cross, value_cross, output_cross,
        feed_up, feed_down,
    ) = whole
    memory_flat = item_memory.reshape(-1, D)
    vectors = vectors.astype(F32)
    bias_start = shifts.shape[0] + gains.shape[0]
    shift_rows = vectors[: shifts.shape[0]]
    gain_rows = vectors[shifts.shape[0] : bias_start]
    inner_shift = (
        vectors[bias_start:].reshape(bias_rows, items_count, shift_width).transpose(1, 0, 2).reshape(-1)
    )

    own_dec = lax.dynamic_slice_in_dim(dec_len, member * item_count, item_count)
    own_mem = lax.dynamic_slice_in_dim(mem_len, member * item_count, item_count)
    bases = lax.rem(member - jnp.arange(members, dtype=jnp.int32) + members, members) * mem_local

    tokens_float = tokens.astype(F32)
    queries_one = ((product(tokens, query_self) + shift_rows[0]) * 0.125).astype(BF16)
    keys_one = product(tokens, key_self).astype(BF16)
    values_one = (product(tokens, value_self) + shift_rows[1]).astype(BF16)
    mixed_one, exact_one, scale_one = attend_forward(
        True, DEC, own_dec, bases, queries_one, keys_one, values_one
    )
    resid_one = tokens_float + product(mixed_one, output_self) + shift_rows[2]
    hidden_one, normed_one, inverse_one = norm_forward(resid_one, gain_rows[0], shift_rows[7])
    hidden_one_low = hidden_one.astype(BF16)
    queries_two = ((product(hidden_one_low, query_cross) + shift_rows[3]) * 0.125).astype(BF16)
    keys_two = product(memory_flat, key_cross).astype(BF16)
    values_two = (product(memory_flat, value_cross) + shift_rows[4]).astype(BF16)
    mixed_two, exact_two, scale_two = attend_forward(
        False, mem_local, own_mem, bases, queries_two, keys_two, values_two
    )
    resid_two = hidden_one + product(mixed_two, output_cross) + shift_rows[5]
    hidden_two, normed_two, inverse_two = norm_forward(resid_two, gain_rows[1], shift_rows[8])
    hidden_two_low = hidden_two.astype(BF16)
    inner_pre = product(hidden_two_low, feed_up) + inner_shift
    cdf_part = 0.5 * (1.0 + jax.scipy.special.erf(inner_pre * half_root))
    active_low = (inner_pre * cdf_part).astype(BF16)
    resid_three = hidden_two + product(active_low, feed_down) + shift_rows[6]
    layer_out, normed_three, inverse_three = norm_forward(resid_three, gain_rows[2], shift_rows[9])

    grad_three, gain_grad_three, shift_grad_three = norm_backward(
        cotangent.astype(F32), normed_three, inverse_three, gain_rows[2]
    )
    grad_down = grad_three.astype(BF16)

    out_bias_grad = column_sums(grad_down)
    grad_active = right_product(grad_down, feed_down)
    slope = cdf_part + inner_pre * jnp.exp(-0.5 * inner_pre * inner_pre) * normal_peak
    grad_inner = (grad_active * slope).astype(BF16)
    inner_bias_grad = column_sums(grad_inner)
    grad_hidden_two = grad_three + right_product(grad_inner, feed_up)
    grad_two, gain_grad_two, shift_grad_two = norm_backward(
        grad_hidden_two, normed_two, inverse_two, gain_rows[1]
    )
    grad_cross_branch = grad_two.astype(BF16)
    cross_out_bias_grad = column_sums(grad_cross_branch)
    grad_mixed_two = right_product(grad_cross_branch, output_cross)
    query_grad_two, key_grad_two, value_grad_two = attend_backward(
        False, mem_local, own_mem, bases, queries_two, keys_two, values_two, grad_mixed_two, exact_two, scale_two
    )
    query_grad_two = query_grad_two * jnp.asarray(0.125, BF16)

    memory_part = (
        right_product(key_grad_two, key_cross) + right_product(value_grad_two, value_cross)
    ).astype(BF16).reshape(item_count, members, mem_local, D)
    cross_value_bias_grad = column_sums(value_grad_two)
    cross_query_bias_grad = column_sums(query_grad_two)
    grad_hidden_one = grad_two + right_product(query_grad_two, query_cross)
    grad_one, gain_grad_one, shift_grad_one = norm_backward(
        grad_hidden_one, normed_one, inverse_one, gain_rows[0]
    )
    grad_self_branch = grad_one.astype(BF16)
    self_out_bias_grad = column_sums(grad_self_branch)
    grad_mixed_one = right_product(grad_self_branch, output_self)
    query_grad_one, key_grad_one, value_grad_one = attend_backward(
        True, DEC, own_dec, bases, queries_one, keys_one, values_one, grad_mixed_one, exact_one, scale_one
    )
    query_grad_one = query_grad_one * jnp.asarray(0.125, BF16)
    pairs = (
        (active_low, grad_down),
        (hidden_two_low, grad_inner),
        (mixed_two, grad_cross_branch),
        (memory_flat, key_grad_two),
        (memory_flat, value_grad_two),
        (hidden_one_low, query_grad_two),
        (mixed_one, grad_self_branch),
        (tokens, query_grad_one),
        (tokens, key_grad_one),
        (tokens, value_grad_one),
    )
    blocks = tuple(
        weight.shape
        for weight in (
            feed_out, feed_in, cross_out, cross_key, cross_value, cross_query, self_out, self_query, self_key, self_value,
        )
    )
    if by_kernel:
        grads, memory_back = scatter_by_kernel(pairs, blocks, memory_part, members)
    else:
        grads, memory_back = scatter_by_collectives(pairs, blocks, memory_part, row, member, items_count, members)
    (
        feed_down_grad, feed_up_grad, output_cross_grad, key_cross_grad, value_cross_grad, query_cross_grad,
        output_self_grad, query_self_grad, key_self_grad, value_self_grad,
    ) = grads
    memory_grad = lax.dynamic_update_slice_in_dim(
        memory_back.astype(F32), memory_part[:, 0].astype(F32), member * item_count, 0
    )
    tokens_grad = (
        grad_one
        + right_product(query_grad_one, query_self)
        + right_product(key_grad_one, key_self)
        + right_product(value_grad_one, value_self)
    )
    vectors = jnp.concatenate(
        [
            column_sums(query_grad_one),
            column_sums(value_grad_one),
            self_out_bias_grad,
            cross_query_bias_grad,
            cross_value_bias_grad,
            cross_out_bias_grad,
            out_bias_grad,
            shift_grad_one,
            shift_grad_two,
            shift_grad_three,
            gain_grad_one,
            gain_grad_two,
            gain_grad_three,
            inner_bias_grad,
        ]
    )
    vectors = lax.psum(vectors.reshape(-1, 128), ("items", "mem")).reshape(-1)
    shift_count = shifts.shape[0] * D
    gain_count = gains.shape[0] * D
    shift_width, gain_width, bias_width = shifts.shape[1], gains.shape[1], inner_bias.shape[0]
    shifts_grad = lax.dynamic_slice_in_dim(
        vectors[:shift_count].reshape(-1, D), row * shift_width, shift_width, 1
    )
    gains_grad = lax.dynamic_slice_in_dim(
        vectors[shift_count : shift_count + gain_count].reshape(-1, D), row * gain_width, gain_width, 1
    )
    bias_grad = lax.dynamic_slice_in_dim(vectors[shift_count + gain_count :], row * bias_width, bias_width)
    return (
        layer_out,
        tokens_grad,
        memory_grad,
        query_self_grad,
        key_self_grad,
        value_self_grad,
        output_self_grad,
        query_cross_grad,
        key_cross_grad,
        value_cross_grad,
        output_cross_grad,
        feed_up_grad,
        feed_down_grad,
        shifts_grad,
        gains_grad,
        bias_grad,
    )


def solution(mesh):
    tiles = P("items", "mem")
    rows = P(("items", "mem"), None)
    blocks = P("items", "mem", None)
    return jax.shard_map(
        functools.partial(body, mesh.shape["items"], mesh.shape["mem"]),
        mesh=mesh,
        in_specs=(rows, blocks, rows, P("items"), P("items"))
        + (tiles,) * 10
        + (P(None, "items"), P(None, "items"), P("items")),
        out_specs=(rows, rows, blocks) + (tiles,) * 10 + (P(None, "items"), P(None, "items"), P("items")),
        check_vma=False,
    )
```

```python
import functools

import jax
import jax.numpy as jnp
from jax import lax
from jax.experimental import pallas as pl
from jax.experimental.pallas import tpu as pltpu
from jax.sharding import PartitionSpec as P

D = 1024
HEADS = 16
HEAD_DIM = 64
PAIR = 2 * HEAD_DIM
PAIRS = HEADS // 2
DEC = 128
half_root = 0.7071067811865476
normal_peak = 0.3989422804014327
MESH = pl.DeviceIdType.MESH
F32 = jnp.float32
BF16 = jnp.bfloat16
Z_LAG, X_LAG, FIRST_PIECE, SPREAD = 1, 1, 3, 17
ANY = pl.BlockSpec(memory_space=pl.ANY)
VMEM = pl.BlockSpec(memory_space=pltpu.VMEM)


def product(first_op, second_op):
    return jnp.dot(first_op, second_op, preferred_element_type=F32)


def left_product(first_op, second_op):
    return lax.dot_general(
        first_op, second_op, (((0,), (0,)), ((), ())), preferred_element_type=F32
    )


def right_product(first_op, second_op):
    return lax.dot_general(
        first_op, second_op, (((1,), (1,)), ((), ())), preferred_element_type=F32
    )


def column_sums(values):
    return jnp.sum(values.astype(F32), 0)


def norm_forward(values, gain, shift):
    center = values - jnp.mean(values, -1, keepdims=True)
    inverse = lax.rsqrt(jnp.mean(center * center, -1, keepdims=True) + 1e-05)
    normed = center * inverse
    return (normed * gain + shift, normed, inverse)


def norm_backward(grad_out, normed, inverse, gain):
    scaled = grad_out * gain
    grad_in = inverse * (
        scaled
        - jnp.mean(scaled, -1, keepdims=True)
        - normed * jnp.mean(scaled * normed, -1, keepdims=True)
    )
    return (grad_in, jnp.sum(grad_out * normed, 0), jnp.sum(grad_out, 0))


def gather_kernel(members, items_here, units, forward, *refs):
    count = len(units)
    weights = 1 + max(unit[0] for unit in units)
    shard_refs = refs[:weights]
    memory_ref, vector_ref, tokens_ref, limits_ref = refs[weights : weights + 4]
    refs = refs[weights + 4 :]
    whole_refs, items_ref, vectors_ref = refs[:weights], refs[weights], refs[weights + 1]
    refs = refs[weights + 2 :]
    outs, refs = refs[: forward.outs], refs[forward.outs :]
    send_sem, recv_sem, copy_sem, mem_send, mem_recv, mem_copy, vec_send, vec_recv, bounce = refs[:9]
    row = lax.axis_index("items")
    member = lax.axis_index("mem")
    hops = members - 1
    core_peer, first_peer, second_peer = row ^ 1, row ^ 2, row ^ 4
    UP, DOWN = 0, hops
    ALONG_X, ALONG_Y, HALF_A, HALF_B, CORE = 2 * hops, 2 * hops + 1, 2 * hops + 2, 2 * hops + 3, 2 * hops + 4

    barrier = pltpu.get_barrier_semaphore()
    partners = [(row ^ distance, member) for distance in range(1, 8)]
    partners += [(row, lax.rem(member + step, members)) for step in range(1, members)]
    for partner in partners:
        pl.semaphore_signal(barrier, inc=1, device_id=partner, device_id_type=MESH)
    pl.semaphore_wait(barrier, len(partners))

    def place(unit, owner):
        weight, start, depth, height = units[unit]
        return pl.ds(pl.multiple_of(owner * height + start, depth), depth)

    def cols(unit, who):
        width = shard_refs[units[unit][0]].shape[1]
        return pl.ds(pl.multiple_of(who * width, width), width)

    def shard(unit):
        weight, start, depth, height = units[unit]
        return shard_refs[weight].at[pl.ds(start, depth)]

    def remote(unit, kind, src, dst, device):
        return pltpu.make_async_remote_copy(
            src_ref=src,
            dst_ref=dst,
            send_sem=send_sem.at[unit, kind],
            recv_sem=recv_sem.at[unit, kind],
            device_id=device,
            device_id_type=MESH,
        )

    def along(unit, hop, upward):
        whole = whole_refs[units[unit][0]]
        origin = member - hop if upward else member + hop
        origin = jnp.clip(origin, 0, members - 1)
        piece = whole.at[place(unit, row), cols(unit, origin)]
        target = jnp.clip(member + 1 if upward else member - 1, 0, members - 1)
        return remote(
            unit, (UP if upward else DOWN) + hop, shard(unit) if hop == 0 else piece, piece, (row, target)
        )

    def along_start(unit, hop):
        @pl.when((member >= hop) & (member < members - 1))
        def _():
            along(unit, hop, True).start()

        @pl.when((member <= members - 1 - hop) & (member > 0))
        def _():
            along(unit, hop, False).start()

    def along_arrive(unit, hop):
        @pl.when(member >= hop + 1)
        def _():
            along(unit, hop, True).wait_recv()

        @pl.when(member <= members - 2 - hop)
        def _():
            along(unit, hop, False).wait_recv()

    def along_sent(unit, hop):
        @pl.when((member >= hop) & (member < members - 1))
        def _():
            along(unit, hop, True).wait_send()

        @pl.when((member <= members - 1 - hop) & (member > 0))
        def _():
            along(unit, hop, False).wait_send()

    def own_copy(unit):
        return pltpu.make_async_copy(
            shard(unit), whole_refs[units[unit][0]].at[place(unit, row), cols(unit, member)], copy_sem.at[unit]
        )

    def block(unit, kind, owner, device, half=None):
        weight, start, depth, height = units[unit]
        if half is None:
            rows = place(unit, owner)
        else:
            part = depth // 2
            rows = pl.ds(pl.multiple_of(owner * height + start + half * part, part), part)
        ref = whole_refs[weight].at[rows]
        return remote(unit, kind, ref, ref, (device, member))

    def to_x(unit):
        return block(unit, ALONG_X, row, first_peer)

    def to_y(unit):
        return block(unit, ALONG_Y, row, second_peer)

    def half_a(unit):
        return block(unit, HALF_A, first_peer, second_peer, 0)

    def half_b(unit):
        return block(unit, HALF_B, second_peer, first_peer, 1)

    def to_core(unit, which):
        owner = (row, first_peer, second_peer, row ^ 6)[which]
        return block(unit, CORE + which, owner, core_peer)

    pieces = memory_ref.shape[1] // 32 * items_here

    def memory_send(piece, step):
        which, start = piece // (pieces // items_here), piece % (pieces // items_here) * 32
        target = lax.rem(member + step, members)
        return pltpu.make_async_remote_copy(
            src_ref=memory_ref.at[target * items_here + which, pl.ds(start, 32)],
            dst_ref=items_ref.at[which, step, pl.ds(start, 32)],
            send_sem=mem_send.at[piece, step],
            recv_sem=mem_recv.at[piece, step],
            device_id=(row, target),
            device_id_type=MESH,
        )

    fetch = pltpu.make_async_copy(memory_ref.at[pl.ds(member * items_here, items_here)], bounce, mem_copy.at[0])
    local = pltpu.make_async_copy(bounce, items_ref.at[:, 0], mem_copy.at[1])
    fetch.start()
    spot = vectors_ref.at[:, pl.ds(pl.multiple_of(row * 128, 128), 128)]
    vector_copies = [
        pltpu.make_async_remote_copy(
            src_ref=vector_ref,
            dst_ref=spot,
            send_sem=vec_send.at[distance],
            recv_sem=vec_recv.at[distance],
            device_id=(row ^ distance, member),
            device_id_type=MESH,
        )
        for distance in range(1, 8)
    ]
    vector_copies.append(pltpu.make_async_copy(vector_ref, spot, vec_send.at[0]))
    for copy in vector_copies:
        copy.start()

    due = [FIRST_PIECE + piece * SPREAD // pieces for piece in range(pieces)]
    done_lag = Z_LAG * hops + 2 * X_LAG + 1
    jobs = forward.jobs(
        members, items_here, member, tokens_ref, limits_ref, whole_refs, items_ref, vectors_ref, outs, refs[9:],
        done_lag, due,
    )
    last = max([count - 1 + done_lag, due[-1] + 2] + list(jobs))
    for tick in range(last + 1):
        unit = tick
        if unit < count:
            along_start(unit, 0)
            own_copy(unit).start()
        for piece in range(pieces):
            if due[piece] == tick:
                for step in range(1, members):
                    memory_send(piece, step).start()
        for hop in range(1, hops):
            unit = tick - Z_LAG * hop
            if 0 <= unit < count:
                along_arrive(unit, hop - 1)
                along_start(unit, hop)
        unit = tick - Z_LAG * hops
        if 0 <= unit < count:
            along_arrive(unit, hops - 1)
            own_copy(unit).wait()
            to_x(unit).start()
            to_y(unit).start()
            to_core(unit, 0).start()
        unit = tick - Z_LAG * hops - X_LAG
        if 0 <= unit < count:
            to_x(unit).wait_recv()
            half_a(unit).start()
            to_core(unit, 1).start()
            to_y(unit).wait_recv()
            half_b(unit).start()
            to_core(unit, 2).start()
        unit = tick - Z_LAG * hops - 2 * X_LAG
        if 0 <= unit < count:
            half_a(unit).wait_recv()
            half_b(unit).wait_recv()
            to_core(unit, 3).start()
        if tick == 1:
            fetch.wait()
            local.start()
        if tick == 3:
            local.wait()
            for copy in vector_copies:
                copy.wait()
        unit = tick - done_lag
        if 0 <= unit < count:
            for which in range(4):
                to_core(unit, which).wait_recv()
        for piece in range(pieces):
            if due[piece] + 2 == tick:
                for step in range(1, members):
                    memory_send(piece, step).wait_recv()
        for job in jobs.get(tick, ()):
            job()
    for unit in range(count):
        for hop in range(hops):
            along_sent(unit, hop)
        to_x(unit).wait_send()
        to_y(unit).wait_send()
        half_a(unit).wait_send()
        half_b(unit).wait_send()
        for which in range(4):
            to_core(unit, which).wait_send()
    for piece in range(pieces):
        for step in range(1, members):
            memory_send(piece, step).wait_send()
    forward.finish()


def attend_pair(queries, keys_at, values_at, allowed_at, chunks):
    lane_low = low_lanes(DEC)
    q2 = stack_pair(queries, lane_low)
    numer, total = None, None
    for step in range(chunks):
        scores = right_product(q2, keys_at(step))
        exp_scores = jnp.where(allowed_at(step), jnp.exp(scores), 0.0)
        part = jnp.sum(exp_scores, -1, keepdims=True)
        term = product(exp_scores.astype(BF16), values_at(step))
        total = part if total is None else total + part
        numer = term if numer is None else numer + term
    numer = jnp.where(lane_low, numer[:DEC], numer[DEC:])
    scale = 1.0 / jnp.where(lane_low, total[:DEC], total[DEC:])
    return numer * scale, scale


class Forward:
    outs = 15

    def __init__(self, rows, items_here, members, mem_local):
        self.rows, self.items_here, self.members, self.mem_local = rows, items_here, members, mem_local
        self.slots = members * mem_local

    def out_shapes(self):
        wide, low = jax.ShapeDtypeStruct((self.rows, D), F32), jax.ShapeDtypeStruct((self.rows, D), BF16)
        keys = jax.ShapeDtypeStruct((self.items_here, self.members, self.mem_local, D), BF16)
        inverse = jax.ShapeDtypeStruct((self.rows, 1), F32)
        return [low, low, low, low, wide, wide, wide, wide, inverse, low, low, wide, wide, keys, keys]

    def out_specs(self):
        return [VMEM] * 13 + [ANY] * 2

    def scratch(self):
        return [
            pltpu.VMEM((2, D, D), BF16),
            pltpu.VMEM((2, D, D), BF16),
            pltpu.VMEM((2, self.members, self.mem_local // 4, D), BF16),
            pltpu.VMEM((self.items_here, self.members, self.mem_local, D), BF16),
            pltpu.VMEM((self.items_here, self.members, self.mem_local, D), BF16),
            pltpu.SemaphoreType.DMA((16,)),
        ]

    def jobs(
        self, members, items_here, member, tokens_ref, limits_ref, whole_refs, items_ref, vectors_ref, outs, scratch,
        done_lag, due,
    ):
        (
            q_one, k_one, v_one, mixed_one, exact_one, scale_one, hidden_one, normed_one, inverse_one, q_two, mixed_two,
            exact_two, scale_two, keys_out, values_out,
        ) = outs
        weight_buf, cross_buf, rows_buf, keys, values, sems = scratch
        part = self.mem_local // 4
        schedule = {}

        def at(tick, job):
            schedule.setdefault(tick, []).append(job)

        def vector(index):
            return vectors_ref[...].astype(F32)[index : index + 1]

        def fetch_weight(unit, slot):
            return pltpu.make_async_copy(whole_refs[unit], weight_buf.at[slot], sems.at[slot])

        def fetch_cross(unit):
            return pltpu.make_async_copy(whole_refs[unit], cross_buf.at[unit], sems.at[2 + unit])

        def fetch_rows(which, chunk):
            slot = chunk % 2
            return pltpu.make_async_copy(
                items_ref.at[which, :, pl.ds(chunk * part, part)], rows_buf.at[slot], sems.at[4 + slot]
            )

        def store(which, value):
            source, target = ((keys, keys_out), (values, values_out))[value]
            return pltpu.make_async_copy(source.at[which], target.at[which], sems.at[6 + 2 * which + value])

        self.pending = []

        def project(slot, unit, result, shift, scale):
            def job():
                fetch_weight(unit, slot).wait()
                total = product(tokens_ref[...], weight_buf[slot])
                if shift is not None:
                    total = total + vector(shift)
                if scale is not None:
                    total = total * scale
                result[...] = total.astype(BF16)

            return job

        def self_attend(which):
            def job():
                limit = limits_ref[0:1, which : which + 1]
                slot = lax.broadcasted_iota(jnp.int32, (2 * DEC, DEC), 1)
                query = lax.broadcasted_iota(jnp.int32, (2 * DEC, DEC), 0) % DEC
                allowed = (slot <= query) & (slot < limit)
                rows = pl.ds(which * DEC, DEC)

                def pair(p, _):
                    cols = pl.ds(pl.multiple_of(p * PAIR, PAIR), PAIR)
                    exact, scale = attend_pair(
                        q_one[rows, cols], lambda _: k_one[rows, cols], lambda _: v_one[rows, cols], lambda _: allowed, 1
                    )
                    mixed_one[rows, cols] = exact.astype(BF16)
                    exact_one[rows, cols] = exact
                    scale_one[rows, cols] = scale
                    return 0

                lax.fori_loop(0, PAIRS, pair, 0)

            return job

        def first_norm(slot, unit):
            def job():
                fetch_weight(unit, slot).wait()
                resid = tokens_ref[...].astype(F32) + product(mixed_one[...], weight_buf[slot]) + vector(2)
                hidden, normed, inverse = norm_forward(resid, vector(10), vector(7))
                hidden_one[...] = hidden
                normed_one[...] = normed
                inverse_one[...] = inverse

            return job

        def cross_query(slot, unit):
            def job():
                fetch_weight(unit, slot).wait()
                total = (product(hidden_one[...].astype(BF16), weight_buf[slot]) + vector(3)) * 0.125
                q_two[...] = total.astype(BF16)

            return job

        def project_rows(which, chunk):
            def job():
                fetch_rows(which, chunk).wait()
                rows = rows_buf[chunk % 2].reshape(members * part, D)
                new_keys = product(rows, cross_buf[0]).astype(BF16).reshape(members, part, D)
                new_values = (product(rows, cross_buf[1]) + vector(4)).astype(BF16).reshape(members, part, D)
                keys[which, :, pl.ds(chunk * part, part)] = new_keys
                values[which, :, pl.ds(chunk * part, part)] = new_values
                if chunk == 3:
                    store(which, 0).start()
                    store(which, 1).start()

            return job

        def cross_attend(which, low, high):
            def job():
                rows = pl.ds(which * DEC, DEC)
                limit = limits_ref[1:2, which : which + 1]
                slot = lax.broadcasted_iota(jnp.int32, (2 * DEC, self.mem_local), 1)

                def allowed(step):
                    return slot < limit - lax.rem(member - step + members, members) * self.mem_local

                def pair(p, _):
                    cols = pl.ds(pl.multiple_of(p * PAIR, PAIR), PAIR)
                    exact, scale = attend_pair(
                        q_two[rows, cols],
                        lambda step: keys[which, step, :, cols],
                        lambda step: values[which, step, :, cols],
                        allowed,
                        members,
                    )
                    mixed_two[rows, cols] = exact.astype(BF16)
                    exact_two[rows, cols] = exact
                    scale_two[rows, cols] = scale
                    return 0

                lax.fori_loop(low, high, pair, 0)

            return job

        for unit in range(2):
            at(unit + done_lag, fetch_cross(unit).start)
        for unit in range(2, 7):
            at(unit + done_lag, fetch_weight(unit, unit % 2).start)
        at(1 + done_lag + 1, fetch_cross(0).wait)
        at(1 + done_lag + 1, fetch_cross(1).wait)
        start = 2 + done_lag + 1
        at(start, project(0, 2, q_one, 0, 0.125))
        at(start + 1, project(1, 3, k_one, None, None))
        at(start + 2, project(0, 4, v_one, 1, None))
        at(start + 2, self_attend(0))
        at(start + 3, self_attend(1))
        at(start + 3, first_norm(1, 5))
        at(start + 4, cross_query(0, 6))
        previous = 1 + done_lag
        per_item = len(due) // items_here
        for which in range(items_here):
            for chunk in range(4):
                ready = due[which * per_item + (chunk + 1) * per_item // 4 - 1] + 2
                begin = max(ready, previous)
                at(begin, fetch_rows(which, chunk).start)
                late = begin if which == items_here - 1 and chunk == 3 else begin + 1
                at(late, project_rows(which, chunk))
                previous = begin + 1
            begin = max(previous, start + 5)
            if which < items_here - 1:
                for quarter in range(4):
                    at(begin + quarter, cross_attend(which, 2 * quarter, 2 * quarter + 2))
            else:
                at(late, cross_attend(which, 0, PAIRS))
        self.pending = [store(which, value) for which in range(items_here) for value in range(2)]
        return schedule

    def finish(self):
        for copy in self.pending:
            copy.wait()


def gather_by_kernel(shards, memory, vector, tokens, limits, items_count, members):
    items_here = memory.shape[0] // members
    units = []
    for weight, shard in enumerate(shards):
        height, width = shard.shape
        depth = height * 256 // max(height * width // 128, 256)
        for start in range(0, height, depth):
            units.append((weight, start, depth, height))
    forward = Forward(tokens.shape[0], items_here, members, memory.shape[1])
    pieces = memory.shape[1] // 32 * items_here
    hops = members - 1
    kinds = 2 * hops + 8
    out_shape = [jax.ShapeDtypeStruct((s.shape[0] * items_count, s.shape[1] * members), s.dtype) for s in shards]
    out_shape.append(
        jax.ShapeDtypeStruct((items_here, members, memory.shape[1], memory.shape[2]), memory.dtype)
    )
    out_shape.append(jax.ShapeDtypeStruct((vector.shape[0], vector.shape[1] * items_count), vector.dtype))
    gathered = len(out_shape)
    out_shape += forward.out_shapes()
    outs = pl.pallas_call(
        functools.partial(gather_kernel, members, items_here, tuple(units), forward),
        out_shape=out_shape,
        in_specs=[VMEM] * len(shards) + [ANY, VMEM, VMEM, VMEM],
        out_specs=[ANY] * (gathered - 1) + [VMEM] + forward.out_specs(),
        scratch_shapes=[
            pltpu.SemaphoreType.DMA((len(units), kinds)),
            pltpu.SemaphoreType.DMA((len(units), kinds)),
            pltpu.SemaphoreType.DMA((len(units),)),
            pltpu.SemaphoreType.DMA((pieces, members)),
            pltpu.SemaphoreType.DMA((pieces, members)),
            pltpu.SemaphoreType.DMA((2,)),
            pltpu.SemaphoreType.DMA((items_count,)),
            pltpu.SemaphoreType.DMA((items_count,)),
            pltpu.VMEM((items_here,) + memory.shape[1:], memory.dtype),
        ]
        + forward.scratch(),
        compiler_params=pltpu.CompilerParams(
            collective_id=0, has_side_effects=True, vmem_limit_bytes=60 * 1024 * 1024
        ),
        name="gather_all",
    )(*shards, memory, vector, tokens, limits)
    return outs[: gathered - 2], outs[gathered - 2], outs[gathered - 1], outs[gathered:]


def gather_by_collectives(shards, memory, vector, items_count, members):
    whole = []
    for shard in shards:
        cols = lax.all_gather(shard, "mem", axis=1, tiled=True)
        whole.append(lax.all_gather(cols, "items", axis=0, tiled=True))
    items_here = memory.shape[0] // members
    member = lax.axis_index("mem")
    parts = []
    for step in range(members):
        target = lax.rem(member + step, members)
        part = lax.dynamic_slice_in_dim(memory, target * items_here, items_here)
        if step:
            part = lax.ppermute(part, "mem", [(a, (a + step) % members) for a in range(members)])
        parts.append(part)
    return whole, jnp.stack(parts, 1), lax.all_gather(vector, "items", axis=1, tiled=True)


def stack_pair(values, lane_low):
    zero = jnp.zeros_like(values)
    return jnp.concatenate([jnp.where(lane_low, values, zero), jnp.where(lane_low, zero, values)], 0)


def low_lanes(rows):
    return lax.broadcasted_iota(jnp.int32, (rows, PAIR), 1) < HEAD_DIM


def allowed_slots(causal, chunk, lens_ref, bases_ref, which, step, key_dim):
    shape = (2 * DEC, chunk) if key_dim == 1 else (chunk, 2 * DEC)
    slot = lax.broadcasted_iota(jnp.int32, shape, key_dim)
    if causal:
        query = lax.broadcasted_iota(jnp.int32, shape, 1 - key_dim) % DEC
        return (slot <= query) & (slot < lens_ref[which])
    return slot < lens_ref[which] - bases_ref[step]


def attend_forward_kernel(causal, chunk, lens_ref, bases_ref, q_ref, k_ref, v_ref, mixed_ref, exact_ref, scale_ref):
    which = pl.program_id(0)
    lane_low = low_lanes(DEC)
    q2 = stack_pair(q_ref[...], lane_low)
    numer = jnp.zeros((2 * DEC, PAIR), F32)
    total = jnp.zeros((2 * DEC, 1), F32)
    for step in range(k_ref.shape[0] // chunk):
        rows = pl.ds(step * chunk, chunk)
        scores = right_product(q2, k_ref[rows, :])
        allowed = allowed_slots(causal, chunk, lens_ref, bases_ref, which, step, 1)
        exp_scores = jnp.where(allowed, jnp.exp(scores), 0.0)
        total += jnp.sum(exp_scores, -1, keepdims=True)
        numer += product(exp_scores.astype(BF16), v_ref[rows, :])
    numer = jnp.where(lane_low, numer[:DEC], numer[DEC:])
    scale = 1.0 / jnp.where(lane_low, total[:DEC], total[DEC:])
    exact = numer * scale
    mixed_ref[...] = exact.astype(BF16)
    exact_ref[...] = exact
    scale_ref[...] = scale


def attend_backward_kernel(
    causal, chunk, lens_ref, bases_ref, q_ref, k_ref, v_ref, grad_ref, exact_ref, scale_ref, gq_ref, gk_ref, gv_ref
):
    which = pl.program_id(0)
    lane_low = low_lanes(DEC)
    q2 = stack_pair(q_ref[...], lane_low)
    grad_numer = grad_ref[...] * scale_ref[...]
    gn2 = stack_pair(grad_numer.astype(BF16), lane_low)
    weighted = jnp.transpose(grad_numer * exact_ref[...])
    grad_total = -jnp.concatenate(
        [
            jnp.sum(weighted[:HEAD_DIM], 0, keepdims=True),
            jnp.sum(weighted[HEAD_DIM:], 0, keepdims=True),
        ],
        1,
    )
    gq2 = jnp.zeros((2 * DEC, PAIR), F32)
    for step in range(k_ref.shape[0] // chunk):
        rows = pl.ds(step * chunk, chunk)
        keys = k_ref[rows, :]
        scores = right_product(keys, q2)
        allowed = allowed_slots(causal, chunk, lens_ref, bases_ref, which, step, 0)
        exp_scores = jnp.where(allowed, jnp.exp(scores), 0.0)
        grad_exp = right_product(v_ref[rows, :], gn2) + grad_total
        grad_scores = (exp_scores * grad_exp).astype(BF16)
        gk_ref[rows, :] = product(grad_scores, q2).astype(BF16)
        gv_ref[rows, :] = product(exp_scores.astype(BF16), gn2).astype(BF16)
        gq2 += left_product(grad_scores, keys)
    gq_ref[...] = jnp.where(lane_low, gq2[:DEC], gq2[DEC:]).astype(BF16)


def attention_call(kernel, causal, chunk, lens, bases, queries, keys, values, more, outs):
    item_count = lens.shape[0]
    slots = keys.shape[0] // item_count
    q_spec = pl.BlockSpec((DEC, PAIR), lambda a, p, *_: (a, p))
    k_spec = pl.BlockSpec((slots, PAIR), lambda a, p, *_: (a, p))
    spec = {"q": q_spec, "k": k_spec}
    rows = {"q": queries.shape[0], "k": keys.shape[0]}
    return pl.pallas_call(
        functools.partial(kernel, causal, chunk),
        grid_spec=pltpu.PrefetchScalarGridSpec(
            num_scalar_prefetch=2,
            grid=(item_count, PAIRS),
            in_specs=[q_spec, k_spec, k_spec] + [q_spec] * len(more),
            out_specs=[spec[kind] for kind, _ in outs],
        ),
        out_shape=[jax.ShapeDtypeStruct((rows[kind], D), dtype) for kind, dtype in outs],
        cost_estimate=pl.CostEstimate(
            flops=4 * item_count * HEADS * DEC * slots * 256, bytes_accessed=16 * D * slots, transcendentals=0
        ),
        name="self_attention" if causal else "cross_attention",
    )(lens, bases, queries, keys, values, *more)


def attend_forward(causal, chunk, lens, bases, queries, keys, values):
    return attention_call(
        attend_forward_kernel, causal, chunk, lens, bases, queries, keys, values, (),
        (("q", BF16), ("q", F32), ("q", F32)),
    )


def attend_backward(causal, chunk, lens, bases, queries, keys, values, grad_mixed, exact, scale):
    return attention_call(
        attend_backward_kernel, causal, chunk, lens, bases, queries, keys, values, (grad_mixed, exact, scale),
        (("q", BF16), ("k", BF16), ("k", BF16)),
    )


def halving_order(items_count, flipped):
    bits = [1 << b for b in range(1, items_count.bit_length() - 1)]
    return [1] + (bits if flipped else bits[::-1])


def block_order(items_count, flipped):
    bits = halving_order(items_count, flipped)
    order = []
    for spot in range(items_count):
        distance = 0
        for place, bit in enumerate(bits):
            if spot >> (len(bits) - 1 - place) & 1:
                distance |= bit
        order.append(distance)
    return order


def order_columns(values, row, items_count, flipped):
    width = values.shape[1] // items_count
    return jnp.concatenate(
        [
            lax.dynamic_slice_in_dim(values, (row ^ distance) * width, width, 1)
            for distance in block_order(items_count, flipped)
        ],
        1,
    )


def reduce_rows(partial, items_count, flipped):
    for bit in halving_order(items_count, flipped):
        half = partial.shape[0] // 2
        arrived = lax.ppermute(partial[half:], "items", [(a, a ^ bit) for a in range(items_count)])
        partial = (partial[:half].astype(F32) + arrived.astype(F32)).astype(BF16)
    return partial


def reduce_columns(partial, member, members):
    bit = members // 2
    while bit:
        half = partial.shape[1] // 2
        high = (member & bit) != 0
        left, right = partial[:, :half], partial[:, half:]
        arrived = lax.ppermute(
            jnp.where(high, left, right), "mem", [(a, a ^ bit) for a in range(members)]
        )
        partial = jnp.where(high, right, left).astype(F32) + arrived.astype(F32)
        if bit > 1:
            partial = partial.astype(BF16)
        bit //= 2
    return partial


def weight_gradients(left_ordered, grads, items_count, member, members, flipped):
    width = grads[0].shape[1]
    joined = grads[0] if len(grads) == 1 else jnp.concatenate(grads, 1)
    partial = left_product(left_ordered, joined).astype(BF16)
    partial = reduce_rows(partial, items_count, flipped)
    return [
        reduce_columns(partial[:, k * width : (k + 1) * width], member, members) for k in range(len(grads))
    ]

RING, KEPT, ROUND = 4, 6, 8
S_LAG = 2


def scatter_kernel(members, units, back_rows, *refs):
    lefts = 1 + max(unit[0] for unit in units)
    rights = 1 + max(unit[1] for unit in units)
    outs = 1 + max(unit[2] for unit in units)
    count = len(units)
    left_refs, right_refs, part_ref = refs[:lefts], refs[lefts : lefts + rights], refs[lefts + rights]
    refs = refs[lefts + rights + 1 :]
    out_refs, back_ref = refs[:outs], refs[outs]
    (
        core_out, core_in, near_out, near_in, near_kept, far_out, far_in, own, hop_out, hop_in,
        send_sem, recv_sem, back_send, back_recv, credit,
    ) = refs[outs + 1 :]
    row = lax.axis_index("items")
    member = lax.axis_index("mem")
    hops = members - 1
    core_peer = row ^ 1

    barrier = pltpu.get_barrier_semaphore()
    partners = [(core_peer, member), (row ^ 2, member), (row ^ 4, member)]
    partners += [(row, lax.rem(member + step, members)) for step in range(1, members)]
    for partner in partners:
        pl.semaphore_signal(barrier, inc=1, device_id=partner, device_id_type=MESH)
    pl.semaphore_wait(barrier, len(partners))

    def bits(unit):
        return (2, 4) if unit % 2 == 0 else (4, 2)

    def owners(unit, who):
        near, far = bits(unit)
        return (who ^ near, who ^ near ^ far, who ^ far, who)

    def partial(unit, owner):
        left, right, _, left_start, left_step, right_start, right_step = units[unit]
        left_ref, right_ref = left_refs[left], right_refs[right]
        cols = pl.ds(pl.multiple_of(owner * left_step + left_start, 128), 128)
        depth = left_ref.shape[0]
        chunk = min(depth, 512)

        def term(start):
            rows = pl.ds(start, chunk)
            if right_step == 256:
                right_value = right_ref[rows, :]
            else:
                right_value = jnp.concatenate(
                    [
                        right_ref[rows, pl.ds(right_start + k * right_step, 256)]
                        for k in range(members)
                    ],
                    1,
                )
            return left_product(left_ref[rows, cols], right_value)

        total = term(0)
        if depth > chunk:
            total = lax.fori_loop(
                1, depth // chunk, lambda k, sums: sums + term(pl.multiple_of(k * chunk, chunk)), total
            )
        return total

    def remote(unit, kind, src, dst, device):
        return pltpu.make_async_remote_copy(
            src_ref=src,
            dst_ref=dst,
            send_sem=send_sem.at[unit, kind],
            recv_sem=recv_sem.at[unit, kind],
            device_id=device,
            device_id_type=MESH,
        )

    def core_copy(unit):
        return remote(unit, 0, core_out.at[unit % 2], core_in.at[unit % RING], (core_peer, member))

    def near_copy(unit):
        return remote(unit, 1, near_out.at[unit % RING], near_in.at[unit % ROUND], (row ^ bits(unit)[0], member))

    def far_copy(unit):
        return remote(unit, 2, far_out.at[unit % RING], far_in.at[unit % ROUND], (row ^ bits(unit)[1], member))

    def hop_copy(unit, hop, upward):
        target = jnp.clip(member + 1 if upward else member - 1, 0, members - 1)
        place = hop if upward else hops + hop
        return remote(unit, 3 + place, hop_out.at[unit % RING, place], hop_in.at[unit, place], (row, target))

    def hop_sends(hop, upward):
        distance = members - 1 - hop
        return (member + distance <= members - 1) if upward else (member - distance >= 0)

    def hop_gets(hop, upward):
        distance = members - 1 - hop
        return (
            ((member >= 1) & (member - 1 + distance <= members - 1))
            if upward
            else ((member <= members - 2) & (member + 1 - distance >= 0))
        )

    def core_stage(unit):
        if unit >= 2:
            core_copy(unit - 2).wait_send()
        targets = owners(unit, core_peer)

        def fill(spot, _):
            owner = targets[3]
            for k in range(3):
                owner = jnp.where(spot == k, targets[k], owner)
            core_out[unit % 2, spot] = partial(unit, owner).astype(BF16)
            return 0

        lax.fori_loop(0, 4, fill, 0)
        if unit >= RING:
            pl.semaphore_wait(credit, 1)
        core_copy(unit).start()

    def near_stage(unit):
        core_copy(unit).wait_recv()
        if unit >= RING:
            near_copy(unit - RING).wait_send()
        mine = owners(unit, row)

        def give(spot, _):
            total = partial(unit, jnp.where(spot == 0, mine[0], mine[1])) + core_in[unit % RING, spot].astype(F32)
            near_out[unit % RING, spot] = total.astype(BF16)
            return 0

        lax.fori_loop(0, 2, give, 0)
        near_copy(unit).start()

        def keep(spot, _):
            near_kept[unit % KEPT, spot] = partial(unit, jnp.where(spot == 0, mine[2], mine[3])) + core_in[
                unit % RING, 2 + spot
            ].astype(F32)
            return 0

        lax.fori_loop(0, 2, keep, 0)
        if unit + RING < count:
            pl.semaphore_signal(credit, inc=1, device_id=(core_peer, member), device_id_type=MESH)

    def far_stage(unit):
        near_copy(unit).wait_recv()
        if unit >= RING:
            far_copy(unit - RING).wait_send()
        far_out[unit % RING] = (near_kept[unit % KEPT, 0] + near_in[unit % ROUND, 1].astype(F32)).astype(BF16)
        far_copy(unit).start()

    def hop_stage(unit, hop):
        if hop == 0:
            far_copy(unit).wait_recv()
            own[unit % RING] = (
                near_kept[unit % KEPT, 1] + near_in[unit % ROUND, 0].astype(F32) + far_in[unit % ROUND].astype(F32)
            )
        for upward in (True, False):
            distance = members - 1 - hop
            owner = jnp.clip(member + distance if upward else member - distance, 0, members - 1)
            place = hop if upward else hops + hop
            block = pl.ds(pl.multiple_of(owner * 256, 256), 256)
            if unit >= RING:
                @pl.when(hop_sends(hop, upward))
                def _():
                    hop_copy(unit - RING, hop, upward).wait_send()

            if hop > 0:
                @pl.when(hop_gets(hop - 1, upward))
                def _():
                    hop_copy(unit, hop - 1, upward).wait_recv()
                    hop_out[unit % RING, place] = (
                        own[unit % RING, :, block] + hop_in[unit, place - 1].astype(F32)
                    ).astype(BF16)

                @pl.when(hop_sends(hop, upward) & jnp.logical_not(hop_gets(hop - 1, upward)))
                def _():
                    hop_out[unit % RING, place] = own[unit % RING, :, block].astype(BF16)

            else:
                @pl.when(hop_sends(hop, upward))
                def _():
                    hop_out[unit % RING, place] = own[unit % RING, :, block].astype(BF16)

            @pl.when(hop_sends(hop, upward))
            def _():
                hop_copy(unit, hop, upward).start()

    def last_stage(unit):
        _, _, out, left_start, left_step, right_start, right_step = units[unit]
        rows, cols = pl.ds(left_start, 128), pl.ds(right_start, 256)
        block = pl.ds(pl.multiple_of(member * 256, 256), 256)
        out_refs[out][rows, cols] = own[unit % RING, :, block]
        for upward in (True, False):
            place = hops - 1 if upward else 2 * hops - 1

            @pl.when(hop_gets(hops - 1, upward))
            def _():
                hop_copy(unit, hops - 1, upward).wait_recv()
                out_refs[out][rows, cols] += hop_in[unit, place].astype(F32)

    pieces = part_ref.shape[2] // back_rows * part_ref.shape[0]
    items_here = part_ref.shape[0]

    def back_copy(piece, step):
        which, start = piece // (pieces // items_here), piece % (pieces // items_here) * back_rows
        target = lax.rem(member - step + members, members)
        return pltpu.make_async_remote_copy(
            src_ref=part_ref.at[which, step, pl.ds(start, back_rows)],
            dst_ref=back_ref.at[member * items_here + which, pl.ds(start, back_rows)],
            send_sem=back_send.at[piece, step],
            recv_sem=back_recv.at[piece, step],
            device_id=(row, target),
            device_id_type=MESH,
        )

    far_tick, hop_tick = 1 + S_LAG, 1 + 2 * S_LAG
    last_tick = hop_tick + hops
    for tick in range(max(count + last_tick, pieces)):
        if tick < pieces:
            for step in range(1, members):
                back_copy(tick, step).start()
        if 0 <= tick - far_tick < count:
            far_stage(tick - far_tick)
        for hop in range(hops):
            if 0 <= tick - hop_tick - hop < count:
                hop_stage(tick - hop_tick - hop, hop)
        if 0 <= tick - last_tick < count:
            last_stage(tick - last_tick)
        if 0 <= tick < count:
            core_stage(tick)
        if 0 <= tick - 1 < count:
            near_stage(tick - 1)
    for unit in range(count - 2, count):
        core_copy(unit).wait_send()
    for unit in range(count - RING, count):
        near_copy(unit).wait_send()
        far_copy(unit).wait_send()
        for hop in range(hops):
            for upward in (True, False):
                @pl.when(hop_sends(hop, upward))
                def _():
                    hop_copy(unit, hop, upward).wait_send()
    for piece in range(pieces):
        for step in range(1, members):
            back_copy(piece, step).wait()


def scatter_by_kernel(pairs, blocks, memory_part, members):
    lefts, rights, units = [], [], []
    for out, ((left, right), (height, width)) in enumerate(zip(pairs, blocks)):
        spots = []
        for value, found in ((left, lefts), (right, rights)):
            for place, other in enumerate(found):
                if other is value:
                    spots.append(place)
                    break
            else:
                spots.append(len(found))
                found.append(value)
        for left_start in range(0, height, 128):
            for right_start in range(0, width, 256):
                units.append((spots[0], spots[1], out, left_start, height, right_start, width))
    count, hops = len(units), members - 1
    items_here, _, mem_local, width = memory_part.shape
    back_rows = 32
    pieces = mem_local // back_rows * items_here
    outs = pl.pallas_call(
        functools.partial(scatter_kernel, members, tuple(units), back_rows),
        out_shape=[jax.ShapeDtypeStruct(block, F32) for block in blocks]
        + [jax.ShapeDtypeStruct((items_here * members, mem_local, width), BF16)],
        in_specs=[VMEM] * (len(lefts) + len(rights)) + [ANY],
        out_specs=[VMEM] * len(blocks) + [ANY],
        scratch_shapes=[
            pltpu.VMEM((2, 4, 128, 1024), BF16),
            pltpu.VMEM((RING, 4, 128, 1024), BF16),
            pltpu.VMEM((RING, 2, 128, 1024), BF16),
            pltpu.VMEM((ROUND, 2, 128, 1024), BF16),
            pltpu.VMEM((KEPT, 2, 128, 1024), F32),
            pltpu.VMEM((RING, 128, 1024), BF16),
            pltpu.VMEM((ROUND, 128, 1024), BF16),
            pltpu.VMEM((RING, 128, 1024), F32),
            pltpu.VMEM((RING, 2 * hops, 128, 256), BF16),
            pltpu.VMEM((count, 2 * hops, 128, 256), BF16),
            pltpu.SemaphoreType.DMA((count, 3 + 2 * hops)),
            pltpu.SemaphoreType.DMA((count, 3 + 2 * hops)),
            pltpu.SemaphoreType.DMA((pieces, members)),
            pltpu.SemaphoreType.DMA((pieces, members)),
            pltpu.SemaphoreType.REGULAR,
        ],
        compiler_params=pltpu.CompilerParams(
            collective_id=1, has_side_effects=True, vmem_limit_bytes=60 * 1024 * 1024
        ),
        name="scatter_all",
    )(*lefts, *rights, memory_part)
    return outs[:-1], outs[-1]


def scatter_by_collectives(pairs, blocks, memory_part, row, member, items_count, members):
    grads = []
    for place, (left, right) in enumerate(pairs):
        ordered = order_columns(left, row, items_count, place % 2 == 1)
        grads += weight_gradients(ordered, [right], items_count, member, members, place % 2 == 1)
    items_here = memory_part.shape[0]
    back = jnp.zeros((items_here * members,) + memory_part.shape[2:], BF16)
    for step in range(1, members):
        part = lax.ppermute(memory_part[:, step], "mem", [(a, (a - step) % members) for a in range(members)])
        owner = lax.rem(member + step, members)
        back = lax.dynamic_update_slice_in_dim(back, part, owner * items_here, 0)
    return grads, back


def body(
    items_count,
    members,
    tokens,
    memory,
    cotangent,
    mem_len,
    dec_len,
    self_query,
    self_key,
    self_value,
    self_out,
    cross_query,
    cross_key,
    cross_value,
    cross_out,
    feed_in,
    feed_out,
    shifts,
    gains,
    inner_bias,
):
    row = lax.axis_index("items")
    member = lax.axis_index("mem")
    rows_here = tokens.shape[0]
    item_count = rows_here // DEC
    group_items = memory.shape[0]
    mem_local = memory.shape[1]
    shards = (
        cross_key, cross_value, self_query, self_key, self_value, self_out, cross_query, cross_out, feed_in, feed_out,
    )
    by_kernel = (items_count, members) == (8, 4)
    shift_width, bias_rows = shifts.shape[1], inner_bias.shape[0] // shifts.shape[1]
    vector = jnp.concatenate([shifts, gains, inner_bias.reshape(bias_rows, shift_width)], 0)
    own_dec = lax.dynamic_slice_in_dim(dec_len, member * item_count, item_count)
    own_mem = lax.dynamic_slice_in_dim(mem_len, member * item_count, item_count)
    if by_kernel:
        whole, item_memory, vectors, forward = gather_by_kernel(
            shards, memory, vector, tokens, jnp.stack([own_dec, own_mem]), items_count, members
        )
    else:
        whole, item_memory, vectors = gather_by_collectives(shards, memory, vector, items_count, members)
    (
        key_cross, value_cross, query_self, key_self, value_self, output_self, query_cross, output_cross,
        feed_up, feed_down,
    ) = whole
    memory_flat = item_memory.reshape(-1, D)
    vectors = vectors.astype(F32)
    bias_start = shifts.shape[0] + gains.shape[0]
    shift_rows = vectors[: shifts.shape[0]]
    gain_rows = vectors[shifts.shape[0] : bias_start]
    inner_shift = (
        vectors[bias_start:].reshape(bias_rows, items_count, shift_width).transpose(1, 0, 2).reshape(-1)
    )

    bases = lax.rem(member - jnp.arange(members, dtype=jnp.int32) + members, members) * mem_local

    if by_kernel:
        (
            queries_one, keys_one, values_one, mixed_one, exact_one, scale_one, hidden_one, normed_one, inverse_one,
            queries_two, mixed_two, exact_two, scale_two, keys_two, values_two,
        ) = forward
        hidden_one_low = hidden_one.astype(BF16)
        keys_two, values_two = keys_two.reshape(-1, D), values_two.reshape(-1, D)
    else:
        tokens_float = tokens.astype(F32)
        queries_one = ((product(tokens, query_self) + shift_rows[0]) * 0.125).astype(BF16)
        keys_one = product(tokens, key_self).astype(BF16)
        values_one = (product(tokens, value_self) + shift_rows[1]).astype(BF16)
        mixed_one, exact_one, scale_one = attend_forward(
            True, DEC, own_dec, bases, queries_one, keys_one, values_one
        )
        resid_one = tokens_float + product(mixed_one, output_self) + shift_rows[2]
        hidden_one, normed_one, inverse_one = norm_forward(resid_one, gain_rows[0], shift_rows[7])
        hidden_one_low = hidden_one.astype(BF16)
        queries_two = ((product(hidden_one_low, query_cross) + shift_rows[3]) * 0.125).astype(BF16)
        keys_two = product(memory_flat, key_cross).astype(BF16)
        values_two = (product(memory_flat, value_cross) + shift_rows[4]).astype(BF16)
        mixed_two, exact_two, scale_two = attend_forward(
            False, mem_local, own_mem, bases, queries_two, keys_two, values_two
        )
    resid_two = hidden_one + product(mixed_two, output_cross) + shift_rows[5]
    hidden_two, normed_two, inverse_two = norm_forward(resid_two, gain_rows[1], shift_rows[8])
    hidden_two_low = hidden_two.astype(BF16)
    inner_pre = product(hidden_two_low, feed_up) + inner_shift
    cdf_part = 0.5 * (1.0 + jax.scipy.special.erf(inner_pre * half_root))
    active_low = (inner_pre * cdf_part).astype(BF16)
    resid_three = hidden_two + product(active_low, feed_down) + shift_rows[6]
    layer_out, normed_three, inverse_three = norm_forward(resid_three, gain_rows[2], shift_rows[9])

    grad_three, gain_grad_three, shift_grad_three = norm_backward(
        cotangent.astype(F32), normed_three, inverse_three, gain_rows[2]
    )
    grad_down = grad_three.astype(BF16)

    out_bias_grad = column_sums(grad_down)
    grad_active = right_product(grad_down, feed_down)
    slope = cdf_part + inner_pre * jnp.exp(-0.5 * inner_pre * inner_pre) * normal_peak
    grad_inner = (grad_active * slope).astype(BF16)
    inner_bias_grad = column_sums(grad_inner)
    grad_hidden_two = grad_three + right_product(grad_inner, feed_up)
    grad_two, gain_grad_two, shift_grad_two = norm_backward(
        grad_hidden_two, normed_two, inverse_two, gain_rows[1]
    )
    grad_cross_branch = grad_two.astype(BF16)
    cross_out_bias_grad = column_sums(grad_cross_branch)
    grad_mixed_two = right_product(grad_cross_branch, output_cross)
    query_grad_two, key_grad_two, value_grad_two = attend_backward(
        False, mem_local, own_mem, bases, queries_two, keys_two, values_two, grad_mixed_two, exact_two, scale_two
    )
    query_grad_two = query_grad_two * jnp.asarray(0.125, BF16)

    memory_part = (
        right_product(key_grad_two, key_cross) + right_product(value_grad_two, value_cross)
    ).astype(BF16).reshape(item_count, members, mem_local, D)
    cross_value_bias_grad = column_sums(value_grad_two)
    cross_query_bias_grad = column_sums(query_grad_two)
    grad_hidden_one = grad_two + right_product(query_grad_two, query_cross)
    grad_one, gain_grad_one, shift_grad_one = norm_backward(
        grad_hidden_one, normed_one, inverse_one, gain_rows[0]
    )
    grad_self_branch = grad_one.astype(BF16)
    self_out_bias_grad = column_sums(grad_self_branch)
    grad_mixed_one = right_product(grad_self_branch, output_self)
    query_grad_one, key_grad_one, value_grad_one = attend_backward(
        True, DEC, own_dec, bases, queries_one, keys_one, values_one, grad_mixed_one, exact_one, scale_one
    )
    query_grad_one = query_grad_one * jnp.asarray(0.125, BF16)
    pairs = (
        (active_low, grad_down),
        (hidden_two_low, grad_inner),
        (mixed_two, grad_cross_branch),
        (memory_flat, key_grad_two),
        (memory_flat, value_grad_two),
        (hidden_one_low, query_grad_two),
        (mixed_one, grad_self_branch),
        (tokens, query_grad_one),
        (tokens, key_grad_one),
        (tokens, value_grad_one),
    )
    blocks = tuple(
        weight.shape
        for weight in (
            feed_out, feed_in, cross_out, cross_key, cross_value, cross_query, self_out, self_query, self_key, self_value,
        )
    )
    if by_kernel:
        grads, memory_back = scatter_by_kernel(pairs, blocks, memory_part, members)
    else:
        grads, memory_back = scatter_by_collectives(pairs, blocks, memory_part, row, member, items_count, members)
    (
        feed_down_grad, feed_up_grad, output_cross_grad, key_cross_grad, value_cross_grad, query_cross_grad,
        output_self_grad, query_self_grad, key_self_grad, value_self_grad,
    ) = grads
    memory_grad = lax.dynamic_update_slice_in_dim(
        memory_back.astype(F32), memory_part[:, 0].astype(F32), member * item_count, 0
    )
    tokens_grad = (
        grad_one
        + right_product(query_grad_one, query_self)
        + right_product(key_grad_one, key_self)
        + right_product(value_grad_one, value_self)
    )
    vectors = jnp.concatenate(
        [
            column_sums(query_grad_one),
            column_sums(value_grad_one),
            self_out_bias_grad,
            cross_query_bias_grad,
            cross_value_bias_grad,
            cross_out_bias_grad,
            out_bias_grad,
            shift_grad_one,
            shift_grad_two,
            shift_grad_three,
            gain_grad_one,
            gain_grad_two,
            gain_grad_three,
            inner_bias_grad,
        ]
    )
    vectors = lax.psum(vectors.reshape(-1, 128), ("items", "mem")).reshape(-1)
    shift_count = shifts.shape[0] * D
    gain_count = gains.shape[0] * D
    shift_width, gain_width, bias_width = shifts.shape[1], gains.shape[1], inner_bias.shape[0]
    shifts_grad = lax.dynamic_slice_in_dim(
        vectors[:shift_count].reshape(-1, D), row * shift_width, shift_width, 1
    )
    gains_grad = lax.dynamic_slice_in_dim(
        vectors[shift_count : shift_count + gain_count].reshape(-1, D), row * gain_width, gain_width, 1
    )
    bias_grad = lax.dynamic_slice_in_dim(vectors[shift_count + gain_count :], row * bias_width, bias_width)
    return (
        layer_out,
        tokens_grad,
        memory_grad,
        query_self_grad,
        key_self_grad,
        value_self_grad,
        output_self_grad,
        query_cross_grad,
        key_cross_grad,
        value_cross_grad,
        output_cross_grad,
        feed_up_grad,
        feed_down_grad,
        shifts_grad,
        gains_grad,
        bias_grad,
    )


def solution(mesh):
    tiles = P("items", "mem")
    rows = P(("items", "mem"), None)
    blocks = P("items", "mem", None)
    return jax.shard_map(
        functools.partial(body, mesh.shape["items"], mesh.shape["mem"]),
        mesh=mesh,
        in_specs=(rows, blocks, rows, P("items"), P("items"))
        + (tiles,) * 10
        + (P(None, "items"), P(None, "items"), P("items")),
        out_specs=(rows, rows, blocks) + (tiles,) * 10 + (P(None, "items"), P(None, "items"), P("items")),
        check_vma=False,
    )
```

```python
import functools

import jax
import jax.numpy as jnp
from jax import lax
from jax.experimental import pallas as pl
from jax.experimental.pallas import tpu as pltpu
from jax.sharding import PartitionSpec as P

D = 1024
HEADS = 16
HEAD_DIM = 64
PAIR = 2 * HEAD_DIM
PAIRS = HEADS // 2
DEC = 128
half_root = 0.7071067811865476
normal_peak = 0.3989422804014327
MESH = pl.DeviceIdType.MESH
F32 = jnp.float32
BF16 = jnp.bfloat16
X_LAG, FIRST_PIECE, SPREAD, STRAIGHT = 1, 2, 16, 3
ANY = pl.BlockSpec(memory_space=pl.ANY)
VMEM = pl.BlockSpec(memory_space=pltpu.VMEM)


def product(first_op, second_op):
    return jnp.dot(first_op, second_op, preferred_element_type=F32)


def left_product(first_op, second_op):
    return lax.dot_general(
        first_op, second_op, (((0,), (0,)), ((), ())), preferred_element_type=F32
    )


def right_product(first_op, second_op):
    return lax.dot_general(
        first_op, second_op, (((1,), (1,)), ((), ())), preferred_element_type=F32
    )


def column_sums(values):
    return jnp.sum(values.astype(F32), 0)


def norm_forward(values, gain, shift):
    center = values - jnp.mean(values, -1, keepdims=True)
    inverse = lax.rsqrt(jnp.mean(center * center, -1, keepdims=True) + 1e-05)
    normed = center * inverse
    return (normed * gain + shift, normed, inverse)


def norm_backward(grad_out, normed, inverse, gain):
    scaled = grad_out * gain
    grad_in = inverse * (
        scaled
        - jnp.mean(scaled, -1, keepdims=True)
        - normed * jnp.mean(scaled * normed, -1, keepdims=True)
    )
    return (grad_in, jnp.sum(grad_out * normed, 0), jnp.sum(grad_out, 0))


def gather_kernel(members, items_here, units, forward, *refs):
    count = len(units)
    weights = 1 + max(unit[0] for unit in units)
    shard_refs = refs[:weights]
    memory_ref, vector_ref, tokens_ref, limits_ref = refs[weights : weights + 4]
    refs = refs[weights + 4 :]
    whole_refs, items_ref, vectors_ref = refs[:weights], refs[weights], refs[weights + 1]
    refs = refs[weights + 2 :]
    outs, refs = refs[: forward.outs], refs[forward.outs :]
    send_sem, recv_sem, copy_sem, mem_send, mem_recv, mem_copy, vec_send, vec_recv, bounce = refs[:9]
    row = lax.axis_index("items")
    member = lax.axis_index("mem")
    hops = members - 1
    core_peer, first_peer, second_peer = row ^ 1, row ^ 2, row ^ 4
    UP, DOWN = 0, hops
    ALONG_X, ALONG_Y, HALF_A, HALF_B, CORE = 2 * hops, 2 * hops + 1, 2 * hops + 2, 2 * hops + 3, 2 * hops + 4

    barrier = pltpu.get_barrier_semaphore()
    partners = [(row ^ distance, member) for distance in range(1, 8)]
    partners += [(row, lax.rem(member + step, members)) for step in range(1, members)]
    for partner in partners:
        pl.semaphore_signal(barrier, inc=1, device_id=partner, device_id_type=MESH)
    pl.semaphore_wait(barrier, len(partners))

    def place(unit, owner):
        weight, start, depth, height = units[unit]
        return pl.ds(pl.multiple_of(owner * height + start, depth), depth)

    def cols(unit, who):
        width = shard_refs[units[unit][0]].shape[1]
        return pl.ds(pl.multiple_of(who * width, width), width)

    def shard(unit):
        weight, start, depth, height = units[unit]
        return shard_refs[weight].at[pl.ds(start, depth)]

    def remote(unit, kind, src, dst, device):
        return pltpu.make_async_remote_copy(
            src_ref=src,
            dst_ref=dst,
            send_sem=send_sem.at[unit, kind],
            recv_sem=recv_sem.at[unit, kind],
            device_id=device,
            device_id_type=MESH,
        )

    def along(unit, hop, upward):
        whole = whole_refs[units[unit][0]]
        origin = member - hop if upward else member + hop
        origin = jnp.clip(origin, 0, members - 1)
        piece = whole.at[place(unit, row), cols(unit, origin)]
        target = jnp.clip(member + 1 if upward else member - 1, 0, members - 1)
        return remote(
            unit, (UP if upward else DOWN) + hop, shard(unit) if hop == 0 else piece, piece, (row, target)
        )

    straight = range(STRAIGHT)

    def straight_copy(unit, hop, upward):
        target = jnp.clip(member + hop + 1 if upward else member - hop - 1, 0, members - 1)
        piece = whole_refs[units[unit][0]].at[place(unit, row), cols(unit, member)]
        return remote(unit, (UP if upward else DOWN) + hop, shard(unit), piece, (row, target))

    def straight_each(unit, act):
        for hop in range(hops):
            @pl.when(member + hop + 1 <= members - 1)
            def _():
                act(straight_copy(unit, hop, True))

            @pl.when(member - hop - 1 >= 0)
            def _():
                act(straight_copy(unit, hop, False))

    def along_start(unit, hop):
        @pl.when((member >= hop) & (member < members - 1))
        def _():
            along(unit, hop, True).start()

        @pl.when((member <= members - 1 - hop) & (member > 0))
        def _():
            along(unit, hop, False).start()

    def along_arrive(unit, hop):
        @pl.when(member >= hop + 1)
        def _():
            along(unit, hop, True).wait_recv()

        @pl.when(member <= members - 2 - hop)
        def _():
            along(unit, hop, False).wait_recv()

    def along_sent(unit, hop):
        @pl.when((member >= hop) & (member < members - 1))
        def _():
            along(unit, hop, True).wait_send()

        @pl.when((member <= members - 1 - hop) & (member > 0))
        def _():
            along(unit, hop, False).wait_send()

    def own_copy(unit):
        return pltpu.make_async_copy(
            shard(unit), whole_refs[units[unit][0]].at[place(unit, row), cols(unit, member)], copy_sem.at[unit]
        )

    def block(unit, kind, owner, device, half=None):
        weight, start, depth, height = units[unit]
        if half is None:
            rows = place(unit, owner)
        else:
            part = depth // 2
            rows = pl.ds(pl.multiple_of(owner * height + start + half * part, part), part)
        ref = whole_refs[weight].at[rows]
        return remote(unit, kind, ref, ref, (device, member))

    def to_x(unit):
        return block(unit, ALONG_X, row, first_peer)

    def to_y(unit):
        return block(unit, ALONG_Y, row, second_peer)

    def half_a(unit):
        return block(unit, HALF_A, first_peer, second_peer, 0)

    def half_b(unit):
        return block(unit, HALF_B, second_peer, first_peer, 1)

    def to_core(unit, which):
        owner = (row, first_peer, second_peer, row ^ 6)[which]
        return block(unit, CORE + which, owner, core_peer)

    pieces = memory_ref.shape[1] // 32 * items_here

    def memory_send(piece, step):
        which, start = piece // (pieces // items_here), piece % (pieces // items_here) * 32
        target = lax.rem(member + step, members)
        return pltpu.make_async_remote_copy(
            src_ref=memory_ref.at[target * items_here + which, pl.ds(start, 32)],
            dst_ref=items_ref.at[which, step, pl.ds(start, 32)],
            send_sem=mem_send.at[piece, step],
            recv_sem=mem_recv.at[piece, step],
            device_id=(row, target),
            device_id_type=MESH,
        )

    fetch = pltpu.make_async_copy(memory_ref.at[pl.ds(member * items_here, items_here)], bounce, mem_copy.at[0])
    local = pltpu.make_async_copy(bounce, items_ref.at[:, 0], mem_copy.at[1])
    fetch.start()
    spot = vectors_ref.at[:, pl.ds(pl.multiple_of(row * 128, 128), 128)]
    vector_copies = [
        pltpu.make_async_remote_copy(
            src_ref=vector_ref,
            dst_ref=spot,
            send_sem=vec_send.at[distance],
            recv_sem=vec_recv.at[distance],
            device_id=(row ^ distance, member),
            device_id_type=MESH,
        )
        for distance in range(1, 8)
    ]
    vector_copies.append(pltpu.make_async_copy(vector_ref, spot, vec_send.at[0]))
    for copy in vector_copies:
        copy.start()

    due = [FIRST_PIECE + piece * SPREAD // pieces for piece in range(pieces)]
    plane_lag = 1
    done_lag = plane_lag + 2 * X_LAG + 1
    jobs = forward.jobs(
        members, items_here, member, tokens_ref, limits_ref, whole_refs, items_ref, vectors_ref, outs, refs[9:],
        done_lag, due,
    )
    last = max([count - 1 + done_lag, due[-1] + 2] + list(jobs))
    for tick in range(last + 1):
        if tick in straight:
            straight_each(tick, lambda copy: copy.start())
            own_copy(tick).start()
        for hop in range(hops):
            unit = tick + hops - plane_lag - hop
            if unit not in straight and 0 <= unit < count:
                if hop == 0:
                    own_copy(unit).start()
                else:
                    along_arrive(unit, hop - 1)
                along_start(unit, hop)
        for piece in range(pieces):
            if due[piece] == tick:
                for step in range(1, members):
                    memory_send(piece, step).start()
        unit = tick - plane_lag
        if 0 <= unit < count:
            for hop in range(hops) if unit in straight else (hops - 1,):
                along_arrive(unit, hop)
            own_copy(unit).wait()
            to_x(unit).start()
            to_y(unit).start()
            to_core(unit, 0).start()
        unit = tick - plane_lag - X_LAG
        if 0 <= unit < count:
            to_x(unit).wait_recv()
            half_a(unit).start()
            to_core(unit, 1).start()
            to_y(unit).wait_recv()
            half_b(unit).start()
            to_core(unit, 2).start()
        unit = tick - plane_lag - 2 * X_LAG
        if 0 <= unit < count:
            half_a(unit).wait_recv()
            half_b(unit).wait_recv()
            to_core(unit, 3).start()
        if tick == 1:
            fetch.wait()
            local.start()
        if tick == 3:
            local.wait()
            for copy in vector_copies:
                copy.wait()
        unit = tick - done_lag
        if 0 <= unit < count:
            for which in range(4):
                to_core(unit, which).wait_recv()
        for piece in range(pieces):
            if due[piece] + 2 == tick:
                for step in range(1, members):
                    memory_send(piece, step).wait_recv()
        for job in jobs.get(tick, ()):
            job()
    for unit in range(count):
        if unit in straight:
            straight_each(unit, lambda copy: copy.wait_send())
        else:
            for hop in range(hops):
                along_sent(unit, hop)
        to_x(unit).wait_send()
        to_y(unit).wait_send()
        half_a(unit).wait_send()
        half_b(unit).wait_send()
        for which in range(4):
            to_core(unit, which).wait_send()
    for piece in range(pieces):
        for step in range(1, members):
            memory_send(piece, step).wait_send()
    forward.finish()


def attend_pair(queries, keys_at, values_at, allowed_at, chunks):
    lane_low = low_lanes(DEC)
    q2 = stack_pair(queries, lane_low)
    numer, total = None, None
    for step in range(chunks):
        scores = right_product(q2, keys_at(step))
        exp_scores = jnp.where(allowed_at(step), jnp.exp(scores), 0.0)
        part = jnp.sum(exp_scores, -1, keepdims=True)
        term = product(exp_scores.astype(BF16), values_at(step))
        total = part if total is None else total + part
        numer = term if numer is None else numer + term
    numer = jnp.where(lane_low, numer[:DEC], numer[DEC:])
    scale = 1.0 / jnp.where(lane_low, total[:DEC], total[DEC:])
    return numer * scale, scale


class Forward:
    outs = 16

    def __init__(self, rows, items_here, members, mem_local):
        self.rows, self.items_here, self.members, self.mem_local = rows, items_here, members, mem_local
        self.slots = members * mem_local

    def out_shapes(self):
        wide, low = jax.ShapeDtypeStruct((self.rows, D), F32), jax.ShapeDtypeStruct((self.rows, D), BF16)
        keys = jax.ShapeDtypeStruct((self.items_here, self.members, self.mem_local, D), BF16)
        inverse = jax.ShapeDtypeStruct((self.rows, 1), F32)
        return [low, low, low, low, wide, wide, wide, low, wide, inverse, low, low, wide, wide, keys, keys]

    def out_specs(self):
        return [VMEM] * 14 + [ANY] * 2

    def scratch(self):
        return [
            pltpu.VMEM((2, D, D), BF16),
            pltpu.VMEM((2, D, D), BF16),
            pltpu.VMEM((2, self.members, self.mem_local // 4, D), BF16),
            pltpu.VMEM((self.items_here, self.members, self.mem_local, D), BF16),
            pltpu.VMEM((self.items_here, self.members, self.mem_local, D), BF16),
            pltpu.SemaphoreType.DMA((16,)),
        ]

    def jobs(
        self, members, items_here, member, tokens_ref, limits_ref, whole_refs, items_ref, vectors_ref, outs, scratch,
        done_lag, due,
    ):
        (
            q_one, k_one, v_one, mixed_one, exact_one, scale_one, hidden_one, hidden_low, normed_one, inverse_one, q_two,
            mixed_two, exact_two, scale_two, keys_out, values_out,
        ) = outs
        weight_buf, cross_buf, rows_buf, keys, values, sems = scratch
        part = self.mem_local // 4
        schedule = {}

        def at(tick, job):
            schedule.setdefault(tick, []).append(job)

        def vector(index):
            return vectors_ref[...].astype(F32)[index : index + 1]

        def fetch_weight(unit, slot):
            return pltpu.make_async_copy(whole_refs[unit], weight_buf.at[slot], sems.at[slot])

        def fetch_cross(unit):
            return pltpu.make_async_copy(whole_refs[unit], cross_buf.at[unit], sems.at[2 + unit])

        def fetch_rows(which, chunk):
            slot = chunk % 2
            return pltpu.make_async_copy(
                items_ref.at[which, :, pl.ds(chunk * part, part)], rows_buf.at[slot], sems.at[4 + slot]
            )

        def store(which, value):
            source, target = ((keys, keys_out), (values, values_out))[value]
            return pltpu.make_async_copy(source.at[which], target.at[which], sems.at[6 + 2 * which + value])

        self.pending = []

        def project(slot, unit, result, shift, scale):
            def job():
                fetch_weight(unit, slot).wait()
                total = product(tokens_ref[...], weight_buf[slot])
                if shift is not None:
                    total = total + vector(shift)
                if scale is not None:
                    total = total * scale
                result[...] = total.astype(BF16)

            return job

        def self_attend(which):
            def job():
                limit = limits_ref[0:1, which : which + 1]
                slot = lax.broadcasted_iota(jnp.int32, (2 * DEC, DEC), 1)
                query = lax.broadcasted_iota(jnp.int32, (2 * DEC, DEC), 0) % DEC
                allowed = (slot <= query) & (slot < limit)
                rows = pl.ds(which * DEC, DEC)

                def pair(p, _):
                    cols = pl.ds(pl.multiple_of(p * PAIR, PAIR), PAIR)
                    exact, scale = attend_pair(
                        q_one[rows, cols], lambda _: k_one[rows, cols], lambda _: v_one[rows, cols], lambda _: allowed, 1
                    )
                    mixed_one[rows, cols] = exact.astype(BF16)
                    exact_one[rows, cols] = exact
                    scale_one[rows, cols] = scale
                    return 0

                lax.fori_loop(0, PAIRS, pair, 0)

            return job

        def first_norm(slot, unit):
            def job():
                fetch_weight(unit, slot).wait()
                resid = tokens_ref[...].astype(F32) + product(mixed_one[...], weight_buf[slot]) + vector(2)
                hidden, normed, inverse = norm_forward(resid, vector(10), vector(7))
                hidden_one[...] = hidden
                hidden_low[...] = hidden.astype(BF16)
                normed_one[...] = normed
                inverse_one[...] = inverse

            return job

        def cross_query(slot, unit):
            def job():
                fetch_weight(unit, slot).wait()
                total = (product(hidden_low[...], weight_buf[slot]) + vector(3)) * 0.125
                q_two[...] = total.astype(BF16)

            return job

        def project_rows(which, chunk):
            def job():
                fetch_rows(which, chunk).wait()
                rows = rows_buf[chunk % 2].reshape(members * part, D)
                new_keys = product(rows, cross_buf[0]).astype(BF16).reshape(members, part, D)
                new_values = (product(rows, cross_buf[1]) + vector(4)).astype(BF16).reshape(members, part, D)
                keys[which, :, pl.ds(chunk * part, part)] = new_keys
                values[which, :, pl.ds(chunk * part, part)] = new_values
                if chunk == 3:
                    store(which, 0).start()
                    store(which, 1).start()

            return job

        def cross_attend(which, low, high):
            def job():
                rows = pl.ds(which * DEC, DEC)
                limit = limits_ref[1:2, which : which + 1]
                slot = lax.broadcasted_iota(jnp.int32, (2 * DEC, self.mem_local), 1)

                def allowed(step):
                    return slot < limit - lax.rem(member - step + members, members) * self.mem_local

                def pair(p, _):
                    cols = pl.ds(pl.multiple_of(p * PAIR, PAIR), PAIR)
                    exact, scale = attend_pair(
                        q_two[rows, cols],
                        lambda step: keys[which, step, :, cols],
                        lambda step: values[which, step, :, cols],
                        allowed,
                        members,
                    )
                    mixed_two[rows, cols] = exact.astype(BF16)
                    exact_two[rows, cols] = exact
                    scale_two[rows, cols] = scale
                    return 0

                lax.fori_loop(low, high, pair, 0)

            return job

        for unit in range(2):
            at(unit + done_lag, fetch_cross(unit).start)
        for unit in range(2, 7):
            at(unit + done_lag, fetch_weight(unit, unit % 2).start)
        at(1 + done_lag + 1, fetch_cross(0).wait)
        at(1 + done_lag + 1, fetch_cross(1).wait)
        start = 2 + done_lag + 1
        at(start, project(0, 2, q_one, 0, 0.125))
        at(start + 1, project(1, 3, k_one, None, None))
        at(start + 2, project(0, 4, v_one, 1, None))
        at(start + 2, self_attend(0))
        at(start + 3, self_attend(1))
        at(start + 3, first_norm(1, 5))
        at(start + 4, cross_query(0, 6))
        previous = 1 + done_lag
        per_item = len(due) // items_here
        for which in range(items_here):
            for chunk in range(4):
                ready = due[which * per_item + (chunk + 1) * per_item // 4 - 1] + 2
                begin = max(ready, previous)
                at(begin, fetch_rows(which, chunk).start)
                late = begin if which == items_here - 1 and chunk == 3 else begin + 1
                at(late, project_rows(which, chunk))
                previous = begin + 1
            begin = max(previous, start + 5)
            if which < items_here - 1:
                for quarter in range(4):
                    at(begin + quarter, cross_attend(which, 2 * quarter, 2 * quarter + 2))
            else:
                at(late, cross_attend(which, 0, PAIRS))
        self.pending = [store(which, value) for which in range(items_here) for value in range(2)]
        return schedule

    def finish(self):
        for copy in self.pending:
            copy.wait()


def gather_by_kernel(shards, memory, vector, tokens, limits, items_count, members):
    items_here = memory.shape[0] // members
    units = []
    for weight, shard in enumerate(shards):
        height, width = shard.shape
        depth = height * 256 // max(height * width // 128, 256)
        for start in range(0, height, depth):
            units.append((weight, start, depth, height))
    forward = Forward(tokens.shape[0], items_here, members, memory.shape[1])
    pieces = memory.shape[1] // 32 * items_here
    hops = members - 1
    kinds = 2 * hops + 8
    out_shape = [jax.ShapeDtypeStruct((s.shape[0] * items_count, s.shape[1] * members), s.dtype) for s in shards]
    out_shape.append(
        jax.ShapeDtypeStruct((items_here, members, memory.shape[1], memory.shape[2]), memory.dtype)
    )
    out_shape.append(jax.ShapeDtypeStruct((vector.shape[0], vector.shape[1] * items_count), vector.dtype))
    gathered = len(out_shape)
    out_shape += forward.out_shapes()
    outs = pl.pallas_call(
        functools.partial(gather_kernel, members, items_here, tuple(units), forward),
        out_shape=out_shape,
        in_specs=[VMEM] * len(shards) + [ANY, VMEM, VMEM, VMEM],
        out_specs=[ANY] * (gathered - 1) + [VMEM] + forward.out_specs(),
        scratch_shapes=[
            pltpu.SemaphoreType.DMA((len(units), kinds)),
            pltpu.SemaphoreType.DMA((len(units), kinds)),
            pltpu.SemaphoreType.DMA((len(units),)),
            pltpu.SemaphoreType.DMA((pieces, members)),
            pltpu.SemaphoreType.DMA((pieces, members)),
            pltpu.SemaphoreType.DMA((2,)),
            pltpu.SemaphoreType.DMA((items_count,)),
            pltpu.SemaphoreType.DMA((items_count,)),
            pltpu.VMEM((items_here,) + memory.shape[1:], memory.dtype),
        ]
        + forward.scratch(),
        compiler_params=pltpu.CompilerParams(
            collective_id=0, has_side_effects=True, vmem_limit_bytes=60 * 1024 * 1024
        ),
        name="gather_all",
    )(*shards, memory, vector, tokens, limits)
    return outs[: gathered - 2], outs[gathered - 2], outs[gathered - 1], outs[gathered:]


def gather_by_collectives(shards, memory, vector, items_count, members):
    whole = []
    for shard in shards:
        cols = lax.all_gather(shard, "mem", axis=1, tiled=True)
        whole.append(lax.all_gather(cols, "items", axis=0, tiled=True))
    items_here = memory.shape[0] // members
    member = lax.axis_index("mem")
    parts = []
    for step in range(members):
        target = lax.rem(member + step, members)
        part = lax.dynamic_slice_in_dim(memory, target * items_here, items_here)
        if step:
            part = lax.ppermute(part, "mem", [(a, (a + step) % members) for a in range(members)])
        parts.append(part)
    return whole, jnp.stack(parts, 1), lax.all_gather(vector, "items", axis=1, tiled=True)


def stack_pair(values, lane_low):
    zero = jnp.zeros_like(values)
    return jnp.concatenate([jnp.where(lane_low, values, zero), jnp.where(lane_low, zero, values)], 0)


def low_lanes(rows):
    return lax.broadcasted_iota(jnp.int32, (rows, PAIR), 1) < HEAD_DIM


def allowed_slots(causal, chunk, lens_ref, bases_ref, which, step, key_dim):
    shape = (2 * DEC, chunk) if key_dim == 1 else (chunk, 2 * DEC)
    slot = lax.broadcasted_iota(jnp.int32, shape, key_dim)
    if causal:
        query = lax.broadcasted_iota(jnp.int32, shape, 1 - key_dim) % DEC
        return (slot <= query) & (slot < lens_ref[which])
    return slot < lens_ref[which] - bases_ref[step]


def attend_forward_kernel(causal, chunk, lens_ref, bases_ref, q_ref, k_ref, v_ref, mixed_ref, exact_ref, scale_ref):
    which = pl.program_id(0)
    lane_low = low_lanes(DEC)
    q2 = stack_pair(q_ref[...], lane_low)
    numer = jnp.zeros((2 * DEC, PAIR), F32)
    total = jnp.zeros((2 * DEC, 1), F32)
    for step in range(k_ref.shape[0] // chunk):
        rows = pl.ds(step * chunk, chunk)
        scores = right_product(q2, k_ref[rows, :])
        allowed = allowed_slots(causal, chunk, lens_ref, bases_ref, which, step, 1)
        exp_scores = jnp.where(allowed, jnp.exp(scores), 0.0)
        total += jnp.sum(exp_scores, -1, keepdims=True)
        numer += product(exp_scores.astype(BF16), v_ref[rows, :])
    numer = jnp.where(lane_low, numer[:DEC], numer[DEC:])
    scale = 1.0 / jnp.where(lane_low, total[:DEC], total[DEC:])
    exact = numer * scale
    mixed_ref[...] = exact.astype(BF16)
    exact_ref[...] = exact
    scale_ref[...] = scale


def attend_backward_kernel(
    causal, chunk, lens_ref, bases_ref, q_ref, k_ref, v_ref, grad_ref, exact_ref, scale_ref, gq_ref, gk_ref, gv_ref
):
    which = pl.program_id(0)
    lane_low = low_lanes(DEC)
    q2 = stack_pair(q_ref[...], lane_low)
    grad_numer = grad_ref[...] * scale_ref[...]
    gn2 = stack_pair(grad_numer.astype(BF16), lane_low)
    weighted = jnp.transpose(grad_numer * exact_ref[...])
    grad_total = -jnp.concatenate(
        [
            jnp.sum(weighted[:HEAD_DIM], 0, keepdims=True),
            jnp.sum(weighted[HEAD_DIM:], 0, keepdims=True),
        ],
        1,
    )
    gq2 = jnp.zeros((2 * DEC, PAIR), F32)
    for step in range(k_ref.shape[0] // chunk):
        rows = pl.ds(step * chunk, chunk)
        keys = k_ref[rows, :]
        scores = right_product(keys, q2)
        allowed = allowed_slots(causal, chunk, lens_ref, bases_ref, which, step, 0)
        exp_scores = jnp.where(allowed, jnp.exp(scores), 0.0)
        grad_exp = right_product(v_ref[rows, :], gn2) + grad_total
        grad_scores = (exp_scores * grad_exp).astype(BF16)
        gk_ref[rows, :] = product(grad_scores, q2).astype(BF16)
        gv_ref[rows, :] = product(exp_scores.astype(BF16), gn2).astype(BF16)
        gq2 += left_product(grad_scores, keys)
    gq_ref[...] = jnp.where(lane_low, gq2[:DEC], gq2[DEC:]).astype(BF16)


def attention_call(kernel, causal, chunk, lens, bases, queries, keys, values, more, outs):
    item_count = lens.shape[0]
    slots = keys.shape[0] // item_count
    q_spec = pl.BlockSpec((DEC, PAIR), lambda a, p, *_: (a, p))
    k_spec = pl.BlockSpec((slots, PAIR), lambda a, p, *_: (a, p))
    spec = {"q": q_spec, "k": k_spec}
    rows = {"q": queries.shape[0], "k": keys.shape[0]}
    return pl.pallas_call(
        functools.partial(kernel, causal, chunk),
        grid_spec=pltpu.PrefetchScalarGridSpec(
            num_scalar_prefetch=2,
            grid=(item_count, PAIRS),
            in_specs=[q_spec, k_spec, k_spec] + [q_spec] * len(more),
            out_specs=[spec[kind] for kind, _ in outs],
        ),
        out_shape=[jax.ShapeDtypeStruct((rows[kind], D), dtype) for kind, dtype in outs],
        cost_estimate=pl.CostEstimate(
            flops=4 * item_count * HEADS * DEC * slots * 256, bytes_accessed=16 * D * slots, transcendentals=0
        ),
        name="self_attention" if causal else "cross_attention",
    )(lens, bases, queries, keys, values, *more)


def attend_forward(causal, chunk, lens, bases, queries, keys, values):
    return attention_call(
        attend_forward_kernel, causal, chunk, lens, bases, queries, keys, values, (),
        (("q", BF16), ("q", F32), ("q", F32)),
    )


def attend_backward(causal, chunk, lens, bases, queries, keys, values, grad_mixed, exact, scale):
    return attention_call(
        attend_backward_kernel, causal, chunk, lens, bases, queries, keys, values, (grad_mixed, exact, scale),
        (("q", BF16), ("k", BF16), ("k", BF16)),
    )


def halving_order(items_count, flipped):
    bits = [1 << b for b in range(1, items_count.bit_length() - 1)]
    return [1] + (bits if flipped else bits[::-1])


def block_order(items_count, flipped):
    bits = halving_order(items_count, flipped)
    order = []
    for spot in range(items_count):
        distance = 0
        for place, bit in enumerate(bits):
            if spot >> (len(bits) - 1 - place) & 1:
                distance |= bit
        order.append(distance)
    return order


def order_columns(values, row, items_count, flipped):
    width = values.shape[1] // items_count
    return jnp.concatenate(
        [
            lax.dynamic_slice_in_dim(values, (row ^ distance) * width, width, 1)
            for distance in block_order(items_count, flipped)
        ],
        1,
    )


def reduce_rows(partial, items_count, flipped):
    for bit in halving_order(items_count, flipped):
        half = partial.shape[0] // 2
        arrived = lax.ppermute(partial[half:], "items", [(a, a ^ bit) for a in range(items_count)])
        partial = (partial[:half].astype(F32) + arrived.astype(F32)).astype(BF16)
    return partial


def reduce_columns(partial, member, members):
    bit = members // 2
    while bit:
        half = partial.shape[1] // 2
        high = (member & bit) != 0
        left, right = partial[:, :half], partial[:, half:]
        arrived = lax.ppermute(
            jnp.where(high, left, right), "mem", [(a, a ^ bit) for a in range(members)]
        )
        partial = jnp.where(high, right, left).astype(F32) + arrived.astype(F32)
        if bit > 1:
            partial = partial.astype(BF16)
        bit //= 2
    return partial


def weight_gradients(left_ordered, grads, items_count, member, members, flipped):
    width = grads[0].shape[1]
    joined = grads[0] if len(grads) == 1 else jnp.concatenate(grads, 1)
    partial = left_product(left_ordered, joined).astype(BF16)
    partial = reduce_rows(partial, items_count, flipped)
    return [
        reduce_columns(partial[:, k * width : (k + 1) * width], member, members) for k in range(len(grads))
    ]

RING, KEPT, ROUND, CORES = 4, 6, 10, 3
BACK_PIECES, BACK_WEIGHT, DIRECT = 8, 4, 0
S_LAG = 3


def total_grads(weighted):
    weighted = jnp.transpose(weighted)
    return -jnp.concatenate(
        [jnp.sum(weighted[:HEAD_DIM], 0, keepdims=True), jnp.sum(weighted[HEAD_DIM:], 0, keepdims=True)], 1
    )


def attend_back_chunk(q2, gn2, grad_total, keys, values, allowed):
    exp_scores = jnp.where(allowed, jnp.exp(right_product(keys, q2)), 0.0)
    grad_exp = right_product(values, gn2) + grad_total
    grad_scores = (exp_scores * grad_exp).astype(BF16)
    return product(grad_scores, q2), product(exp_scores.astype(BF16), gn2), left_product(grad_scores, keys)


class Given:
    (
        active, grad_down, hidden_two, slope, feed_down, feed_up, grad_three, normed_two, mixed_two, q_two, exact_two,
        scale_two, tokens, mixed_one, hidden_one, normed_one, q_one, k_one, v_one, keys, values, memory, exact_one,
        scale_one, output_cross, key_cross, value_cross, query_cross, output_self, query_self, key_self, value_self,
    ) = range(32)
    count = 32


class Small:
    inverse_one, inverse_two, gains, limits, vectors = range(5)
    count = 5


class Block:
    fo, fi, co, ck, cv, cq, so, sq, sk, sv = range(10)
    count = 10


def scatter_kernel(members, items_here, mem_local, *refs):
    big, refs = refs[: Given.count], refs[Given.count :]
    small, refs = refs[: Small.count], refs[Small.count :]
    out_refs, refs = refs[: Block.count], refs[Block.count :]
    tokens_grad, vector_out, part_ref, back_ref = refs[:4]
    (
        wide, grad_down, hidden_two, mixed_two, grad_cross, q_two, tokens, mixed_one, hidden_one, normed_one,
        grad_mixed, exact, scale, grad_numer_low, grad_total, key_buf, value_buf, gk_two, gv_two,
        gq_two, weight_buf,
        grad_self, stage, vector_sum, vector_in, vector_far,
        core_out, core_in, near_out, near_in, near_kept, far_out, far_in, own, hop_out, hop_in,
        send_sem, recv_sem, back_send, back_recv, credit, load_sem, kv_sem, stage_sem, vec_send, vec_recv,
    ) = refs[4:]
    gq_one, q_one, k_one, v_one = key_buf.at[0], key_buf.at[1], value_buf.at[0], value_buf.at[1]
    gk_one, gv_one = stage.at[0], stage.at[1]
    row = lax.axis_index("items")
    member = lax.axis_index("mem")
    hops = members - 1
    core_peer = row ^ 1
    slots = members * mem_local

    loads = {}

    def load(name, source, target):
        loads[name] = pltpu.make_async_copy(source, target, load_sem.at[len(loads)])
        loads[name].start()

    def loaded(*names):
        for name in names:
            loads[name].wait()

    def whole(name, target):
        load(name, big[name], target)

    def down_load(k):
        load((Given.feed_down, k), big[Given.feed_down].at[pl.ds(k * D, D)], weight_buf.at[0])

    def up_load(k):
        load((Given.feed_up, k), big[Given.feed_up].at[:, pl.ds(k * D, D)], weight_buf.at[1])

    def slope_load(k):
        load((Given.slope, k), big[Given.slope].at[:, pl.ds(k * D, D)], (exact, scale)[k % 2])

    whole(Given.grad_down, grad_down)
    for k in range(4):
        load((Given.active, k), big[Given.active].at[:, pl.ds(k * D, D)], wide.at[pl.ds(k * 256, 256)])
    down_load(0)
    slope_load(0)
    up_load(0)
    slope_load(1)
    whole(Given.grad_three, tokens_grad)
    whole(Given.normed_two, normed_one)
    whole(Given.q_two, q_two)
    whole(Given.hidden_two, hidden_two)
    whole(Given.mixed_two, mixed_two)
    whole(Given.hidden_one, hidden_one)
    whole(Given.mixed_one, mixed_one)
    whole(Given.tokens, tokens)

    barrier = pltpu.get_barrier_semaphore()
    partners = [(row ^ distance, member) for distance in range(1, 8)]
    partners += [(row, lax.rem(member + step, members)) for step in range(1, members)]
    for partner in partners:
        pl.semaphore_signal(barrier, inc=1, device_id=partner, device_id_type=MESH)
    pl.semaphore_wait(barrier, len(partners))

    units = [(Block.fo, k) for k in range(4)] + [(Block.fi, k) for k in range(4)]
    units += [(name, 0) for name in range(Block.co, Block.count)]
    count = len(units)
    factors = {
        Block.co: (mixed_two, grad_cross),
        Block.ck: (wide, gk_two),
        Block.cv: (wide, gv_two),
        Block.cq: (hidden_one, gq_two),
        Block.so: (mixed_one, grad_self),
        Block.sq: (tokens, gq_one),
        Block.sk: (tokens, gk_one),
        Block.sv: (tokens, gv_one),
    }
    needs = {
        0: (Given.grad_down,) + tuple((Given.active, k) for k in range(4)),
        4: (Given.hidden_two,),
        8: (Given.mixed_two,),
        9: (Given.memory,),
        11: (Given.hidden_one,),
        12: (Given.mixed_one,),
        13: (Given.tokens,),
    }

    def bits(unit):
        return (2, 4) if unit % 2 == 0 else (4, 2)

    def owners(unit, who):
        near, far = bits(unit)
        return (who ^ near, who ^ near ^ far, who ^ far, who)

    def lanes(start, size):
        return pl.ds(pl.multiple_of(start, 128), size)

    def partial(unit, owner):
        name, k = units[unit]
        if name == Block.fo:
            left = wide[pl.ds(pl.multiple_of(owner // 2 * 256, 256), 256), lanes(owner % 2 * 512 + k * 128, 128)]
            return left_product(left, grad_down[...])
        if name == Block.fi:
            right = jnp.concatenate(
                [wide[pl.ds(D + part * 256, 256), pl.ds(k * 256, 256)] for part in range(members)], 1
            )
            return left_product(hidden_two[:, lanes(owner * 128, 128)], right)
        left_ref, right_ref = factors[name]
        depth = right_ref.shape[0]
        if depth <= 512:
            return left_product(left_ref[:, lanes(owner * 128, 128)], right_ref[...])

        def term(spot, sums):
            rows = pl.ds(pl.multiple_of(spot * 512, 512), 512)
            return sums + left_product(left_ref[rows, lanes(owner * 128, 128)], right_ref[rows, :])

        return lax.fori_loop(0, depth // 512, term, jnp.zeros((128, D), F32))

    def remote(unit, kind, src, dst, device):
        return pltpu.make_async_remote_copy(
            src_ref=src,
            dst_ref=dst,
            send_sem=send_sem.at[unit, kind],
            recv_sem=recv_sem.at[unit, kind],
            device_id=device,
            device_id_type=MESH,
        )

    def core_copy(unit):
        return remote(unit, 0, core_out.at[unit % 2], core_in.at[unit % CORES], (core_peer, member))

    def near_copy(unit):
        return remote(
            unit, 1, near_out.at[unit % RING], near_in.at[unit % ROUND], (row ^ bits(unit)[0], member)
        )

    def far_copy(unit):
        return remote(unit, 2, far_out.at[unit % RING], far_in.at[unit % ROUND], (row ^ bits(unit)[1], member))

    direct = range(count - DIRECT, count)

    def hop_copy(unit, hop, upward):
        reach = members - 1 - hop if unit in direct else 1
        target = jnp.clip(member + reach if upward else member - reach, 0, members - 1)
        place = hop if upward else hops + hop
        return remote(
            unit, 3 + place, hop_out.at[unit % RING, place], hop_in.at[unit % ROUND, place], (row, target)
        )

    def hop_sends(hop, upward):
        distance = members - 1 - hop
        return (member + distance <= members - 1) if upward else (member - distance >= 0)

    def hop_gets(unit, hop, upward):
        distance = members - 1 - hop
        if unit in direct:
            return (member >= distance) if upward else (member <= members - 1 - distance)
        return (
            ((member >= 1) & (member - 1 + distance <= members - 1))
            if upward
            else ((member <= members - 2) & (member + 1 - distance >= 0))
        )

    def core_stage(unit):
        loaded(*needs.get(unit, ()))
        if unit >= 2:
            core_copy(unit - 2).wait_send()
        targets = owners(unit, core_peer)

        def fill(spot, _):
            owner = targets[3]
            for k in range(3):
                owner = jnp.where(spot == k, targets[k], owner)
            core_out[unit % 2, spot] = partial(unit, owner).astype(BF16)
            return 0

        lax.fori_loop(0, 4, fill, 0)
        if unit >= CORES:
            pl.semaphore_wait(credit, 1)
        core_copy(unit).start()

    def near_stage(unit):
        core_copy(unit).wait_recv()
        if unit >= RING:
            near_copy(unit - RING).wait_send()
        mine = owners(unit, row)

        def give(spot, _):
            total = partial(unit, jnp.where(spot == 0, mine[0], mine[1])) + core_in[unit % CORES, spot].astype(F32)
            near_out[unit % RING, spot] = total.astype(BF16)
            return 0

        lax.fori_loop(0, 2, give, 0)
        near_copy(unit).start()

        def keep(spot, _):
            total = partial(unit, jnp.where(spot == 0, mine[2], mine[3])) + core_in[unit % CORES, 2 + spot].astype(F32)
            near_kept[unit % KEPT, spot] = total.astype(BF16)
            return 0

        lax.fori_loop(0, 2, keep, 0)
        if unit + CORES < count:
            pl.semaphore_signal(credit, inc=1, device_id=(core_peer, member), device_id_type=MESH)

    def far_stage(unit):
        near_copy(unit).wait_recv()
        if unit >= RING:
            far_copy(unit - RING).wait_send()
        far_out[unit % RING] = (
            near_kept[unit % KEPT, 0].astype(F32) + near_in[unit % ROUND, 1].astype(F32)
        ).astype(BF16)
        far_copy(unit).start()

    def hop_stage(unit, hop):
        if hop == 0:
            far_copy(unit).wait_recv()
            own[unit % RING] = (
                near_kept[unit % KEPT, 1].astype(F32)
                + near_in[unit % ROUND, 0].astype(F32)
                + far_in[unit % ROUND].astype(F32)
            )
        for upward in (True, False):
            distance = members - 1 - hop
            owner = jnp.clip(member + distance if upward else member - distance, 0, members - 1)
            place = hop if upward else hops + hop
            block = lanes(owner * 256, 256)
            if unit >= RING:
                @pl.when(hop_sends(hop, upward))
                def _():
                    hop_copy(unit - RING, hop, upward).wait_send()

            if hop > 0 and unit not in direct:
                arrived = hop_gets(unit, hop - 1, upward)

                @pl.when(arrived)
                def _():
                    hop_copy(unit, hop - 1, upward).wait_recv()
                    hop_out[unit % RING, place] = (
                        own[unit % RING, :, block] + hop_in[unit % ROUND, place - 1].astype(F32)
                    ).astype(BF16)

                @pl.when(hop_sends(hop, upward) & jnp.logical_not(arrived))
                def _():
                    hop_out[unit % RING, place] = own[unit % RING, :, block].astype(BF16)

            else:
                @pl.when(hop_sends(hop, upward))
                def _():
                    hop_out[unit % RING, place] = own[unit % RING, :, block].astype(BF16)

            @pl.when(hop_sends(hop, upward))
            def _():
                hop_copy(unit, hop, upward).start()

    def last_stage(unit):
        name, k = units[unit]
        rows = pl.ds(k * 128 if name == Block.fo else 0, 128)
        cols = pl.ds(k * 256 if name == Block.fi else 0, 256)
        out_refs[name][rows, cols] = own[unit % RING, :, lanes(member * 256, 256)]
        for upward in (True, False):
            for hop in range(hops) if unit in direct else (hops - 1,):
                place = hop if upward else hops + hop

                @pl.when(hop_gets(unit, hop, upward))
                def _():
                    hop_copy(unit, hop, upward).wait_recv()
                    out_refs[name][rows, cols] += hop_in[unit % ROUND, place].astype(F32)

    vector_sum[...] = small[Small.vectors][...]

    def add_vector(index, cols, values):
        vector_sum[index : index + 1, cols] += jnp.sum(values, 0, keepdims=True)

    chunks = [(which, step % members) for which in range(items_here) for step in range(1, members + 1)]

    def key_load(order):
        which, step = chunks[order]
        rows, slot = pl.ds(which * slots + step * mem_local, mem_local), order % 2
        return (
            pltpu.make_async_copy(big[Given.keys].at[rows], key_buf.at[slot], kv_sem.at[0, slot]),
            pltpu.make_async_copy(big[Given.values].at[rows], value_buf.at[slot], kv_sem.at[1, slot]),
        )

    for copy in key_load(0):
        copy.start()

    def feed_back(k):
        def job():
            loaded((Given.feed_down, k), (Given.slope, k))
            grad_active = right_product(grad_down[...], weight_buf[0])
            if k < 3:
                down_load(k + 1)
            else:
                whole(Given.output_cross, weight_buf.at[0])
            grad = (grad_active * (exact, scale)[k % 2][...]).astype(BF16)
            if k < 2:
                slope_load(k + 2)
            wide[pl.ds(D + k * 256, 256), :] = grad
            sums = jnp.sum(grad.astype(F32), 0, keepdims=True)
            for part in range(8):
                target, place = 2 * k + part // 4, part % 4
                vector_sum[13 + place : 14 + place, target * 128 : target * 128 + 128] = sums[
                    :, part * 128 : part * 128 + 128
                ]
            loaded((Given.feed_up, k))
            if k == 0:
                loaded(Given.grad_three)
            tokens_grad[...] += right_product(grad, weight_buf[1])
            if k < 3:
                up_load(k + 1)
            else:
                whole(Given.key_cross, weight_buf.at[1])

        return job

    def middle_norm_back():
        loaded(Given.normed_two)
        grad_in, gain_grad, shift_grad = norm_backward(
            tokens_grad[...], normed_one[...], small[Small.inverse_two][...], small[Small.gains][1:2]
        )
        whole(Given.normed_one, normed_one)
        whole(Given.exact_two, exact)
        whole(Given.scale_two, scale)
        vector_sum[11:12, :] = gain_grad.reshape(1, D)
        vector_sum[8:9, :] = shift_grad.reshape(1, D)
        tokens_grad[...] = grad_in
        grad_cross[...] = grad_in.astype(BF16)
        add_vector(5, pl.ds(0, D), grad_in)
        loaded(Given.output_cross)
        grad_mixed[...] = right_product(grad_cross[...], weight_buf[0])
        whole(Given.value_cross, weight_buf.at[0])
        loaded(Given.q_two, Given.exact_two, Given.scale_two)

    def cross_prepare():
        def pair(p, _):
            cols = lanes(p * PAIR, PAIR)
            for which in range(items_here):
                rows = pl.ds(which * DEC, DEC)
                grad_numer = grad_mixed[rows, cols] * scale[rows, cols]
                grad_numer_low[rows, cols] = grad_numer.astype(BF16)
                grad_total[which, pl.ds(p, 1), :] = total_grads(grad_numer * exact[rows, cols])
            return 0

        lax.fori_loop(0, PAIRS, pair, 0)

    def cross_chunk(order):
        which, step = chunks[order]

        def job():
            for copy in key_load(order):
                copy.wait()
            if order + 1 < len(chunks):
                for copy in key_load(order + 1):
                    copy.start()
            rows, slot = pl.ds(which * DEC, DEC), order % 2
            limit = small[Small.limits][1:2, which : which + 1] - lax.rem(member - step + members, members) * mem_local
            allowed = lax.broadcasted_iota(jnp.int32, (mem_local, 2 * DEC), 0) < limit
            lane_low = low_lanes(DEC)
            at_rows = pl.ds(which * slots + step * mem_local, mem_local)

            def pair(p, _):
                cols = lanes(p * PAIR, PAIR)
                q2 = stack_pair(q_two[rows, cols], lane_low)
                gn2 = stack_pair(grad_numer_low[rows, cols], lane_low)
                gk, gv, gq2 = attend_back_chunk(
                    q2, gn2, grad_total[which, pl.ds(p, 1), :], key_buf[slot, :, cols], value_buf[slot, :, cols], allowed
                )
                gk_two[at_rows, cols] = gk.astype(BF16)
                gv_two[at_rows, cols] = gv.astype(BF16)
                add_vector(4, cols, gv)
                grad = jnp.where(lane_low, gq2[:DEC], gq2[DEC:]) * 0.125
                if step == 1:
                    grad_mixed[rows, cols] = grad
                else:
                    grad_mixed[rows, cols] += grad
                return 0

            lax.fori_loop(0, PAIRS, pair, 0)
            if step == 0:
                gq_two[rows, :] = grad_mixed[rows, :].astype(BF16)
                add_vector(3, pl.ds(0, D), grad_mixed[rows, :])

        return job

    def stage_copy(order):
        which, step = chunks[order]
        own_place = back_ref.at[member * items_here + which]
        target = own_place if step == 0 else part_ref.at[which, step]
        return pltpu.make_async_copy(stage.at[order % 2], target, stage_sem.at[order % 2])

    def memory_part(order):
        which, step = chunks[order]

        def job():
            if order == 0:
                loaded(Given.key_cross, Given.value_cross)
            rows = pl.ds(which * slots + step * mem_local, mem_local)
            total = right_product(gk_two[rows, :], weight_buf[1]) + right_product(gv_two[rows, :], weight_buf[0])
            stage[order % 2] = total.astype(BF16)
            stage_copy(order).start()
            if order == len(chunks) - 1:
                whole(Given.query_cross, weight_buf.at[1])
                whole(Given.output_self, weight_buf.at[0])
                whole(Given.exact_one, exact)
                whole(Given.scale_one, scale)
                whole(Given.q_one, q_one)
                whole(Given.k_one, k_one)
                whole(Given.v_one, v_one)

        return job

    def norm_back():
        loaded(Given.query_cross, Given.normed_one)
        grad = tokens_grad[...] + right_product(gq_two[...], weight_buf[1])
        whole(Given.query_self, weight_buf.at[1])
        grad_in, gain_grad, shift_grad = norm_backward(
            grad, normed_one[...], small[Small.inverse_one][...], small[Small.gains][0:1]
        )
        vector_sum[10:11, :] = gain_grad.reshape(1, D)
        vector_sum[7:8, :] = shift_grad.reshape(1, D)
        tokens_grad[...] = grad_in
        grad_self[...] = grad_in.astype(BF16)
        add_vector(2, pl.ds(0, D), grad_in)
        loaded(Given.output_self)
        grad_mixed[...] = right_product(grad_self[...], weight_buf[0])
        whole(Given.key_self, weight_buf.at[0])
        loaded(Given.exact_one, Given.scale_one, Given.q_one, Given.k_one, Given.v_one)

    def self_back(which, low, high):
        def job():
            rows = pl.ds(which * DEC, DEC)
            limit = small[Small.limits][0:1, which : which + 1]
            slot = lax.broadcasted_iota(jnp.int32, (DEC, 2 * DEC), 0)
            query = lax.broadcasted_iota(jnp.int32, (DEC, 2 * DEC), 1) % DEC
            allowed = (slot <= query) & (slot < limit)

            def pair(p, _):
                cols = lanes(p * PAIR, PAIR)

                lane_low = low_lanes(DEC)
                grad_numer = grad_mixed[rows, cols] * scale[rows, cols]
                gk, gv, gq2 = attend_back_chunk(
                    stack_pair(q_one[rows, cols], lane_low),
                    stack_pair(grad_numer.astype(BF16), lane_low),
                    total_grads(grad_numer * exact[rows, cols]),
                    k_one[rows, cols],
                    v_one[rows, cols],
                    allowed,
                )
                gk_one[rows, cols] = gk.astype(BF16)
                gv_one[rows, cols] = gv.astype(BF16)
                add_vector(1, cols, gv)
                grad = jnp.where(lane_low, gq2[:DEC], gq2[DEC:]) * 0.125
                gq_one[rows, cols] = grad.astype(BF16)
                add_vector(0, cols, grad)
                return 0

            lax.fori_loop(low, high, pair, 0)

        return job

    def token_term(name, slot, grads, following=None):
        def job():
            loaded(name)
            tokens_grad[...] += right_product(grads[...], weight_buf[slot])
            if following:
                whole(following, weight_buf.at[slot])

        return job

    def plane_vector(distance):
        return pltpu.make_async_remote_copy(
            src_ref=vector_sum.at[:, lanes((row ^ distance) * 128, 128)],
            dst_ref=vector_in.at[distance],
            send_sem=vec_send.at[0, distance],
            recv_sem=vec_recv.at[0, distance],
            device_id=(row ^ distance, member),
            device_id_type=MESH,
        )

    def line_vector(step):
        return pltpu.make_async_remote_copy(
            src_ref=vector_in.at[0],
            dst_ref=vector_far.at[step],
            send_sem=vec_send.at[1, step],
            recv_sem=vec_recv.at[1, step],
            device_id=(row, lax.rem(member + step, members)),
            device_id_type=MESH,
        )

    def vectors_start():
        for distance in range(1, 8):
            plane_vector(distance).start()

    def vectors_pass():
        total = vector_sum[:, lanes(row * 128, 128)]
        for distance in range(1, 8):
            plane_vector(distance).wait()
            total = total + vector_in[distance]
        vector_in[0] = total
        for step in range(1, members):
            line_vector(step).start()

    def vectors_end():
        total = vector_in[0]
        for step in range(1, members):
            line_vector(step).wait()
            total = total + vector_far[step]
        vector_out[...] = total

    back_rows = mem_local // BACK_PIECES

    def back_copy(which, step, piece):
        target = lax.rem(member - step + members, members)
        rows = pl.ds(piece * back_rows, back_rows)
        place = (which * members + step) * BACK_PIECES + piece
        return pltpu.make_async_remote_copy(
            src_ref=part_ref.at[which, step, rows],
            dst_ref=back_ref.at[member * items_here + which, rows],
            send_sem=back_send.at[place],
            recv_sem=back_recv.at[place],
            device_id=(row, target),
            device_id_type=MESH,
        )

    schedule = {}

    def at(tick, *jobs):
        schedule.setdefault(tick, []).extend(jobs)

    steps = {}
    for tick, orders in enumerate(((0,), (1,), (2, 3), (4,), (5,), (6,), (7,)), 2):
        for order in orders:
            steps[order] = tick
    at(0, feed_back(0), feed_back(1))
    at(1, feed_back(2), feed_back(3), middle_norm_back)
    at(2, cross_prepare)
    for order in range(len(chunks)):
        at(steps[order], cross_chunk(order))
        if order:
            at(steps[order], stage_copy(order - 1).wait)
        at(steps[order], memory_part(order))
    at(steps[len(chunks) - 1], stage_copy(len(chunks) - 1).wait)
    at(9, norm_back)
    at(10, self_back(0, 0, 8))
    at(11, self_back(1, 0, 4))
    at(12, self_back(1, 4, 8), vectors_start)
    at(14, token_term(Given.query_self, 1, gq_one, Given.value_self), vectors_pass)
    at(15, token_term(Given.key_self, 0, gk_one))
    at(16, token_term(Given.value_self, 1, gv_one), vectors_end)
    moves, tick, weight = [], 0, 0
    for order, (which, step) in enumerate(chunks):
        if step == 0:
            continue
        for piece in range(BACK_PIECES):
            ready = steps[min(order + 1, len(chunks) - 1)]
            if ready > tick:
                tick, weight = ready, 0
            elif weight >= BACK_WEIGHT:
                tick, weight = tick + 1, 0
            weight += 2 if step == members // 2 else 1
            moves.append((which, step, piece))
            at(tick, back_copy(which, step, piece).start)
    far_tick, hop_tick = 1 + S_LAG, 1 + 2 * S_LAG
    last_tick = hop_tick + hops
    end = count + last_tick

    for tick in range(end):
        if 0 <= tick - far_tick < count:
            far_stage(tick - far_tick)
        for hop in range(hops):
            if 0 <= tick - hop_tick - hop < count and tick - hop_tick - hop not in direct:
                hop_stage(tick - hop_tick - hop, hop)
        if tick - hop_tick in direct:
            for hop in range(hops):
                hop_stage(tick - hop_tick, hop)
        if 0 <= tick - last_tick < count and tick - last_tick not in direct:
            last_stage(tick - last_tick)
        if tick - hop_tick - 1 in direct:
            last_stage(tick - hop_tick - 1)
        if 0 <= tick - 1 < count:
            near_stage(tick - 1)
        if tick == 8:
            whole(Given.memory, wide)
        if 0 <= tick < count:
            core_stage(tick)
        for job in schedule.get(tick, ()):
            job()
    for unit in range(count - 2, count):
        core_copy(unit).wait_send()
    for unit in range(count - RING, count):
        near_copy(unit).wait_send()
        far_copy(unit).wait_send()
        for hop in range(hops):
            for upward in (True, False):
                @pl.when(hop_sends(hop, upward))
                def _():
                    hop_copy(unit, hop, upward).wait_send()
    for move in moves:
        back_copy(*move).wait()


def scatter_by_kernel(big, small, blocks, members, items_here, mem_local):
    count, hops = 16, members - 1
    rows = big[Given.tokens].shape[0]
    low = pltpu.VMEM((rows, D), BF16)
    high = pltpu.VMEM((rows, D), F32)
    slots = items_here * members * mem_local
    out_shape = [jax.ShapeDtypeStruct(block, F32) for block in blocks]
    out_shape += [
        jax.ShapeDtypeStruct((rows, D), F32),
        jax.ShapeDtypeStruct((small[Small.vectors].shape[0], 128), F32),
        jax.ShapeDtypeStruct((items_here, members, mem_local, D), BF16),
        jax.ShapeDtypeStruct((items_here * members, mem_local, D), BF16),
    ]
    outs = pl.pallas_call(
        functools.partial(scatter_kernel, members, items_here, mem_local),
        out_shape=out_shape,
        in_specs=[ANY] * Given.count + [VMEM] * Small.count,
        out_specs=[VMEM] * (len(blocks) + 2) + [ANY, ANY],
        scratch_shapes=[
            pltpu.VMEM((2 * D, D), BF16),
            low, low, low, low, low, low, low, low,
            high,
            high, high, high,
            low,
            pltpu.VMEM((items_here, PAIRS, 2 * DEC), F32),
            pltpu.VMEM((2, mem_local, D), BF16),
            pltpu.VMEM((2, mem_local, D), BF16),
            pltpu.VMEM((slots, D), BF16),
            pltpu.VMEM((slots, D), BF16),
            low,
            pltpu.VMEM((2, D, D), BF16),
            low,
            pltpu.VMEM((2, mem_local, D), BF16),
            pltpu.VMEM(small[Small.vectors].shape, F32),
            pltpu.VMEM((8, small[Small.vectors].shape[0], 128), F32),
            pltpu.VMEM((members, small[Small.vectors].shape[0], 128), F32),
            pltpu.VMEM((2, 4, 128, D), BF16),
            pltpu.VMEM((CORES, 4, 128, D), BF16),
            pltpu.VMEM((RING, 2, 128, D), BF16),
            pltpu.VMEM((ROUND, 2, 128, D), BF16),
            pltpu.VMEM((KEPT, 2, 128, D), BF16),
            pltpu.VMEM((RING, 128, D), BF16),
            pltpu.VMEM((ROUND, 128, D), BF16),
            pltpu.VMEM((RING, 128, D), F32),
            pltpu.VMEM((RING, 2 * hops, 128, 256), BF16),
            pltpu.VMEM((ROUND, 2 * hops, 128, 256), BF16),
            pltpu.SemaphoreType.DMA((count, 3 + 2 * hops)),
            pltpu.SemaphoreType.DMA((count, 3 + 2 * hops)),
            pltpu.SemaphoreType.DMA((items_here * members * BACK_PIECES,)),
            pltpu.SemaphoreType.DMA((items_here * members * BACK_PIECES,)),
            pltpu.SemaphoreType.REGULAR,
            pltpu.SemaphoreType.DMA((48,)),
            pltpu.SemaphoreType.DMA((2, 2)),
            pltpu.SemaphoreType.DMA((2,)),
            pltpu.SemaphoreType.DMA((2, 8)),
            pltpu.SemaphoreType.DMA((2, 8)),
        ],
        compiler_params=pltpu.CompilerParams(
            collective_id=1, has_side_effects=True, vmem_limit_bytes=62 * 1024 * 1024
        ),
        name="scatter_all",
    )(*big, *small)
    return outs[: len(blocks)], outs[len(blocks)], outs[len(blocks) + 1], outs[len(blocks) + 3]


def scatter_by_collectives(pairs, blocks, memory_part, row, member, items_count, members):
    grads = []
    for place, (left, right) in enumerate(pairs):
        ordered = order_columns(left, row, items_count, place % 2 == 1)
        grads += weight_gradients(ordered, [right], items_count, member, members, place % 2 == 1)
    items_here = memory_part.shape[0]
    back = jnp.zeros((items_here * members,) + memory_part.shape[2:], BF16)
    for step in range(1, members):
        part = lax.ppermute(memory_part[:, step], "mem", [(a, (a - step) % members) for a in range(members)])
        owner = lax.rem(member + step, members)
        back = lax.dynamic_update_slice_in_dim(back, part, owner * items_here, 0)
    return grads, back


def body(
    items_count,
    members,
    tokens,
    memory,
    cotangent,
    mem_len,
    dec_len,
    self_query,
    self_key,
    self_value,
    self_out,
    cross_query,
    cross_key,
    cross_value,
    cross_out,
    feed_in,
    feed_out,
    shifts,
    gains,
    inner_bias,
):
    row = lax.axis_index("items")
    member = lax.axis_index("mem")
    rows_here = tokens.shape[0]
    item_count = rows_here // DEC
    group_items = memory.shape[0]
    mem_local = memory.shape[1]
    shards = (
        cross_key, cross_value, self_query, self_key, self_value, self_out, cross_query, cross_out, feed_in, feed_out,
    )
    by_kernel = (items_count, members) == (8, 4)
    shift_width, bias_rows = shifts.shape[1], inner_bias.shape[0] // shifts.shape[1]
    vector = jnp.concatenate([shifts, gains, inner_bias.reshape(bias_rows, shift_width)], 0)
    own_dec = lax.dynamic_slice_in_dim(dec_len, member * item_count, item_count)
    own_mem = lax.dynamic_slice_in_dim(mem_len, member * item_count, item_count)
    if by_kernel:
        whole, item_memory, vectors, forward = gather_by_kernel(
            shards, memory, vector, tokens, jnp.stack([own_dec, own_mem]), items_count, members
        )
    else:
        whole, item_memory, vectors = gather_by_collectives(shards, memory, vector, items_count, members)
    (
        key_cross, value_cross, query_self, key_self, value_self, output_self, query_cross, output_cross,
        feed_up, feed_down,
    ) = whole
    memory_flat = item_memory.reshape(-1, D)
    vectors = vectors.astype(F32)
    bias_start = shifts.shape[0] + gains.shape[0]
    shift_rows = vectors[: shifts.shape[0]]
    gain_rows = vectors[shifts.shape[0] : bias_start]
    inner_shift = (
        vectors[bias_start:].reshape(bias_rows, items_count, shift_width).transpose(1, 0, 2).reshape(-1)
    )

    bases = lax.rem(member - jnp.arange(members, dtype=jnp.int32) + members, members) * mem_local

    if by_kernel:
        (
            queries_one, keys_one, values_one, mixed_one, exact_one, scale_one, hidden_one, hidden_one_low, normed_one,
            inverse_one, queries_two, mixed_two, exact_two, scale_two, keys_two, values_two,
        ) = forward
        keys_two, values_two = keys_two.reshape(-1, D), values_two.reshape(-1, D)
    else:
        tokens_float = tokens.astype(F32)
        queries_one = ((product(tokens, query_self) + shift_rows[0]) * 0.125).astype(BF16)
        keys_one = product(tokens, key_self).astype(BF16)
        values_one = (product(tokens, value_self) + shift_rows[1]).astype(BF16)
        mixed_one, exact_one, scale_one = attend_forward(
            True, DEC, own_dec, bases, queries_one, keys_one, values_one
        )
        resid_one = tokens_float + product(mixed_one, output_self) + shift_rows[2]
        hidden_one, normed_one, inverse_one = norm_forward(resid_one, gain_rows[0], shift_rows[7])
        hidden_one_low = hidden_one.astype(BF16)
        queries_two = ((product(hidden_one_low, query_cross) + shift_rows[3]) * 0.125).astype(BF16)
        keys_two = product(memory_flat, key_cross).astype(BF16)
        values_two = (product(memory_flat, value_cross) + shift_rows[4]).astype(BF16)
        mixed_two, exact_two, scale_two = attend_forward(
            False, mem_local, own_mem, bases, queries_two, keys_two, values_two
        )
    resid_two = hidden_one + product(mixed_two, output_cross) + shift_rows[5]
    hidden_two, normed_two, inverse_two = norm_forward(resid_two, gain_rows[1], shift_rows[8])
    hidden_two_low = hidden_two.astype(BF16)
    inner_pre = product(hidden_two_low, feed_up) + inner_shift
    cdf_part = 0.5 * (1.0 + jax.scipy.special.erf(inner_pre * half_root))
    active_low = (inner_pre * cdf_part).astype(BF16)
    resid_three = hidden_two + product(active_low, feed_down) + shift_rows[6]
    layer_out, normed_three, inverse_three = norm_forward(resid_three, gain_rows[2], shift_rows[9])

    grad_three, gain_grad_three, shift_grad_three = norm_backward(
        cotangent.astype(F32), normed_three, inverse_three, gain_rows[2]
    )
    grad_down = grad_three.astype(BF16)

    out_bias_grad = column_sums(grad_down)
    slope = cdf_part + inner_pre * jnp.exp(-0.5 * inner_pre * inner_pre) * normal_peak
    blocks = tuple(
        weight.shape
        for weight in (
            feed_out, feed_in, cross_out, cross_key, cross_value, cross_query, self_out, self_query, self_key, self_value,
        )
    )
    if by_kernel:
        vector_rows = (
            jnp.zeros((24, D), F32).at[6].set(out_bias_grad).at[9].set(shift_grad_three).at[12].set(gain_grad_three)
        )
        big = (
            active_low, grad_down, hidden_two_low, slope, feed_down, feed_up, grad_three, normed_two, mixed_two,
            queries_two, exact_two, scale_two, tokens, mixed_one, hidden_one_low, normed_one, queries_one, keys_one,
            values_one, keys_two, values_two, memory_flat, exact_one, scale_one, output_cross, key_cross, value_cross,
            query_cross, output_self, query_self, key_self, value_self,
        )
        small = (inverse_one, inverse_two, gain_rows, jnp.stack([own_dec, own_mem]), vector_rows)
        grads, tokens_grad, sums, memory_back = scatter_by_kernel(
            big, small, blocks, members, item_count, mem_local
        )
        memory_grad = memory_back.astype(F32)
        (
            feed_down_grad, feed_up_grad, output_cross_grad, key_cross_grad, value_cross_grad, query_cross_grad,
            output_self_grad, query_self_grad, key_self_grad, value_self_grad,
        ) = grads
        shifts_grad = sums[: shifts.shape[0]]
        gains_grad = sums[shifts.shape[0] : bias_start]
        bias_grad = sums[bias_start : bias_start + bias_rows].reshape(-1)
    else:
        grad_active = right_product(grad_down, feed_down)
        grad_inner = (grad_active * slope).astype(BF16)
        inner_bias_grad = column_sums(grad_inner)
        grad_hidden_two = grad_three + right_product(grad_inner, feed_up)
        grad_two, gain_grad_two, shift_grad_two = norm_backward(
            grad_hidden_two, normed_two, inverse_two, gain_rows[1]
        )
        grad_cross_branch = grad_two.astype(BF16)
        cross_out_bias_grad = column_sums(grad_cross_branch)
        grad_mixed_two = right_product(grad_cross_branch, output_cross)
        query_grad_two, key_grad_two, value_grad_two = attend_backward(
            False, mem_local, own_mem, bases, queries_two, keys_two, values_two, grad_mixed_two, exact_two, scale_two
        )
        query_grad_two = query_grad_two * jnp.asarray(0.125, BF16)

        memory_part = (
            right_product(key_grad_two, key_cross) + right_product(value_grad_two, value_cross)
        ).astype(BF16).reshape(item_count, members, mem_local, D)
        cross_value_bias_grad = column_sums(value_grad_two)
        cross_query_bias_grad = column_sums(query_grad_two)
        grad_hidden_one = grad_two + right_product(query_grad_two, query_cross)
        grad_one, gain_grad_one, shift_grad_one = norm_backward(
            grad_hidden_one, normed_one, inverse_one, gain_rows[0]
        )
        grad_self_branch = grad_one.astype(BF16)
        self_out_bias_grad = column_sums(grad_self_branch)
        grad_mixed_one = right_product(grad_self_branch, output_self)
        query_grad_one, key_grad_one, value_grad_one = attend_backward(
            True, DEC, own_dec, bases, queries_one, keys_one, values_one, grad_mixed_one, exact_one, scale_one
        )
        query_grad_one = query_grad_one * jnp.asarray(0.125, BF16)
        pairs = (
            (active_low, grad_down),
            (hidden_two_low, grad_inner),
            (mixed_two, grad_cross_branch),
            (memory_flat, key_grad_two),
            (memory_flat, value_grad_two),
            (hidden_one_low, query_grad_two),
            (mixed_one, grad_self_branch),
            (tokens, query_grad_one),
            (tokens, key_grad_one),
            (tokens, value_grad_one),
        )
        grads, memory_back = scatter_by_collectives(pairs, blocks, memory_part, row, member, items_count, members)
        (
            feed_down_grad, feed_up_grad, output_cross_grad, key_cross_grad, value_cross_grad, query_cross_grad,
            output_self_grad, query_self_grad, key_self_grad, value_self_grad,
        ) = grads
        memory_grad = lax.dynamic_update_slice_in_dim(
            memory_back.astype(F32), memory_part[:, 0].astype(F32), member * item_count, 0
        )
        tokens_grad = (
            grad_one
            + right_product(query_grad_one, query_self)
            + right_product(key_grad_one, key_self)
            + right_product(value_grad_one, value_self)
        )
        vectors = jnp.concatenate(
            [
                column_sums(query_grad_one),
                column_sums(value_grad_one),
                self_out_bias_grad,
                cross_query_bias_grad,
                cross_value_bias_grad,
                cross_out_bias_grad,
                out_bias_grad,
                shift_grad_one,
                shift_grad_two,
                shift_grad_three,
                gain_grad_one,
                gain_grad_two,
                gain_grad_three,
                inner_bias_grad,
            ]
        )
        vectors = lax.psum(vectors.reshape(-1, 128), ("items", "mem")).reshape(-1)
        shift_count = shifts.shape[0] * D
        gain_count = gains.shape[0] * D
        shift_width, gain_width, bias_width = shifts.shape[1], gains.shape[1], inner_bias.shape[0]
        shifts_grad = lax.dynamic_slice_in_dim(
            vectors[:shift_count].reshape(-1, D), row * shift_width, shift_width, 1
        )
        gains_grad = lax.dynamic_slice_in_dim(
            vectors[shift_count : shift_count + gain_count].reshape(-1, D), row * gain_width, gain_width, 1
        )
        bias_grad = lax.dynamic_slice_in_dim(vectors[shift_count + gain_count :], row * bias_width, bias_width)
    return (
        layer_out,
        tokens_grad,
        memory_grad,
        query_self_grad,
        key_self_grad,
        value_self_grad,
        output_self_grad,
        query_cross_grad,
        key_cross_grad,
        value_cross_grad,
        output_cross_grad,
        feed_up_grad,
        feed_down_grad,
        shifts_grad,
        gains_grad,
        bias_grad,
    )


def solution(mesh):
    tiles = P("items", "mem")
    rows = P(("items", "mem"), None)
    blocks = P("items", "mem", None)
    return jax.shard_map(
        functools.partial(body, mesh.shape["items"], mesh.shape["mem"]),
        mesh=mesh,
        in_specs=(rows, blocks, rows, P("items"), P("items"))
        + (tiles,) * 10
        + (P(None, "items"), P(None, "items"), P("items")),
        out_specs=(rows, rows, blocks) + (tiles,) * 10 + (P(None, "items"), P(None, "items"), P("items")),
        check_vma=False,
    )
```

```python
import functools

import jax
import jax.numpy as jnp
from jax import lax
from jax.experimental import pallas as pl
from jax.experimental.pallas import tpu as pltpu
from jax.sharding import PartitionSpec as P

D = 1024
HEADS = 16
HEAD_DIM = 64
PAIR = 2 * HEAD_DIM
PAIRS = HEADS // 2
DEC = 128
half_root = 0.7071067811865476
normal_peak = 0.3989422804014327
MESH = pl.DeviceIdType.MESH
F32 = jnp.float32
BF16 = jnp.bfloat16
X_LAG, FIRST_PIECE, SPREAD, STRAIGHT = 1, 2, 16, 3
ANY = pl.BlockSpec(memory_space=pl.ANY)
VMEM = pl.BlockSpec(memory_space=pltpu.VMEM)


def product(first_op, second_op):
    return jnp.dot(first_op, second_op, preferred_element_type=F32)


def left_product(first_op, second_op):
    return lax.dot_general(
        first_op, second_op, (((0,), (0,)), ((), ())), preferred_element_type=F32
    )


def right_product(first_op, second_op):
    return lax.dot_general(
        first_op, second_op, (((1,), (1,)), ((), ())), preferred_element_type=F32
    )


def column_sums(values):
    return jnp.sum(values.astype(F32), 0)


def norm_forward(values, gain, shift):
    center = values - jnp.mean(values, -1, keepdims=True)
    inverse = lax.rsqrt(jnp.mean(center * center, -1, keepdims=True) + 1e-05)
    normed = center * inverse
    return (normed * gain + shift, normed, inverse)


def norm_backward(grad_out, normed, inverse, gain):
    scaled = grad_out * gain
    grad_in = inverse * (
        scaled
        - jnp.mean(scaled, -1, keepdims=True)
        - normed * jnp.mean(scaled * normed, -1, keepdims=True)
    )
    return (grad_in, jnp.sum(grad_out * normed, 0), jnp.sum(grad_out, 0))


def gather_kernel(members, items_here, units, forward, *refs):
    count = len(units)
    weights = 1 + max(unit[0] for unit in units)
    shard_refs = refs[:weights]
    memory_ref, vector_ref, tokens_ref, limits_ref = refs[weights : weights + 4]
    refs = refs[weights + 4 :]
    whole_refs, items_ref, vectors_ref = refs[:weights], refs[weights], refs[weights + 1]
    refs = refs[weights + 2 :]
    outs, refs = refs[: forward.outs], refs[forward.outs :]
    send_sem, recv_sem, copy_sem, mem_send, mem_recv, mem_copy, vec_send, vec_recv, bounce = refs[:9]
    row = lax.axis_index("items")
    member = lax.axis_index("mem")
    hops = members - 1
    core_peer, first_peer, second_peer = row ^ 1, row ^ 2, row ^ 4
    UP, DOWN = 0, hops
    ALONG_X, ALONG_Y, HALF_A, HALF_B, CORE = 2 * hops, 2 * hops + 1, 2 * hops + 2, 2 * hops + 3, 2 * hops + 4

    barrier = pltpu.get_barrier_semaphore()
    partners = [(row ^ distance, member) for distance in range(1, 8)]
    partners += [(row, lax.rem(member + step, members)) for step in range(1, members)]
    for partner in partners:
        pl.semaphore_signal(barrier, inc=1, device_id=partner, device_id_type=MESH)
    pl.semaphore_wait(barrier, len(partners))

    def place(unit, owner):
        weight, start, depth, height = units[unit]
        return pl.ds(pl.multiple_of(owner * height + start, depth), depth)

    def cols(unit, who):
        width = shard_refs[units[unit][0]].shape[1]
        return pl.ds(pl.multiple_of(who * width, width), width)

    def shard(unit):
        weight, start, depth, height = units[unit]
        return shard_refs[weight].at[pl.ds(start, depth)]

    def remote(unit, kind, src, dst, device):
        return pltpu.make_async_remote_copy(
            src_ref=src,
            dst_ref=dst,
            send_sem=send_sem.at[unit, kind],
            recv_sem=recv_sem.at[unit, kind],
            device_id=device,
            device_id_type=MESH,
        )

    def along(unit, hop, upward):
        whole = whole_refs[units[unit][0]]
        origin = member - hop if upward else member + hop
        origin = jnp.clip(origin, 0, members - 1)
        piece = whole.at[place(unit, row), cols(unit, origin)]
        target = jnp.clip(member + 1 if upward else member - 1, 0, members - 1)
        return remote(
            unit, (UP if upward else DOWN) + hop, shard(unit) if hop == 0 else piece, piece, (row, target)
        )

    straight = range(STRAIGHT)

    def straight_copy(unit, hop, upward):
        target = jnp.clip(member + hop + 1 if upward else member - hop - 1, 0, members - 1)
        piece = whole_refs[units[unit][0]].at[place(unit, row), cols(unit, member)]
        return remote(unit, (UP if upward else DOWN) + hop, shard(unit), piece, (row, target))

    def straight_each(unit, act):
        for hop in range(hops):
            @pl.when(member + hop + 1 <= members - 1)
            def _():
                act(straight_copy(unit, hop, True))

            @pl.when(member - hop - 1 >= 0)
            def _():
                act(straight_copy(unit, hop, False))

    def along_start(unit, hop):
        @pl.when((member >= hop) & (member < members - 1))
        def _():
            along(unit, hop, True).start()

        @pl.when((member <= members - 1 - hop) & (member > 0))
        def _():
            along(unit, hop, False).start()

    def along_arrive(unit, hop):
        @pl.when(member >= hop + 1)
        def _():
            along(unit, hop, True).wait_recv()

        @pl.when(member <= members - 2 - hop)
        def _():
            along(unit, hop, False).wait_recv()

    def along_sent(unit, hop):
        @pl.when((member >= hop) & (member < members - 1))
        def _():
            along(unit, hop, True).wait_send()

        @pl.when((member <= members - 1 - hop) & (member > 0))
        def _():
            along(unit, hop, False).wait_send()

    def own_copy(unit):
        return pltpu.make_async_copy(
            shard(unit), whole_refs[units[unit][0]].at[place(unit, row), cols(unit, member)], copy_sem.at[unit]
        )

    def block(unit, kind, owner, device, half=None):
        weight, start, depth, height = units[unit]
        if half is None:
            rows = place(unit, owner)
        else:
            part = depth // 2
            rows = pl.ds(pl.multiple_of(owner * height + start + half * part, part), part)
        ref = whole_refs[weight].at[rows]
        return remote(unit, kind, ref, ref, (device, member))

    def to_x(unit):
        return block(unit, ALONG_X, row, first_peer)

    def to_y(unit):
        return block(unit, ALONG_Y, row, second_peer)

    def half_a(unit):
        return block(unit, HALF_A, first_peer, second_peer, 0)

    def half_b(unit):
        return block(unit, HALF_B, second_peer, first_peer, 1)

    def to_core(unit, which):
        owner = (row, first_peer, second_peer, row ^ 6)[which]
        return block(unit, CORE + which, owner, core_peer)

    pieces = memory_ref.shape[1] // 32 * items_here

    def memory_send(piece, step):
        which, start = piece // (pieces // items_here), piece % (pieces // items_here) * 32
        target = lax.rem(member + step, members)
        return pltpu.make_async_remote_copy(
            src_ref=memory_ref.at[target * items_here + which, pl.ds(start, 32)],
            dst_ref=items_ref.at[which, step, pl.ds(start, 32)],
            send_sem=mem_send.at[piece, step],
            recv_sem=mem_recv.at[piece, step],
            device_id=(row, target),
            device_id_type=MESH,
        )

    fetch = pltpu.make_async_copy(memory_ref.at[pl.ds(member * items_here, items_here)], bounce, mem_copy.at[0])
    local = pltpu.make_async_copy(bounce, items_ref.at[:, 0], mem_copy.at[1])
    fetch.start()
    spot = vectors_ref.at[:, pl.ds(pl.multiple_of(row * 128, 128), 128)]
    vector_copies = [
        pltpu.make_async_remote_copy(
            src_ref=vector_ref,
            dst_ref=spot,
            send_sem=vec_send.at[distance],
            recv_sem=vec_recv.at[distance],
            device_id=(row ^ distance, member),
            device_id_type=MESH,
        )
        for distance in range(1, 8)
    ]
    vector_copies.append(pltpu.make_async_copy(vector_ref, spot, vec_send.at[0]))
    for copy in vector_copies:
        copy.start()

    due = [FIRST_PIECE + piece * SPREAD // pieces for piece in range(pieces)]
    plane_lag = 1
    done_lag = plane_lag + 2 * X_LAG + 1
    jobs = forward.jobs(
        members, items_here, member, tokens_ref, limits_ref, whole_refs, items_ref, vectors_ref, outs, refs[9:],
        done_lag, due,
    )
    last = max([count - 1 + done_lag, due[-1] + 2] + list(jobs))
    for tick in range(last + 1):
        unit = tick - plane_lag
        if 0 <= unit < count:
            for hop in range(hops) if unit in straight else (hops - 1,):
                along_arrive(unit, hop)
            own_copy(unit).wait()
            to_x(unit).start()
            to_y(unit).start()
            to_core(unit, 0).start()
        if tick in straight:
            straight_each(tick, lambda copy: copy.start())
            own_copy(tick).start()
        for hop in range(hops):
            unit = tick + hops - plane_lag - hop
            if unit not in straight and 0 <= unit < count:
                if hop == 0:
                    own_copy(unit).start()
                else:
                    along_arrive(unit, hop - 1)
                along_start(unit, hop)
        for piece in range(pieces):
            if due[piece] == tick:
                for step in range(1, members):
                    memory_send(piece, step).start()
        unit = tick - plane_lag - X_LAG
        if 0 <= unit < count:
            to_x(unit).wait_recv()
            half_a(unit).start()
            to_core(unit, 1).start()
            to_y(unit).wait_recv()
            half_b(unit).start()
            to_core(unit, 2).start()
        unit = tick - plane_lag - 2 * X_LAG
        if 0 <= unit < count:
            half_a(unit).wait_recv()
            half_b(unit).wait_recv()
            to_core(unit, 3).start()
        if tick == 1:
            fetch.wait()
            local.start()
        if tick == 3:
            local.wait()
            for copy in vector_copies:
                copy.wait()
        unit = tick - done_lag
        if 0 <= unit < count:
            for which in range(4):
                to_core(unit, which).wait_recv()
        for piece in range(pieces):
            if due[piece] + 2 == tick:
                for step in range(1, members):
                    memory_send(piece, step).wait_recv()
        for job in jobs.get(tick, ()):
            job()
    for unit in range(count):
        if unit in straight:
            straight_each(unit, lambda copy: copy.wait_send())
        else:
            for hop in range(hops):
                along_sent(unit, hop)
        to_x(unit).wait_send()
        to_y(unit).wait_send()
        half_a(unit).wait_send()
        half_b(unit).wait_send()
        for which in range(4):
            to_core(unit, which).wait_send()
    for piece in range(pieces):
        for step in range(1, members):
            memory_send(piece, step).wait_send()
    forward.finish()


def attend_parts(queries, keys_at, values_at, allowed_at, chunks):
    lane_low = low_lanes(DEC)
    q2 = stack_pair(queries, lane_low)
    numer, total = None, None
    for step in range(chunks):
        scores = right_product(q2, keys_at(step))
        exp_scores = jnp.where(allowed_at(step), jnp.exp(scores), 0.0)
        part = jnp.sum(exp_scores, -1, keepdims=True)
        term = product(exp_scores.astype(BF16), values_at(step))
        total = part if total is None else total + part
        numer = term if numer is None else numer + term
    return jnp.where(lane_low, numer[:DEC], numer[DEC:]), jnp.where(lane_low, total[:DEC], total[DEC:])


def attend_pair(queries, keys_at, values_at, allowed_at, chunks):
    numer, total = attend_parts(queries, keys_at, values_at, allowed_at, chunks)
    scale = 1.0 / total
    return numer * scale, scale


class Forward:
    outs = 16

    def __init__(self, rows, items_here, members, mem_local):
        self.rows, self.items_here, self.members, self.mem_local = rows, items_here, members, mem_local
        self.slots = members * mem_local

    def out_shapes(self):
        wide, low = jax.ShapeDtypeStruct((self.rows, D), F32), jax.ShapeDtypeStruct((self.rows, D), BF16)
        keys = jax.ShapeDtypeStruct((self.items_here, self.members, self.mem_local, D), BF16)
        inverse = jax.ShapeDtypeStruct((self.rows, 1), F32)
        return [low, low, low, low, wide, wide, wide, low, wide, low, inverse, low, wide, wide, keys, keys]

    def out_specs(self):
        return [ANY] * 10 + [VMEM] * 4 + [ANY] * 2

    def scratch(self):
        return [pltpu.VMEM(shape.shape, shape.dtype) for shape in self.out_shapes()[:10]] + [
            pltpu.VMEM((2, D, D), BF16),
            pltpu.VMEM((2, D, D), BF16),
            pltpu.VMEM((2, self.members, self.mem_local // 4, D), BF16),
            pltpu.VMEM((self.items_here, self.members, self.mem_local, D), BF16),
            pltpu.VMEM((self.items_here, self.members, self.mem_local, D), BF16),
            pltpu.SemaphoreType.DMA((20,)),
        ]

    def jobs(
        self, members, items_here, member, tokens_ref, limits_ref, whole_refs, items_ref, vectors_ref, outs, scratch,
        done_lag, due,
    ):
        early, (inverse_one, mixed_two, exact_two, scale_two, keys_out, values_out) = outs[:10], outs[10:]
        q_one, k_one, v_one, mixed_one, exact_one, scale_one, hidden_one, hidden_low, normed_one, q_two = scratch[:10]
        weight_buf, cross_buf, rows_buf, keys, values, sems = scratch[10:]
        early_copies = [
            pltpu.make_async_copy(source, target, sems.at[10 + place])
            for place, (source, target) in enumerate(zip(scratch[:10], early))
        ]
        part = self.mem_local // 4
        schedule = {}

        def at(tick, *jobs):
            schedule.setdefault(tick, []).extend(jobs)

        def vector(index):
            return vectors_ref[...].astype(F32)[index : index + 1]

        def fetch_weight(unit, slot):
            return pltpu.make_async_copy(whole_refs[unit], weight_buf.at[slot], sems.at[slot])

        def fetch_cross(unit):
            return pltpu.make_async_copy(whole_refs[unit], cross_buf.at[unit], sems.at[2 + unit])

        def fetch_rows(which, chunk):
            slot = chunk % 2
            return pltpu.make_async_copy(
                items_ref.at[which, :, pl.ds(chunk * part, part)], rows_buf.at[slot], sems.at[4 + slot]
            )

        def store(which, value):
            source, target = ((keys, keys_out), (values, values_out))[value]
            return pltpu.make_async_copy(source.at[which], target.at[which], sems.at[6 + 2 * which + value])

        self.pending = []

        def project(slot, unit, result, shift, scale):
            def job():
                fetch_weight(unit, slot).wait()
                total = product(tokens_ref[...], weight_buf[slot])
                if shift is not None:
                    total = total + vector(shift)
                if scale is not None:
                    total = total * scale
                result[...] = total.astype(BF16)

            return job

        def self_attend(which):
            def job():
                limit = limits_ref[0:1, which : which + 1]
                slot = lax.broadcasted_iota(jnp.int32, (2 * DEC, DEC), 1)
                query = lax.broadcasted_iota(jnp.int32, (2 * DEC, DEC), 0) % DEC
                allowed = (slot <= query) & (slot < limit)
                rows = pl.ds(which * DEC, DEC)

                def pair(p, _):
                    cols = pl.ds(pl.multiple_of(p * PAIR, PAIR), PAIR)
                    exact, scale = attend_pair(
                        q_one[rows, cols], lambda _: k_one[rows, cols], lambda _: v_one[rows, cols], lambda _: allowed, 1
                    )
                    mixed_one[rows, cols] = exact.astype(BF16)
                    exact_one[rows, cols] = exact
                    scale_one[rows, cols] = scale
                    return 0

                lax.fori_loop(0, PAIRS, pair, 0)

            return job

        def first_norm(slot, unit):
            def job():
                fetch_weight(unit, slot).wait()
                resid = tokens_ref[...].astype(F32) + product(mixed_one[...], weight_buf[slot]) + vector(2)
                hidden, normed, inverse = norm_forward(resid, vector(10), vector(7))
                hidden_one[...] = hidden
                hidden_low[...] = hidden.astype(BF16)
                normed_one[...] = normed
                inverse_one[...] = inverse

            return job

        def cross_query(slot, unit):
            def job():
                fetch_weight(unit, slot).wait()
                total = (product(hidden_low[...], weight_buf[slot]) + vector(3)) * 0.125
                q_two[...] = total.astype(BF16)

            return job

        def project_rows(which, chunk):
            def job():
                fetch_rows(which, chunk).wait()
                rows = rows_buf[chunk % 2].reshape(members * part, D)
                new_keys = product(rows, cross_buf[0]).astype(BF16).reshape(members, part, D)
                new_values = (product(rows, cross_buf[1]) + vector(4)).astype(BF16).reshape(members, part, D)
                keys[which, :, pl.ds(chunk * part, part)] = new_keys
                values[which, :, pl.ds(chunk * part, part)] = new_values
                if chunk == 3:
                    store(which, 0).start()
                    store(which, 1).start()

            return job

        def cross_attend(which, low, high, first, size, begin, end):
            def job():
                rows = pl.ds(which * DEC, DEC)
                limit = limits_ref[1:2, which : which + 1] - first
                slot = lax.broadcasted_iota(jnp.int32, (2 * DEC, size), 1)

                def allowed(step):
                    return slot < limit - lax.rem(member - step + members, members) * self.mem_local

                def pair(p, _):
                    cols = pl.ds(pl.multiple_of(p * PAIR, PAIR), PAIR)
                    numer, total = attend_parts(
                        q_two[rows, cols],
                        lambda step: keys[which, step, pl.ds(first, size), cols],
                        lambda step: values[which, step, pl.ds(first, size), cols],
                        allowed,
                        members,
                    )
                    if not begin:
                        numer, total = numer + exact_two[rows, cols], total + scale_two[rows, cols]
                    if end:
                        scale = 1.0 / total
                        exact = numer * scale
                        mixed_two[rows, cols] = exact.astype(BF16)
                        exact_two[rows, cols] = exact
                        scale_two[rows, cols] = scale
                    else:
                        exact_two[rows, cols] = numer
                        scale_two[rows, cols] = total
                    return 0

                lax.fori_loop(low, high, pair, 0)

            return job

        for unit in range(2):
            at(unit + done_lag, fetch_cross(unit).start)
        for unit in range(2, 7):
            at(unit + done_lag, fetch_weight(unit, unit % 2).start)
        at(1 + done_lag + 1, fetch_cross(0).wait)
        at(1 + done_lag + 1, fetch_cross(1).wait)
        start = 2 + done_lag + 1
        at(start, project(0, 2, q_one, 0, 0.125))
        at(start + 1, project(1, 3, k_one, None, None))
        at(start + 2, project(0, 4, v_one, 1, None))
        at(start + 2, self_attend(0))
        at(start + 3, self_attend(1))
        at(start + 3, first_norm(1, 5))
        at(start + 4, cross_query(0, 6))
        at(start + 5, *[copy.start for copy in early_copies])
        previous = 1 + done_lag
        per_item = len(due) // items_here
        for which in range(items_here):
            for chunk in range(4):
                ready = due[which * per_item + (chunk + 1) * per_item // 4 - 1] + 2
                begin = max(ready, previous)
                at(begin, fetch_rows(which, chunk).start)
                late = begin if which == items_here - 1 and chunk == 3 else begin + 1
                at(late, project_rows(which, chunk))
                previous = begin + 1
            begin = max(previous, start + 5)
            if which < items_here - 1:
                for quarter in range(4):
                    at(begin + quarter, cross_attend(which, 2 * quarter, 2 * quarter + 2, 0, self.mem_local, True, True))
            else:
                at(late - 1, cross_attend(which, 0, PAIRS, 0, 3 * part, True, False))
                at(late, cross_attend(which, 0, PAIRS, 3 * part, part, False, True))
        self.pending = early_copies + [store(which, value) for which in range(items_here) for value in range(2)]
        return schedule

    def finish(self):
        for copy in self.pending:
            copy.wait()


def gather_by_kernel(shards, memory, vector, tokens, limits, items_count, members):
    items_here = memory.shape[0] // members
    units = []
    for weight, shard in enumerate(shards):
        height, width = shard.shape
        depth = height * 256 // max(height * width // 128, 256)
        for start in range(0, height, depth):
            units.append((weight, start, depth, height))
    forward = Forward(tokens.shape[0], items_here, members, memory.shape[1])
    pieces = memory.shape[1] // 32 * items_here
    hops = members - 1
    kinds = 2 * hops + 8
    out_shape = [jax.ShapeDtypeStruct((s.shape[0] * items_count, s.shape[1] * members), s.dtype) for s in shards]
    out_shape.append(
        jax.ShapeDtypeStruct((items_here, members, memory.shape[1], memory.shape[2]), memory.dtype)
    )
    out_shape.append(jax.ShapeDtypeStruct((vector.shape[0], vector.shape[1] * items_count), vector.dtype))
    gathered = len(out_shape)
    out_shape += forward.out_shapes()
    outs = pl.pallas_call(
        functools.partial(gather_kernel, members, items_here, tuple(units), forward),
        out_shape=out_shape,
        in_specs=[VMEM] * len(shards) + [ANY, VMEM, VMEM, VMEM],
        out_specs=[ANY] * (gathered - 1) + [VMEM] + forward.out_specs(),
        scratch_shapes=[
            pltpu.SemaphoreType.DMA((len(units), kinds)),
            pltpu.SemaphoreType.DMA((len(units), kinds)),
            pltpu.SemaphoreType.DMA((len(units),)),
            pltpu.SemaphoreType.DMA((pieces, members)),
            pltpu.SemaphoreType.DMA((pieces, members)),
            pltpu.SemaphoreType.DMA((2,)),
            pltpu.SemaphoreType.DMA((items_count,)),
            pltpu.SemaphoreType.DMA((items_count,)),
            pltpu.VMEM((items_here,) + memory.shape[1:], memory.dtype),
        ]
        + forward.scratch(),
        compiler_params=pltpu.CompilerParams(
            collective_id=0, has_side_effects=True, vmem_limit_bytes=60 * 1024 * 1024
        ),
        name="gather_all",
    )(*shards, memory, vector, tokens, limits)
    return outs[: gathered - 2], outs[gathered - 2], outs[gathered - 1], outs[gathered:]


def gather_by_collectives(shards, memory, vector, items_count, members):
    whole = []
    for shard in shards:
        cols = lax.all_gather(shard, "mem", axis=1, tiled=True)
        whole.append(lax.all_gather(cols, "items", axis=0, tiled=True))
    items_here = memory.shape[0] // members
    member = lax.axis_index("mem")
    parts = []
    for step in range(members):
        target = lax.rem(member + step, members)
        part = lax.dynamic_slice_in_dim(memory, target * items_here, items_here)
        if step:
            part = lax.ppermute(part, "mem", [(a, (a + step) % members) for a in range(members)])
        parts.append(part)
    return whole, jnp.stack(parts, 1), lax.all_gather(vector, "items", axis=1, tiled=True)


def stack_pair(values, lane_low):
    zero = jnp.zeros_like(values)
    return jnp.concatenate([jnp.where(lane_low, values, zero), jnp.where(lane_low, zero, values)], 0)


def low_lanes(rows):
    return lax.broadcasted_iota(jnp.int32, (rows, PAIR), 1) < HEAD_DIM


def allowed_slots(causal, chunk, lens_ref, bases_ref, which, step, key_dim):
    shape = (2 * DEC, chunk) if key_dim == 1 else (chunk, 2 * DEC)
    slot = lax.broadcasted_iota(jnp.int32, shape, key_dim)
    if causal:
        query = lax.broadcasted_iota(jnp.int32, shape, 1 - key_dim) % DEC
        return (slot <= query) & (slot < lens_ref[which])
    return slot < lens_ref[which] - bases_ref[step]


def attend_forward_kernel(causal, chunk, lens_ref, bases_ref, q_ref, k_ref, v_ref, mixed_ref, exact_ref, scale_ref):
    which = pl.program_id(0)
    lane_low = low_lanes(DEC)
    q2 = stack_pair(q_ref[...], lane_low)
    numer = jnp.zeros((2 * DEC, PAIR), F32)
    total = jnp.zeros((2 * DEC, 1), F32)
    for step in range(k_ref.shape[0] // chunk):
        rows = pl.ds(step * chunk, chunk)
        scores = right_product(q2, k_ref[rows, :])
        allowed = allowed_slots(causal, chunk, lens_ref, bases_ref, which, step, 1)
        exp_scores = jnp.where(allowed, jnp.exp(scores), 0.0)
        total += jnp.sum(exp_scores, -1, keepdims=True)
        numer += product(exp_scores.astype(BF16), v_ref[rows, :])
    numer = jnp.where(lane_low, numer[:DEC], numer[DEC:])
    scale = 1.0 / jnp.where(lane_low, total[:DEC], total[DEC:])
    exact = numer * scale
    mixed_ref[...] = exact.astype(BF16)
    exact_ref[...] = exact
    scale_ref[...] = scale


def attend_backward_kernel(
    causal, chunk, lens_ref, bases_ref, q_ref, k_ref, v_ref, grad_ref, exact_ref, scale_ref, gq_ref, gk_ref, gv_ref
):
    which = pl.program_id(0)
    lane_low = low_lanes(DEC)
    q2 = stack_pair(q_ref[...], lane_low)
    grad_numer = grad_ref[...] * scale_ref[...]
    gn2 = stack_pair(grad_numer.astype(BF16), lane_low)
    weighted = jnp.transpose(grad_numer * exact_ref[...])
    grad_total = -jnp.concatenate(
        [
            jnp.sum(weighted[:HEAD_DIM], 0, keepdims=True),
            jnp.sum(weighted[HEAD_DIM:], 0, keepdims=True),
        ],
        1,
    )
    gq2 = jnp.zeros((2 * DEC, PAIR), F32)
    for step in range(k_ref.shape[0] // chunk):
        rows = pl.ds(step * chunk, chunk)
        keys = k_ref[rows, :]
        scores = right_product(keys, q2)
        allowed = allowed_slots(causal, chunk, lens_ref, bases_ref, which, step, 0)
        exp_scores = jnp.where(allowed, jnp.exp(scores), 0.0)
        grad_exp = right_product(v_ref[rows, :], gn2) + grad_total
        grad_scores = (exp_scores * grad_exp).astype(BF16)
        gk_ref[rows, :] = product(grad_scores, q2).astype(BF16)
        gv_ref[rows, :] = product(exp_scores.astype(BF16), gn2).astype(BF16)
        gq2 += left_product(grad_scores, keys)
    gq_ref[...] = jnp.where(lane_low, gq2[:DEC], gq2[DEC:]).astype(BF16)


def attention_call(kernel, causal, chunk, lens, bases, queries, keys, values, more, outs):
    item_count = lens.shape[0]
    slots = keys.shape[0] // item_count
    q_spec = pl.BlockSpec((DEC, PAIR), lambda a, p, *_: (a, p))
    k_spec = pl.BlockSpec((slots, PAIR), lambda a, p, *_: (a, p))
    spec = {"q": q_spec, "k": k_spec}
    rows = {"q": queries.shape[0], "k": keys.shape[0]}
    return pl.pallas_call(
        functools.partial(kernel, causal, chunk),
        grid_spec=pltpu.PrefetchScalarGridSpec(
            num_scalar_prefetch=2,
            grid=(item_count, PAIRS),
            in_specs=[q_spec, k_spec, k_spec] + [q_spec] * len(more),
            out_specs=[spec[kind] for kind, _ in outs],
        ),
        out_shape=[jax.ShapeDtypeStruct((rows[kind], D), dtype) for kind, dtype in outs],
        cost_estimate=pl.CostEstimate(
            flops=4 * item_count * HEADS * DEC * slots * 256, bytes_accessed=16 * D * slots, transcendentals=0
        ),
        name="self_attention" if causal else "cross_attention",
    )(lens, bases, queries, keys, values, *more)


def attend_forward(causal, chunk, lens, bases, queries, keys, values):
    return attention_call(
        attend_forward_kernel, causal, chunk, lens, bases, queries, keys, values, (),
        (("q", BF16), ("q", F32), ("q", F32)),
    )


def attend_backward(causal, chunk, lens, bases, queries, keys, values, grad_mixed, exact, scale):
    return attention_call(
        attend_backward_kernel, causal, chunk, lens, bases, queries, keys, values, (grad_mixed, exact, scale),
        (("q", BF16), ("k", BF16), ("k", BF16)),
    )


def halving_order(items_count, flipped):
    bits = [1 << b for b in range(1, items_count.bit_length() - 1)]
    return [1] + (bits if flipped else bits[::-1])


def block_order(items_count, flipped):
    bits = halving_order(items_count, flipped)
    order = []
    for spot in range(items_count):
        distance = 0
        for place, bit in enumerate(bits):
            if spot >> (len(bits) - 1 - place) & 1:
                distance |= bit
        order.append(distance)
    return order


def order_columns(values, row, items_count, flipped):
    width = values.shape[1] // items_count
    return jnp.concatenate(
        [
            lax.dynamic_slice_in_dim(values, (row ^ distance) * width, width, 1)
            for distance in block_order(items_count, flipped)
        ],
        1,
    )


def reduce_rows(partial, items_count, flipped):
    for bit in halving_order(items_count, flipped):
        half = partial.shape[0] // 2
        arrived = lax.ppermute(partial[half:], "items", [(a, a ^ bit) for a in range(items_count)])
        partial = (partial[:half].astype(F32) + arrived.astype(F32)).astype(BF16)
    return partial


def reduce_columns(partial, member, members):
    bit = members // 2
    while bit:
        half = partial.shape[1] // 2
        high = (member & bit) != 0
        left, right = partial[:, :half], partial[:, half:]
        arrived = lax.ppermute(
            jnp.where(high, left, right), "mem", [(a, a ^ bit) for a in range(members)]
        )
        partial = jnp.where(high, right, left).astype(F32) + arrived.astype(F32)
        if bit > 1:
            partial = partial.astype(BF16)
        bit //= 2
    return partial


def weight_gradients(left_ordered, grads, items_count, member, members, flipped):
    width = grads[0].shape[1]
    joined = grads[0] if len(grads) == 1 else jnp.concatenate(grads, 1)
    partial = left_product(left_ordered, joined).astype(BF16)
    partial = reduce_rows(partial, items_count, flipped)
    return [
        reduce_columns(partial[:, k * width : (k + 1) * width], member, members) for k in range(len(grads))
    ]

RING, KEPT, ROUND, CORES = 4, 6, 10, 3
BACK_PIECES, BACK_EARLY, BACK_LATE, DIRECT = 8, 6, 3, 0
S_LAG = 2


def total_grads(weighted):
    weighted = jnp.transpose(weighted)
    return -jnp.concatenate(
        [jnp.sum(weighted[:HEAD_DIM], 0, keepdims=True), jnp.sum(weighted[HEAD_DIM:], 0, keepdims=True)], 1
    )


def attend_back_chunk(q2, gn2, grad_total, keys, values, allowed):
    exp_scores = jnp.where(allowed, jnp.exp(right_product(keys, q2)), 0.0)
    grad_exp = right_product(values, gn2) + grad_total
    grad_scores = (exp_scores * grad_exp).astype(BF16)
    return product(grad_scores, q2), product(exp_scores.astype(BF16), gn2), left_product(grad_scores, keys)


class Given:
    (
        active, grad_down, hidden_two, slope, feed_down, feed_up, grad_three, normed_two, mixed_two, q_two, exact_two,
        scale_two, tokens, mixed_one, hidden_one, normed_one, q_one, k_one, v_one, keys, values, memory, exact_one,
        scale_one, output_cross, key_cross, value_cross, query_cross, output_self, query_self, key_self, value_self,
    ) = range(32)
    count = 32


class Small:
    inverse_one, inverse_two, gains, limits, vectors = range(5)
    count = 5


class Block:
    fo, fi, co, ck, cv, cq, so, sq, sk, sv = range(10)
    count = 10


def scatter_kernel(members, items_here, mem_local, *refs):
    big, refs = refs[: Given.count], refs[Given.count :]
    small, refs = refs[: Small.count], refs[Small.count :]
    out_refs, refs = refs[: Block.count], refs[Block.count :]
    tokens_grad, vector_out, part_ref, back_ref = refs[:4]
    (
        wide, grad_down, hidden_two, mixed_two, grad_cross, q_two, tokens, mixed_one, hidden_one, normed_one,
        grad_mixed, exact, scale, grad_numer_low, grad_total, key_buf, value_buf, gk_two, gv_two,
        gq_two, weight_buf,
        grad_self, stage, vector_sum, vector_in, vector_far,
        core_out, core_in, near_out, near_in, near_kept, far_out, far_in, own, hop_out, hop_in,
        send_sem, recv_sem, back_send, back_recv, credit, load_sem, kv_sem, stage_sem, vec_send, vec_recv,
    ) = refs[4:]
    gq_one, q_one, k_one, v_one = key_buf.at[0], key_buf.at[1], value_buf.at[0], value_buf.at[1]
    gk_one, gv_one = stage.at[0], stage.at[1]
    row = lax.axis_index("items")
    member = lax.axis_index("mem")
    hops = members - 1
    core_peer = row ^ 1
    slots = members * mem_local

    loads = {}

    def load(name, source, target):
        loads[name] = pltpu.make_async_copy(source, target, load_sem.at[len(loads)])
        loads[name].start()

    def loaded(*names):
        for name in names:
            loads[name].wait()

    def whole(name, target):
        load(name, big[name], target)

    def down_load(k):
        load((Given.feed_down, k), big[Given.feed_down].at[pl.ds(k * D, D)], weight_buf.at[0])

    def up_load(k):
        load((Given.feed_up, k), big[Given.feed_up].at[:, pl.ds(k * D, D)], weight_buf.at[1])

    def slope_load(k):
        load((Given.slope, k), big[Given.slope].at[:, pl.ds(k * D, D)], (exact, scale)[k % 2])

    whole(Given.grad_down, grad_down)
    for k in range(4):
        load((Given.active, k), big[Given.active].at[:, pl.ds(k * D, D)], wide.at[pl.ds(k * 256, 256)])
    down_load(0)
    slope_load(0)
    up_load(0)
    slope_load(1)
    whole(Given.grad_three, tokens_grad)
    whole(Given.normed_two, normed_one)
    whole(Given.q_two, q_two)
    whole(Given.hidden_two, hidden_two)
    whole(Given.mixed_two, mixed_two)
    whole(Given.hidden_one, hidden_one)
    whole(Given.mixed_one, mixed_one)
    whole(Given.tokens, tokens)

    barrier = pltpu.get_barrier_semaphore()
    partners = [(row ^ distance, member) for distance in range(1, 8)]
    partners += [(row, lax.rem(member + step, members)) for step in range(1, members)]
    for partner in partners:
        pl.semaphore_signal(barrier, inc=1, device_id=partner, device_id_type=MESH)
    pl.semaphore_wait(barrier, len(partners))

    units = [(Block.fo, k) for k in range(4)] + [(Block.fi, k) for k in range(4)]
    units += [(name, 0) for name in range(Block.co, Block.count)]
    count = len(units)
    factors = {
        Block.co: (mixed_two, grad_cross),
        Block.ck: (wide, gk_two),
        Block.cv: (wide, gv_two),
        Block.cq: (hidden_one, gq_two),
        Block.so: (mixed_one, grad_self),
        Block.sq: (tokens, gq_one),
        Block.sk: (tokens, gk_one),
        Block.sv: (tokens, gv_one),
    }
    needs = {
        0: (Given.grad_down,) + tuple((Given.active, k) for k in range(4)),
        4: (Given.hidden_two,),
        8: (Given.mixed_two,),
        9: (Given.memory,),
        11: (Given.hidden_one,),
        12: (Given.mixed_one,),
        13: (Given.tokens,),
    }

    def bits(unit):
        return (2, 4) if unit % 2 == 0 else (4, 2)

    def owners(unit, who):
        near, far = bits(unit)
        return (who ^ near, who ^ near ^ far, who ^ far, who)

    def lanes(start, size):
        return pl.ds(pl.multiple_of(start, 128), size)

    def partial(unit, owner):
        name, k = units[unit]
        if name == Block.fo:
            left = wide[pl.ds(pl.multiple_of(owner // 2 * 256, 256), 256), lanes(owner % 2 * 512 + k * 128, 128)]
            return left_product(left, grad_down[...])
        if name == Block.fi:
            right = jnp.concatenate(
                [wide[pl.ds(D + part * 256, 256), pl.ds(k * 256, 256)] for part in range(members)], 1
            )
            return left_product(hidden_two[:, lanes(owner * 128, 128)], right)
        left_ref, right_ref = factors[name]
        depth = right_ref.shape[0]
        if depth <= 512:
            return left_product(left_ref[:, lanes(owner * 128, 128)], right_ref[...])

        def term(spot, sums):
            rows = pl.ds(pl.multiple_of(spot * 512, 512), 512)
            return sums + left_product(left_ref[rows, lanes(owner * 128, 128)], right_ref[rows, :])

        return lax.fori_loop(0, depth // 512, term, jnp.zeros((128, D), F32))

    def remote(unit, kind, src, dst, device):
        return pltpu.make_async_remote_copy(
            src_ref=src,
            dst_ref=dst,
            send_sem=send_sem.at[unit, kind],
            recv_sem=recv_sem.at[unit, kind],
            device_id=device,
            device_id_type=MESH,
        )

    def core_copy(unit):
        return remote(unit, 0, core_out.at[unit % 2], core_in.at[unit % CORES], (core_peer, member))

    def near_copy(unit):
        return remote(
            unit, 1, near_out.at[unit % RING], near_in.at[unit % ROUND], (row ^ bits(unit)[0], member)
        )

    def far_copy(unit):
        return remote(unit, 2, far_out.at[unit % RING], far_in.at[unit % ROUND], (row ^ bits(unit)[1], member))

    direct = range(count - DIRECT, count)

    def hop_copy(unit, hop, upward):
        reach = members - 1 - hop if unit in direct else 1
        target = jnp.clip(member + reach if upward else member - reach, 0, members - 1)
        place = hop if upward else hops + hop
        return remote(
            unit, 3 + place, hop_out.at[unit % RING, place], hop_in.at[unit % ROUND, place], (row, target)
        )

    def hop_sends(hop, upward):
        distance = members - 1 - hop
        return (member + distance <= members - 1) if upward else (member - distance >= 0)

    def hop_gets(unit, hop, upward):
        distance = members - 1 - hop
        if unit in direct:
            return (member >= distance) if upward else (member <= members - 1 - distance)
        return (
            ((member >= 1) & (member - 1 + distance <= members - 1))
            if upward
            else ((member <= members - 2) & (member + 1 - distance >= 0))
        )

    def core_stage(unit):
        loaded(*needs.get(unit, ()))
        if unit >= 2:
            core_copy(unit - 2).wait_send()
        targets = owners(unit, core_peer)

        def fill(spot, _):
            owner = targets[3]
            for k in range(3):
                owner = jnp.where(spot == k, targets[k], owner)
            core_out[unit % 2, spot] = partial(unit, owner).astype(BF16)
            return 0

        lax.fori_loop(0, 4, fill, 0)
        if unit >= CORES:
            pl.semaphore_wait(credit, 1)
        core_copy(unit).start()

    def near_stage(unit):
        core_copy(unit).wait_recv()
        if unit >= RING:
            near_copy(unit - RING).wait_send()
        mine = owners(unit, row)

        def give(spot, _):
            total = partial(unit, jnp.where(spot == 0, mine[0], mine[1])) + core_in[unit % CORES, spot].astype(F32)
            near_out[unit % RING, spot] = total.astype(BF16)
            return 0

        lax.fori_loop(0, 2, give, 0)
        near_copy(unit).start()

        def keep(spot, _):
            total = partial(unit, jnp.where(spot == 0, mine[2], mine[3])) + core_in[unit % CORES, 2 + spot].astype(F32)
            near_kept[unit % KEPT, spot] = total.astype(BF16)
            return 0

        lax.fori_loop(0, 2, keep, 0)
        if unit + CORES < count:
            pl.semaphore_signal(credit, inc=1, device_id=(core_peer, member), device_id_type=MESH)

    def far_stage(unit):
        near_copy(unit).wait_recv()
        if unit >= RING:
            far_copy(unit - RING).wait_send()
        far_out[unit % RING] = (
            near_kept[unit % KEPT, 0].astype(F32) + near_in[unit % ROUND, 1].astype(F32)
        ).astype(BF16)
        far_copy(unit).start()

    def hop_stage(unit, hop):
        if hop == 0:
            far_copy(unit).wait_recv()
            own[unit % RING] = (
                near_kept[unit % KEPT, 1].astype(F32)
                + near_in[unit % ROUND, 0].astype(F32)
                + far_in[unit % ROUND].astype(F32)
            )
        for upward in (True, False):
            distance = members - 1 - hop
            owner = jnp.clip(member + distance if upward else member - distance, 0, members - 1)
            place = hop if upward else hops + hop
            block = lanes(owner * 256, 256)
            if unit >= RING:
                @pl.when(hop_sends(hop, upward))
                def _():
                    hop_copy(unit - RING, hop, upward).wait_send()

            if hop > 0 and unit not in direct:
                arrived = hop_gets(unit, hop - 1, upward)

                @pl.when(arrived)
                def _():
                    hop_copy(unit, hop - 1, upward).wait_recv()
                    hop_out[unit % RING, place] = (
                        own[unit % RING, :, block] + hop_in[unit % ROUND, place - 1].astype(F32)
                    ).astype(BF16)

                @pl.when(hop_sends(hop, upward) & jnp.logical_not(arrived))
                def _():
                    hop_out[unit % RING, place] = own[unit % RING, :, block].astype(BF16)

            else:
                @pl.when(hop_sends(hop, upward))
                def _():
                    hop_out[unit % RING, place] = own[unit % RING, :, block].astype(BF16)

            @pl.when(hop_sends(hop, upward))
            def _():
                hop_copy(unit, hop, upward).start()

    def last_stage(unit):
        name, k = units[unit]
        rows = pl.ds(k * 128 if name == Block.fo else 0, 128)
        cols = pl.ds(k * 256 if name == Block.fi else 0, 256)
        out_refs[name][rows, cols] = own[unit % RING, :, lanes(member * 256, 256)]
        for upward in (True, False):
            for hop in range(hops) if unit in direct else (hops - 1,):
                place = hop if upward else hops + hop

                @pl.when(hop_gets(unit, hop, upward))
                def _():
                    hop_copy(unit, hop, upward).wait_recv()
                    out_refs[name][rows, cols] += hop_in[unit % ROUND, place].astype(F32)

    vector_sum[...] = small[Small.vectors][...]

    def add_vector(index, cols, values):
        vector_sum[index : index + 1, cols] += jnp.sum(values, 0, keepdims=True)

    chunks = [(which, step % members) for which in range(items_here) for step in range(1, members + 1)]

    def key_load(order):
        which, step = chunks[order]
        rows, slot = pl.ds(which * slots + step * mem_local, mem_local), order % 2
        return (
            pltpu.make_async_copy(big[Given.keys].at[rows], key_buf.at[slot], kv_sem.at[0, slot]),
            pltpu.make_async_copy(big[Given.values].at[rows], value_buf.at[slot], kv_sem.at[1, slot]),
        )

    for copy in key_load(0):
        copy.start()

    def feed_back(k):
        def job():
            loaded((Given.feed_down, k), (Given.slope, k))
            grad_active = right_product(grad_down[...], weight_buf[0])
            if k < 3:
                down_load(k + 1)
            else:
                whole(Given.output_cross, weight_buf.at[0])
            grad = (grad_active * (exact, scale)[k % 2][...]).astype(BF16)
            if k < 2:
                slope_load(k + 2)
            wide[pl.ds(D + k * 256, 256), :] = grad
            sums = jnp.sum(grad.astype(F32), 0, keepdims=True)
            for part in range(8):
                target, place = 2 * k + part // 4, part % 4
                vector_sum[13 + place : 14 + place, target * 128 : target * 128 + 128] = sums[
                    :, part * 128 : part * 128 + 128
                ]
            loaded((Given.feed_up, k))
            if k == 0:
                loaded(Given.grad_three)
            tokens_grad[...] += right_product(grad, weight_buf[1])
            if k < 3:
                up_load(k + 1)
            else:
                whole(Given.key_cross, weight_buf.at[1])

        return job

    def middle_norm_back():
        loaded(Given.normed_two)
        grad_in, gain_grad, shift_grad = norm_backward(
            tokens_grad[...], normed_one[...], small[Small.inverse_two][...], small[Small.gains][1:2]
        )
        whole(Given.normed_one, normed_one)
        whole(Given.exact_two, exact)
        whole(Given.scale_two, scale)
        vector_sum[11:12, :] = gain_grad.reshape(1, D)
        vector_sum[8:9, :] = shift_grad.reshape(1, D)
        tokens_grad[...] = grad_in
        grad_cross[...] = grad_in.astype(BF16)
        add_vector(5, pl.ds(0, D), grad_in)
        loaded(Given.output_cross)
        grad_mixed[...] = right_product(grad_cross[...], weight_buf[0])
        whole(Given.value_cross, weight_buf.at[0])
        loaded(Given.q_two, Given.exact_two, Given.scale_two)

    def cross_prepare():
        def pair(p, _):
            cols = lanes(p * PAIR, PAIR)
            for which in range(items_here):
                rows = pl.ds(which * DEC, DEC)
                grad_numer = grad_mixed[rows, cols] * scale[rows, cols]
                grad_numer_low[rows, cols] = grad_numer.astype(BF16)
                grad_total[which, pl.ds(p, 1), :] = total_grads(grad_numer * exact[rows, cols])
            return 0

        lax.fori_loop(0, PAIRS, pair, 0)

    def cross_chunk(order):
        which, step = chunks[order]

        def job():
            for copy in key_load(order):
                copy.wait()
            if order + 1 < len(chunks):
                for copy in key_load(order + 1):
                    copy.start()
            rows, slot = pl.ds(which * DEC, DEC), order % 2
            limit = small[Small.limits][1:2, which : which + 1] - lax.rem(member - step + members, members) * mem_local
            allowed = lax.broadcasted_iota(jnp.int32, (mem_local, 2 * DEC), 0) < limit
            lane_low = low_lanes(DEC)
            at_rows = pl.ds(which * slots + step * mem_local, mem_local)

            def pair(p, _):
                cols = lanes(p * PAIR, PAIR)
                q2 = stack_pair(q_two[rows, cols], lane_low)
                gn2 = stack_pair(grad_numer_low[rows, cols], lane_low)
                gk, gv, gq2 = attend_back_chunk(
                    q2, gn2, grad_total[which, pl.ds(p, 1), :], key_buf[slot, :, cols], value_buf[slot, :, cols], allowed
                )
                gk_two[at_rows, cols] = gk.astype(BF16)
                gv_two[at_rows, cols] = gv.astype(BF16)
                add_vector(4, cols, gv)
                grad = jnp.where(lane_low, gq2[:DEC], gq2[DEC:]) * 0.125
                if step == 1:
                    grad_mixed[rows, cols] = grad
                else:
                    grad_mixed[rows, cols] += grad
                return 0

            lax.fori_loop(0, PAIRS, pair, 0)
            if step == 0:
                gq_two[rows, :] = grad_mixed[rows, :].astype(BF16)
                add_vector(3, pl.ds(0, D), grad_mixed[rows, :])

        return job

    def stage_copy(order):
        which, step = chunks[order]
        own_place = back_ref.at[member * items_here + which]
        target = own_place if step == 0 else part_ref.at[which, step]
        return pltpu.make_async_copy(stage.at[order % 2], target, stage_sem.at[order % 2])

    def memory_part(order):
        which, step = chunks[order]

        def job():
            if order == 0:
                loaded(Given.key_cross, Given.value_cross)
            rows = pl.ds(which * slots + step * mem_local, mem_local)
            total = right_product(gk_two[rows, :], weight_buf[1]) + right_product(gv_two[rows, :], weight_buf[0])
            stage[order % 2] = total.astype(BF16)
            stage_copy(order).start()
            if order == len(chunks) - 1:
                whole(Given.query_cross, weight_buf.at[1])
                whole(Given.output_self, weight_buf.at[0])
                whole(Given.exact_one, exact)
                whole(Given.scale_one, scale)
                whole(Given.q_one, q_one)
                whole(Given.k_one, k_one)
                whole(Given.v_one, v_one)

        return job

    def norm_back():
        loaded(Given.query_cross, Given.normed_one)
        grad = tokens_grad[...] + right_product(gq_two[...], weight_buf[1])
        whole(Given.query_self, weight_buf.at[1])
        grad_in, gain_grad, shift_grad = norm_backward(
            grad, normed_one[...], small[Small.inverse_one][...], small[Small.gains][0:1]
        )
        vector_sum[10:11, :] = gain_grad.reshape(1, D)
        vector_sum[7:8, :] = shift_grad.reshape(1, D)
        tokens_grad[...] = grad_in
        grad_self[...] = grad_in.astype(BF16)
        add_vector(2, pl.ds(0, D), grad_in)
        loaded(Given.output_self)
        grad_mixed[...] = right_product(grad_self[...], weight_buf[0])
        whole(Given.key_self, weight_buf.at[0])
        loaded(Given.exact_one, Given.scale_one, Given.q_one, Given.k_one, Given.v_one)

    def self_back(which, low, high):
        def job():
            rows = pl.ds(which * DEC, DEC)
            limit = small[Small.limits][0:1, which : which + 1]
            slot = lax.broadcasted_iota(jnp.int32, (DEC, 2 * DEC), 0)
            query = lax.broadcasted_iota(jnp.int32, (DEC, 2 * DEC), 1) % DEC
            allowed = (slot <= query) & (slot < limit)

            def pair(p, _):
                cols = lanes(p * PAIR, PAIR)

                lane_low = low_lanes(DEC)
                grad_numer = grad_mixed[rows, cols] * scale[rows, cols]
                gk, gv, gq2 = attend_back_chunk(
                    stack_pair(q_one[rows, cols], lane_low),
                    stack_pair(grad_numer.astype(BF16), lane_low),
                    total_grads(grad_numer * exact[rows, cols]),
                    k_one[rows, cols],
                    v_one[rows, cols],
                    allowed,
                )
                gk_one[rows, cols] = gk.astype(BF16)
                gv_one[rows, cols] = gv.astype(BF16)
                add_vector(1, cols, gv)
                grad = jnp.where(lane_low, gq2[:DEC], gq2[DEC:]) * 0.125
                gq_one[rows, cols] = grad.astype(BF16)
                add_vector(0, cols, grad)
                return 0

            lax.fori_loop(low, high, pair, 0)

        return job

    def token_term(name, slot, grads, following=None):
        def job():
            loaded(name)
            tokens_grad[...] += right_product(grads[...], weight_buf[slot])
            if following:
                whole(following, weight_buf.at[slot])

        return job

    def plane_vector(distance):
        return pltpu.make_async_remote_copy(
            src_ref=vector_sum.at[:, lanes((row ^ distance) * 128, 128)],
            dst_ref=vector_in.at[distance],
            send_sem=vec_send.at[0, distance],
            recv_sem=vec_recv.at[0, distance],
            device_id=(row ^ distance, member),
            device_id_type=MESH,
        )

    def line_vector(step):
        return pltpu.make_async_remote_copy(
            src_ref=vector_in.at[0],
            dst_ref=vector_far.at[step],
            send_sem=vec_send.at[1, step],
            recv_sem=vec_recv.at[1, step],
            device_id=(row, lax.rem(member + step, members)),
            device_id_type=MESH,
        )

    def vectors_start():
        for distance in range(1, 8):
            plane_vector(distance).start()

    def vectors_pass():
        total = vector_sum[:, lanes(row * 128, 128)]
        for distance in range(1, 8):
            plane_vector(distance).wait()
            total = total + vector_in[distance]
        vector_in[0] = total
        for step in range(1, members):
            line_vector(step).start()

    def vectors_end():
        total = vector_in[0]
        for step in range(1, members):
            line_vector(step).wait()
            total = total + vector_far[step]
        vector_out[...] = total

    back_rows = mem_local // BACK_PIECES

    def back_copy(which, step, piece):
        target = lax.rem(member - step + members, members)
        rows = pl.ds(piece * back_rows, back_rows)
        place = (which * members + step) * BACK_PIECES + piece
        return pltpu.make_async_remote_copy(
            src_ref=part_ref.at[which, step, rows],
            dst_ref=back_ref.at[member * items_here + which, rows],
            send_sem=back_send.at[place],
            recv_sem=back_recv.at[place],
            device_id=(row, target),
            device_id_type=MESH,
        )

    schedule = {}

    def at(tick, *jobs):
        schedule.setdefault(tick, []).extend(jobs)

    steps = {}
    for tick, orders in enumerate(((0,), (1,), (2, 3), (4,), (5,), (6,), (7,)), 2):
        for order in orders:
            steps[order] = tick
    at(0, feed_back(0), feed_back(1))
    at(1, feed_back(2), feed_back(3), middle_norm_back)
    at(2, cross_prepare)
    for order in range(len(chunks)):
        at(steps[order], cross_chunk(order))
        if order:
            at(steps[order], stage_copy(order - 1).wait)
        at(steps[order], memory_part(order))
    at(steps[len(chunks) - 1], stage_copy(len(chunks) - 1).wait)
    at(9, norm_back)
    at(10, self_back(0, 0, 8))
    at(11, self_back(1, 0, 4))
    at(12, self_back(1, 4, 8), vectors_start)
    at(14, token_term(Given.query_self, 1, gq_one, Given.value_self), vectors_pass)
    at(15, token_term(Given.key_self, 0, gk_one))
    at(16, token_term(Given.value_self, 1, gv_one), vectors_end)
    far_tick, hop_tick = 1 + S_LAG, 1 + 2 * S_LAG
    moves, tick, weight = [], 0, 0
    for order, (which, step) in enumerate(chunks):
        if step == 0:
            continue
        for piece in range(BACK_PIECES):
            ready = steps[min(order + 1, len(chunks) - 1)]
            if ready > tick:
                tick, weight = ready, 0
            elif weight >= (BACK_EARLY if tick < hop_tick else BACK_LATE):
                tick, weight = tick + 1, 0
            weight += 2 if step == members // 2 else 1
            moves.append((which, step, piece))
            at(tick, back_copy(which, step, piece).start)
    last_tick = hop_tick + hops
    end = count + last_tick

    for tick in range(end):
        if 0 <= tick - far_tick < count:
            far_stage(tick - far_tick)
        if 0 <= tick - 1 < count:
            near_stage(tick - 1)
        if tick == 8:
            whole(Given.memory, wide)
        if 0 <= tick < count:
            core_stage(tick)
        for hop in range(hops):
            if 0 <= tick - hop_tick - hop < count and tick - hop_tick - hop not in direct:
                hop_stage(tick - hop_tick - hop, hop)
        if tick - hop_tick in direct:
            for hop in range(hops):
                hop_stage(tick - hop_tick, hop)
        if 0 <= tick - last_tick < count and tick - last_tick not in direct:
            last_stage(tick - last_tick)
        if tick - hop_tick - 1 in direct:
            last_stage(tick - hop_tick - 1)
        for job in schedule.get(tick, ()):
            job()
    for unit in range(count - 2, count):
        core_copy(unit).wait_send()
    for unit in range(count - RING, count):
        near_copy(unit).wait_send()
        far_copy(unit).wait_send()
        for hop in range(hops):
            for upward in (True, False):
                @pl.when(hop_sends(hop, upward))
                def _():
                    hop_copy(unit, hop, upward).wait_send()
    for move in moves:
        back_copy(*move).wait()


def scatter_by_kernel(big, small, blocks, members, items_here, mem_local):
    count, hops = 16, members - 1
    rows = big[Given.tokens].shape[0]
    low = pltpu.VMEM((rows, D), BF16)
    high = pltpu.VMEM((rows, D), F32)
    slots = items_here * members * mem_local
    out_shape = [jax.ShapeDtypeStruct(block, F32) for block in blocks]
    out_shape += [
        jax.ShapeDtypeStruct((rows, D), F32),
        jax.ShapeDtypeStruct((small[Small.vectors].shape[0], 128), F32),
        jax.ShapeDtypeStruct((items_here, members, mem_local, D), BF16),
        jax.ShapeDtypeStruct((items_here * members, mem_local, D), BF16),
    ]
    outs = pl.pallas_call(
        functools.partial(scatter_kernel, members, items_here, mem_local),
        out_shape=out_shape,
        in_specs=[ANY] * Given.count + [VMEM] * Small.count,
        out_specs=[VMEM] * (len(blocks) + 2) + [ANY, ANY],
        scratch_shapes=[
            pltpu.VMEM((2 * D, D), BF16),
            low, low, low, low, low, low, low, low,
            high,
            high, high, high,
            low,
            pltpu.VMEM((items_here, PAIRS, 2 * DEC), F32),
            pltpu.VMEM((2, mem_local, D), BF16),
            pltpu.VMEM((2, mem_local, D), BF16),
            pltpu.VMEM((slots, D), BF16),
            pltpu.VMEM((slots, D), BF16),
            low,
            pltpu.VMEM((2, D, D), BF16),
            low,
            pltpu.VMEM((2, mem_local, D), BF16),
            pltpu.VMEM(small[Small.vectors].shape, F32),
            pltpu.VMEM((8, small[Small.vectors].shape[0], 128), F32),
            pltpu.VMEM((members, small[Small.vectors].shape[0], 128), F32),
            pltpu.VMEM((2, 4, 128, D), BF16),
            pltpu.VMEM((CORES, 4, 128, D), BF16),
            pltpu.VMEM((RING, 2, 128, D), BF16),
            pltpu.VMEM((ROUND, 2, 128, D), BF16),
            pltpu.VMEM((KEPT, 2, 128, D), BF16),
            pltpu.VMEM((RING, 128, D), BF16),
            pltpu.VMEM((ROUND, 128, D), BF16),
            pltpu.VMEM((RING, 128, D), F32),
            pltpu.VMEM((RING, 2 * hops, 128, 256), BF16),
            pltpu.VMEM((ROUND, 2 * hops, 128, 256), BF16),
            pltpu.SemaphoreType.DMA((count, 3 + 2 * hops)),
            pltpu.SemaphoreType.DMA((count, 3 + 2 * hops)),
            pltpu.SemaphoreType.DMA((items_here * members * BACK_PIECES,)),
            pltpu.SemaphoreType.DMA((items_here * members * BACK_PIECES,)),
            pltpu.SemaphoreType.REGULAR,
            pltpu.SemaphoreType.DMA((48,)),
            pltpu.SemaphoreType.DMA((2, 2)),
            pltpu.SemaphoreType.DMA((2,)),
            pltpu.SemaphoreType.DMA((2, 8)),
            pltpu.SemaphoreType.DMA((2, 8)),
        ],
        compiler_params=pltpu.CompilerParams(
            collective_id=1, has_side_effects=True, vmem_limit_bytes=62 * 1024 * 1024
        ),
        name="scatter_all",
    )(*big, *small)
    return outs[: len(blocks)], outs[len(blocks)], outs[len(blocks) + 1], outs[len(blocks) + 3]


def scatter_by_collectives(pairs, blocks, memory_part, row, member, items_count, members):
    grads = []
    for place, (left, right) in enumerate(pairs):
        ordered = order_columns(left, row, items_count, place % 2 == 1)
        grads += weight_gradients(ordered, [right], items_count, member, members, place % 2 == 1)
    items_here = memory_part.shape[0]
    back = jnp.zeros((items_here * members,) + memory_part.shape[2:], BF16)
    for step in range(1, members):
        part = lax.ppermute(memory_part[:, step], "mem", [(a, (a - step) % members) for a in range(members)])
        owner = lax.rem(member + step, members)
        back = lax.dynamic_update_slice_in_dim(back, part, owner * items_here, 0)
    return grads, back


def body(
    items_count,
    members,
    tokens,
    memory,
    cotangent,
    mem_len,
    dec_len,
    self_query,
    self_key,
    self_value,
    self_out,
    cross_query,
    cross_key,
    cross_value,
    cross_out,
    feed_in,
    feed_out,
    shifts,
    gains,
    inner_bias,
):
    row = lax.axis_index("items")
    member = lax.axis_index("mem")
    rows_here = tokens.shape[0]
    item_count = rows_here // DEC
    group_items = memory.shape[0]
    mem_local = memory.shape[1]
    shards = (
        cross_key, cross_value, self_query, self_key, self_value, self_out, cross_query, cross_out, feed_in, feed_out,
    )
    by_kernel = (items_count, members) == (8, 4)
    shift_width, bias_rows = shifts.shape[1], inner_bias.shape[0] // shifts.shape[1]
    vector = jnp.concatenate([shifts, gains, inner_bias.reshape(bias_rows, shift_width)], 0)
    own_dec = lax.dynamic_slice_in_dim(dec_len, member * item_count, item_count)
    own_mem = lax.dynamic_slice_in_dim(mem_len, member * item_count, item_count)
    if by_kernel:
        whole, item_memory, vectors, forward = gather_by_kernel(
            shards, memory, vector, tokens, jnp.stack([own_dec, own_mem]), items_count, members
        )
    else:
        whole, item_memory, vectors = gather_by_collectives(shards, memory, vector, items_count, members)
    (
        key_cross, value_cross, query_self, key_self, value_self, output_self, query_cross, output_cross,
        feed_up, feed_down,
    ) = whole
    memory_flat = item_memory.reshape(-1, D)
    vectors = vectors.astype(F32)
    bias_start = shifts.shape[0] + gains.shape[0]
    shift_rows = vectors[: shifts.shape[0]]
    gain_rows = vectors[shifts.shape[0] : bias_start]
    inner_shift = (
        vectors[bias_start:].reshape(bias_rows, items_count, shift_width).transpose(1, 0, 2).reshape(-1)
    )

    bases = lax.rem(member - jnp.arange(members, dtype=jnp.int32) + members, members) * mem_local

    if by_kernel:
        (
            queries_one, keys_one, values_one, mixed_one, exact_one, scale_one, hidden_one, hidden_one_low, normed_one,
            queries_two, inverse_one, mixed_two, exact_two, scale_two, keys_two, values_two,
        ) = forward
        keys_two, values_two = keys_two.reshape(-1, D), values_two.reshape(-1, D)
    else:
        tokens_float = tokens.astype(F32)
        queries_one = ((product(tokens, query_self) + shift_rows[0]) * 0.125).astype(BF16)
        keys_one = product(tokens, key_self).astype(BF16)
        values_one = (product(tokens, value_self) + shift_rows[1]).astype(BF16)
        mixed_one, exact_one, scale_one = attend_forward(
            True, DEC, own_dec, bases, queries_one, keys_one, values_one
        )
        resid_one = tokens_float + product(mixed_one, output_self) + shift_rows[2]
        hidden_one, normed_one, inverse_one = norm_forward(resid_one, gain_rows[0], shift_rows[7])
        hidden_one_low = hidden_one.astype(BF16)
        queries_two = ((product(hidden_one_low, query_cross) + shift_rows[3]) * 0.125).astype(BF16)
        keys_two = product(memory_flat, key_cross).astype(BF16)
        values_two = (product(memory_flat, value_cross) + shift_rows[4]).astype(BF16)
        mixed_two, exact_two, scale_two = attend_forward(
            False, mem_local, own_mem, bases, queries_two, keys_two, values_two
        )
    resid_two = hidden_one + product(mixed_two, output_cross) + shift_rows[5]
    hidden_two, normed_two, inverse_two = norm_forward(resid_two, gain_rows[1], shift_rows[8])
    hidden_two_low = hidden_two.astype(BF16)
    inner_pre = product(hidden_two_low, feed_up) + inner_shift
    cdf_part = 0.5 * (1.0 + jax.scipy.special.erf(inner_pre * half_root))
    active_low = (inner_pre * cdf_part).astype(BF16)
    resid_three = hidden_two + product(active_low, feed_down) + shift_rows[6]
    layer_out, normed_three, inverse_three = norm_forward(resid_three, gain_rows[2], shift_rows[9])

    grad_three, gain_grad_three, shift_grad_three = norm_backward(
        cotangent.astype(F32), normed_three, inverse_three, gain_rows[2]
    )
    grad_down = grad_three.astype(BF16)

    out_bias_grad = column_sums(grad_down)
    slope = cdf_part + inner_pre * jnp.exp(-0.5 * inner_pre * inner_pre) * normal_peak
    blocks = tuple(
        weight.shape
        for weight in (
            feed_out, feed_in, cross_out, cross_key, cross_value, cross_query, self_out, self_query, self_key, self_value,
        )
    )
    if by_kernel:
        vector_rows = (
            jnp.zeros((24, D), F32).at[6].set(out_bias_grad).at[9].set(shift_grad_three).at[12].set(gain_grad_three)
        )
        big = (
            active_low, grad_down, hidden_two_low, slope, feed_down, feed_up, grad_three, normed_two, mixed_two,
            queries_two, exact_two, scale_two, tokens, mixed_one, hidden_one_low, normed_one, queries_one, keys_one,
            values_one, keys_two, values_two, memory_flat, exact_one, scale_one, output_cross, key_cross, value_cross,
            query_cross, output_self, query_self, key_self, value_self,
        )
        small = (inverse_one, inverse_two, gain_rows, jnp.stack([own_dec, own_mem]), vector_rows)
        grads, tokens_grad, sums, memory_back = scatter_by_kernel(
            big, small, blocks, members, item_count, mem_local
        )
        memory_grad = memory_back.astype(F32)
        (
            feed_down_grad, feed_up_grad, output_cross_grad, key_cross_grad, value_cross_grad, query_cross_grad,
            output_self_grad, query_self_grad, key_self_grad, value_self_grad,
        ) = grads
        shifts_grad = sums[: shifts.shape[0]]
        gains_grad = sums[shifts.shape[0] : bias_start]
        bias_grad = sums[bias_start : bias_start + bias_rows].reshape(-1)
    else:
        grad_active = right_product(grad_down, feed_down)
        grad_inner = (grad_active * slope).astype(BF16)
        inner_bias_grad = column_sums(grad_inner)
        grad_hidden_two = grad_three + right_product(grad_inner, feed_up)
        grad_two, gain_grad_two, shift_grad_two = norm_backward(
            grad_hidden_two, normed_two, inverse_two, gain_rows[1]
        )
        grad_cross_branch = grad_two.astype(BF16)
        cross_out_bias_grad = column_sums(grad_cross_branch)
        grad_mixed_two = right_product(grad_cross_branch, output_cross)
        query_grad_two, key_grad_two, value_grad_two = attend_backward(
            False, mem_local, own_mem, bases, queries_two, keys_two, values_two, grad_mixed_two, exact_two, scale_two
        )
        query_grad_two = query_grad_two * jnp.asarray(0.125, BF16)

        memory_part = (
            right_product(key_grad_two, key_cross) + right_product(value_grad_two, value_cross)
        ).astype(BF16).reshape(item_count, members, mem_local, D)
        cross_value_bias_grad = column_sums(value_grad_two)
        cross_query_bias_grad = column_sums(query_grad_two)
        grad_hidden_one = grad_two + right_product(query_grad_two, query_cross)
        grad_one, gain_grad_one, shift_grad_one = norm_backward(
            grad_hidden_one, normed_one, inverse_one, gain_rows[0]
        )
        grad_self_branch = grad_one.astype(BF16)
        self_out_bias_grad = column_sums(grad_self_branch)
        grad_mixed_one = right_product(grad_self_branch, output_self)
        query_grad_one, key_grad_one, value_grad_one = attend_backward(
            True, DEC, own_dec, bases, queries_one, keys_one, values_one, grad_mixed_one, exact_one, scale_one
        )
        query_grad_one = query_grad_one * jnp.asarray(0.125, BF16)
        pairs = (
            (active_low, grad_down),
            (hidden_two_low, grad_inner),
            (mixed_two, grad_cross_branch),
            (memory_flat, key_grad_two),
            (memory_flat, value_grad_two),
            (hidden_one_low, query_grad_two),
            (mixed_one, grad_self_branch),
            (tokens, query_grad_one),
            (tokens, key_grad_one),
            (tokens, value_grad_one),
        )
        grads, memory_back = scatter_by_collectives(pairs, blocks, memory_part, row, member, items_count, members)
        (
            feed_down_grad, feed_up_grad, output_cross_grad, key_cross_grad, value_cross_grad, query_cross_grad,
            output_self_grad, query_self_grad, key_self_grad, value_self_grad,
        ) = grads
        memory_grad = lax.dynamic_update_slice_in_dim(
            memory_back.astype(F32), memory_part[:, 0].astype(F32), member * item_count, 0
        )
        tokens_grad = (
            grad_one
            + right_product(query_grad_one, query_self)
            + right_product(key_grad_one, key_self)
            + right_product(value_grad_one, value_self)
        )
        vectors = jnp.concatenate(
            [
                column_sums(query_grad_one),
                column_sums(value_grad_one),
                self_out_bias_grad,
                cross_query_bias_grad,
                cross_value_bias_grad,
                cross_out_bias_grad,
                out_bias_grad,
                shift_grad_one,
                shift_grad_two,
                shift_grad_three,
                gain_grad_one,
                gain_grad_two,
                gain_grad_three,
                inner_bias_grad,
            ]
        )
        vectors = lax.psum(vectors.reshape(-1, 128), ("items", "mem")).reshape(-1)
        shift_count = shifts.shape[0] * D
        gain_count = gains.shape[0] * D
        shift_width, gain_width, bias_width = shifts.shape[1], gains.shape[1], inner_bias.shape[0]
        shifts_grad = lax.dynamic_slice_in_dim(
            vectors[:shift_count].reshape(-1, D), row * shift_width, shift_width, 1
        )
        gains_grad = lax.dynamic_slice_in_dim(
            vectors[shift_count : shift_count + gain_count].reshape(-1, D), row * gain_width, gain_width, 1
        )
        bias_grad = lax.dynamic_slice_in_dim(vectors[shift_count + gain_count :], row * bias_width, bias_width)
    return (
        layer_out,
        tokens_grad,
        memory_grad,
        query_self_grad,
        key_self_grad,
        value_self_grad,
        output_self_grad,
        query_cross_grad,
        key_cross_grad,
        value_cross_grad,
        output_cross_grad,
        feed_up_grad,
        feed_down_grad,
        shifts_grad,
        gains_grad,
        bias_grad,
    )


def solution(mesh):
    tiles = P("items", "mem")
    rows = P(("items", "mem"), None)
    blocks = P("items", "mem", None)
    return jax.shard_map(
        functools.partial(body, mesh.shape["items"], mesh.shape["mem"]),
        mesh=mesh,
        in_specs=(rows, blocks, rows, P("items"), P("items"))
        + (tiles,) * 10
        + (P(None, "items"), P(None, "items"), P("items")),
        out_specs=(rows, rows, blocks) + (tiles,) * 10 + (P(None, "items"), P(None, "items"), P("items")),
        check_vma=False,
    )
```

```python
import functools

import jax
import jax.numpy as jnp
from jax import lax
from jax.experimental import pallas as pl
from jax.experimental.pallas import tpu as pltpu
from jax.sharding import PartitionSpec as P

D = 1024
HEADS = 16
HEAD_DIM = 64
PAIR = 2 * HEAD_DIM
PAIRS = HEADS // 2
DEC = 128
half_root = 0.7071067811865476
normal_peak = 0.3989422804014327
MESH = pl.DeviceIdType.MESH
F32 = jnp.float32
BF16 = jnp.bfloat16
X_LAG, FIRST_PIECE, SPREAD, STRAIGHT = 1, 2, 17, 3
ANY = pl.BlockSpec(memory_space=pl.ANY)
VMEM = pl.BlockSpec(memory_space=pltpu.VMEM)


def product(first_op, second_op):
    return jnp.dot(first_op, second_op, preferred_element_type=F32)


def left_product(first_op, second_op):
    return lax.dot_general(
        first_op, second_op, (((0,), (0,)), ((), ())), preferred_element_type=F32
    )


def right_product(first_op, second_op):
    return lax.dot_general(
        first_op, second_op, (((1,), (1,)), ((), ())), preferred_element_type=F32
    )


def column_sums(values):
    return jnp.sum(values.astype(F32), 0)


def norm_forward(values, gain, shift):
    center = values - jnp.mean(values, -1, keepdims=True)
    inverse = lax.rsqrt(jnp.mean(center * center, -1, keepdims=True) + 1e-05)
    normed = center * inverse
    return (normed * gain + shift, normed, inverse)


def norm_backward(grad_out, normed, inverse, gain):
    scaled = grad_out * gain
    grad_in = inverse * (
        scaled
        - jnp.mean(scaled, -1, keepdims=True)
        - normed * jnp.mean(scaled * normed, -1, keepdims=True)
    )
    return (grad_in, jnp.sum(grad_out * normed, 0), jnp.sum(grad_out, 0))


def gather_kernel(members, items_here, units, forward, *refs):
    count = len(units)
    weights = 1 + max(unit[0] for unit in units)
    shard_refs = refs[:weights]
    memory_ref, vector_ref, tokens_ref, limits_ref = refs[weights : weights + 4]
    refs = refs[weights + 4 :]
    whole_refs, items_ref, vectors_ref = refs[:weights], refs[weights], refs[weights + 1]
    refs = refs[weights + 2 :]
    outs, refs = refs[: forward.outs], refs[forward.outs :]
    send_sem, recv_sem, copy_sem, mem_send, mem_recv, mem_copy, vec_send, vec_recv, bounce = refs[:9]
    row = lax.axis_index("items")
    member = lax.axis_index("mem")
    hops = members - 1
    core_peer, first_peer, second_peer = row ^ 1, row ^ 2, row ^ 4
    UP, DOWN = 0, hops
    ALONG_X, ALONG_Y, HALF_A, HALF_B, CORE = 2 * hops, 2 * hops + 1, 2 * hops + 2, 2 * hops + 3, 2 * hops + 4

    barrier = pltpu.get_barrier_semaphore()
    partners = [(row ^ distance, member) for distance in range(1, 8)]
    partners += [(row, lax.rem(member + step, members)) for step in range(1, members)]
    for partner in partners:
        pl.semaphore_signal(barrier, inc=1, device_id=partner, device_id_type=MESH)
    pl.semaphore_wait(barrier, len(partners))

    def place(unit, owner):
        weight, start, depth, height = units[unit]
        return pl.ds(pl.multiple_of(owner * height + start, depth), depth)

    def cols(unit, who):
        width = shard_refs[units[unit][0]].shape[1]
        return pl.ds(pl.multiple_of(who * width, width), width)

    def shard(unit):
        weight, start, depth, height = units[unit]
        return shard_refs[weight].at[pl.ds(start, depth)]

    def remote(unit, kind, src, dst, device):
        return pltpu.make_async_remote_copy(
            src_ref=src,
            dst_ref=dst,
            send_sem=send_sem.at[unit, kind],
            recv_sem=recv_sem.at[unit, kind],
            device_id=device,
            device_id_type=MESH,
        )

    def along(unit, hop, upward):
        whole = whole_refs[units[unit][0]]
        origin = member - hop if upward else member + hop
        origin = jnp.clip(origin, 0, members - 1)
        piece = whole.at[place(unit, row), cols(unit, origin)]
        target = jnp.clip(member + 1 if upward else member - 1, 0, members - 1)
        return remote(
            unit, (UP if upward else DOWN) + hop, shard(unit) if hop == 0 else piece, piece, (row, target)
        )

    straight = range(STRAIGHT)

    def straight_copy(unit, hop, upward):
        target = jnp.clip(member + hop + 1 if upward else member - hop - 1, 0, members - 1)
        piece = whole_refs[units[unit][0]].at[place(unit, row), cols(unit, member)]
        return remote(unit, (UP if upward else DOWN) + hop, shard(unit), piece, (row, target))

    def straight_each(unit, act):
        for hop in range(hops):
            @pl.when(member + hop + 1 <= members - 1)
            def _():
                act(straight_copy(unit, hop, True))

            @pl.when(member - hop - 1 >= 0)
            def _():
                act(straight_copy(unit, hop, False))

    def along_start(unit, hop):
        @pl.when((member >= hop) & (member < members - 1))
        def _():
            along(unit, hop, True).start()

        @pl.when((member <= members - 1 - hop) & (member > 0))
        def _():
            along(unit, hop, False).start()

    def along_arrive(unit, hop):
        @pl.when(member >= hop + 1)
        def _():
            along(unit, hop, True).wait_recv()

        @pl.when(member <= members - 2 - hop)
        def _():
            along(unit, hop, False).wait_recv()

    def along_sent(unit, hop):
        @pl.when((member >= hop) & (member < members - 1))
        def _():
            along(unit, hop, True).wait_send()

        @pl.when((member <= members - 1 - hop) & (member > 0))
        def _():
            along(unit, hop, False).wait_send()

    def own_copy(unit):
        return pltpu.make_async_copy(
            shard(unit), whole_refs[units[unit][0]].at[place(unit, row), cols(unit, member)], copy_sem.at[unit]
        )

    def block(unit, kind, owner, device, half=None):
        weight, start, depth, height = units[unit]
        if half is None:
            rows = place(unit, owner)
        else:
            part = depth // 2
            rows = pl.ds(pl.multiple_of(owner * height + start + half * part, part), part)
        ref = whole_refs[weight].at[rows]
        return remote(unit, kind, ref, ref, (device, member))

    def to_x(unit):
        return block(unit, ALONG_X, row, first_peer)

    def to_y(unit):
        return block(unit, ALONG_Y, row, second_peer)

    def half_a(unit):
        return block(unit, HALF_A, first_peer, second_peer, 0)

    def half_b(unit):
        return block(unit, HALF_B, second_peer, first_peer, 1)

    def to_core(unit, which):
        owner = (row, first_peer, second_peer, row ^ 6)[which]
        return block(unit, CORE + which, owner, core_peer)

    pieces = memory_ref.shape[1] // 32 * items_here

    def memory_send(piece, step):
        which, start = piece // (pieces // items_here), piece % (pieces // items_here) * 32
        target = lax.rem(member + step, members)
        return pltpu.make_async_remote_copy(
            src_ref=memory_ref.at[target * items_here + which, pl.ds(start, 32)],
            dst_ref=items_ref.at[which, step, pl.ds(start, 32)],
            send_sem=mem_send.at[piece, step],
            recv_sem=mem_recv.at[piece, step],
            device_id=(row, target),
            device_id_type=MESH,
        )

    fetch = pltpu.make_async_copy(memory_ref.at[pl.ds(member * items_here, items_here)], bounce, mem_copy.at[0])
    local = pltpu.make_async_copy(bounce, items_ref.at[:, 0], mem_copy.at[1])
    fetch.start()
    spot = vectors_ref.at[:, pl.ds(pl.multiple_of(row * 128, 128), 128)]
    vector_copies = [
        pltpu.make_async_remote_copy(
            src_ref=vector_ref,
            dst_ref=spot,
            send_sem=vec_send.at[distance],
            recv_sem=vec_recv.at[distance],
            device_id=(row ^ distance, member),
            device_id_type=MESH,
        )
        for distance in range(1, 8)
    ]
    vector_copies.append(pltpu.make_async_copy(vector_ref, spot, vec_send.at[0]))
    for copy in vector_copies:
        copy.start()

    due = [FIRST_PIECE + piece * SPREAD // pieces for piece in range(pieces)]
    plane_lag = 1
    done_lag = plane_lag + 2 * X_LAG + 1
    jobs = forward.jobs(
        members, items_here, member, tokens_ref, limits_ref, whole_refs, items_ref, vectors_ref, outs, refs[9:],
        done_lag, due,
    )
    last = max([count - 1 + done_lag, due[-1] + 2] + list(jobs))
    for tick in range(last + 1):
        unit = tick - plane_lag
        if 0 <= unit < count:
            for hop in range(hops) if unit in straight else (hops - 1,):
                along_arrive(unit, hop)
            own_copy(unit).wait()
            to_x(unit).start()
            to_y(unit).start()
            to_core(unit, 0).start()
        if tick in straight:
            straight_each(tick, lambda copy: copy.start())
            own_copy(tick).start()
        for hop in range(hops):
            unit = tick + hops - plane_lag - hop
            if unit not in straight and 0 <= unit < count:
                if hop == 0:
                    own_copy(unit).start()
                else:
                    along_arrive(unit, hop - 1)
                along_start(unit, hop)
        for piece in range(pieces):
            if due[piece] == tick:
                for step in range(1, members):
                    memory_send(piece, step).start()
        unit = tick - plane_lag - X_LAG
        if 0 <= unit < count:
            to_x(unit).wait_recv()
            half_a(unit).start()
            to_core(unit, 1).start()
            to_y(unit).wait_recv()
            half_b(unit).start()
            to_core(unit, 2).start()
        unit = tick - plane_lag - 2 * X_LAG
        if 0 <= unit < count:
            half_a(unit).wait_recv()
            half_b(unit).wait_recv()
            to_core(unit, 3).start()
        if tick == 1:
            fetch.wait()
            local.start()
        if tick == 3:
            local.wait()
            for copy in vector_copies:
                copy.wait()
        unit = tick - done_lag
        if 0 <= unit < count:
            for which in range(4):
                to_core(unit, which).wait_recv()
        for piece in range(pieces):
            if due[piece] + 2 == tick:
                for step in range(1, members):
                    memory_send(piece, step).wait_recv()
        for job in jobs.get(tick, ()):
            job()
    for unit in range(count):
        if unit in straight:
            straight_each(unit, lambda copy: copy.wait_send())
        else:
            for hop in range(hops):
                along_sent(unit, hop)
        to_x(unit).wait_send()
        to_y(unit).wait_send()
        half_a(unit).wait_send()
        half_b(unit).wait_send()
        for which in range(4):
            to_core(unit, which).wait_send()
    for piece in range(pieces):
        for step in range(1, members):
            memory_send(piece, step).wait_send()
    forward.finish()


def attend_parts(queries, keys_at, values_at, allowed_at, chunks):
    lane_low = low_lanes(DEC)
    q2 = stack_pair(queries, lane_low)
    numer, total = None, None
    for step in range(chunks):
        scores = right_product(q2, keys_at(step))
        exp_scores = jnp.where(allowed_at(step), jnp.exp(scores), 0.0)
        part = jnp.sum(exp_scores, -1, keepdims=True)
        term = product(exp_scores.astype(BF16), values_at(step))
        total = part if total is None else total + part
        numer = term if numer is None else numer + term
    return jnp.where(lane_low, numer[:DEC], numer[DEC:]), jnp.where(lane_low, total[:DEC], total[DEC:])


def attend_pair(queries, keys_at, values_at, allowed_at, chunks):
    numer, total = attend_parts(queries, keys_at, values_at, allowed_at, chunks)
    scale = 1.0 / total
    return numer * scale, scale


class Forward:
    outs = 16

    def __init__(self, rows, items_here, members, mem_local):
        self.rows, self.items_here, self.members, self.mem_local = rows, items_here, members, mem_local
        self.slots = members * mem_local

    def out_shapes(self):
        wide, low = jax.ShapeDtypeStruct((self.rows, D), F32), jax.ShapeDtypeStruct((self.rows, D), BF16)
        keys = jax.ShapeDtypeStruct((self.items_here, self.members, self.mem_local, D), BF16)
        inverse = jax.ShapeDtypeStruct((self.rows, 1), F32)
        return [low, low, low, low, wide, wide, wide, low, wide, low, inverse, low, wide, wide, keys, keys]

    def out_specs(self):
        return [ANY] * 10 + [VMEM] * 4 + [ANY] * 2

    def scratch(self):
        return [pltpu.VMEM(shape.shape, shape.dtype) for shape in self.out_shapes()[:10]] + [
            pltpu.VMEM((2, D, D), BF16),
            pltpu.VMEM((2, D, D), BF16),
            pltpu.VMEM((2, self.members, self.mem_local // 4, D), BF16),
            pltpu.VMEM((self.items_here, self.members, self.mem_local, D), BF16),
            pltpu.VMEM((self.items_here, self.members, self.mem_local, D), BF16),
            pltpu.SemaphoreType.DMA((20,)),
        ]

    def jobs(
        self, members, items_here, member, tokens_ref, limits_ref, whole_refs, items_ref, vectors_ref, outs, scratch,
        done_lag, due,
    ):
        early, (inverse_one, mixed_two, exact_two, scale_two, keys_out, values_out) = outs[:10], outs[10:]
        q_one, k_one, v_one, mixed_one, exact_one, scale_one, hidden_one, hidden_low, normed_one, q_two = scratch[:10]
        weight_buf, cross_buf, rows_buf, keys, values, sems = scratch[10:]
        early_copies = [
            pltpu.make_async_copy(source, target, sems.at[10 + place])
            for place, (source, target) in enumerate(zip(scratch[:10], early))
        ]
        part = self.mem_local // 4
        schedule = {}

        def at(tick, *jobs):
            schedule.setdefault(tick, []).extend(jobs)

        def vector(index):
            return vectors_ref[...].astype(F32)[index : index + 1]

        def fetch_weight(unit, slot):
            return pltpu.make_async_copy(whole_refs[unit], weight_buf.at[slot], sems.at[slot])

        def fetch_cross(unit):
            return pltpu.make_async_copy(whole_refs[unit], cross_buf.at[unit], sems.at[2 + unit])

        def fetch_rows(which, chunk):
            slot = chunk % 2
            return pltpu.make_async_copy(
                items_ref.at[which, :, pl.ds(chunk * part, part)], rows_buf.at[slot], sems.at[4 + slot]
            )

        def store(which, value):
            source, target = ((keys, keys_out), (values, values_out))[value]
            return pltpu.make_async_copy(source.at[which], target.at[which], sems.at[6 + 2 * which + value])

        self.pending = []

        def project(slot, unit, result, shift, scale):
            def job():
                fetch_weight(unit, slot).wait()
                total = product(tokens_ref[...], weight_buf[slot])
                if shift is not None:
                    total = total + vector(shift)
                if scale is not None:
                    total = total * scale
                result[...] = total.astype(BF16)

            return job

        def self_attend(which):
            def job():
                limit = limits_ref[0:1, which : which + 1]
                slot = lax.broadcasted_iota(jnp.int32, (2 * DEC, DEC), 1)
                query = lax.broadcasted_iota(jnp.int32, (2 * DEC, DEC), 0) % DEC
                allowed = (slot <= query) & (slot < limit)
                rows = pl.ds(which * DEC, DEC)

                def pair(p, _):
                    cols = pl.ds(pl.multiple_of(p * PAIR, PAIR), PAIR)
                    exact, scale = attend_pair(
                        q_one[rows, cols], lambda _: k_one[rows, cols], lambda _: v_one[rows, cols], lambda _: allowed, 1
                    )
                    mixed_one[rows, cols] = exact.astype(BF16)
                    exact_one[rows, cols] = exact
                    scale_one[rows, cols] = scale
                    return 0

                lax.fori_loop(0, PAIRS, pair, 0)

            return job

        def first_norm(slot, unit):
            def job():
                fetch_weight(unit, slot).wait()
                resid = tokens_ref[...].astype(F32) + product(mixed_one[...], weight_buf[slot]) + vector(2)
                hidden, normed, inverse = norm_forward(resid, vector(10), vector(7))
                hidden_one[...] = hidden
                hidden_low[...] = hidden.astype(BF16)
                normed_one[...] = normed
                inverse_one[...] = inverse

            return job

        def cross_query(slot, unit):
            def job():
                fetch_weight(unit, slot).wait()
                total = (product(hidden_low[...], weight_buf[slot]) + vector(3)) * 0.125
                q_two[...] = total.astype(BF16)

            return job

        def project_rows(which, chunk):
            def job():
                fetch_rows(which, chunk).wait()
                rows = rows_buf[chunk % 2].reshape(members * part, D)
                new_keys = product(rows, cross_buf[0]).astype(BF16).reshape(members, part, D)
                new_values = (product(rows, cross_buf[1]) + vector(4)).astype(BF16).reshape(members, part, D)
                keys[which, :, pl.ds(chunk * part, part)] = new_keys
                values[which, :, pl.ds(chunk * part, part)] = new_values
                if chunk == 3:
                    store(which, 0).start()
                    store(which, 1).start()

            return job

        def cross_attend(which, low, high, first, size, begin, end):
            def job():
                rows = pl.ds(which * DEC, DEC)
                limit = limits_ref[1:2, which : which + 1] - first
                slot = lax.broadcasted_iota(jnp.int32, (2 * DEC, size), 1)

                def allowed(step):
                    return slot < limit - lax.rem(member - step + members, members) * self.mem_local

                def pair(p, _):
                    cols = pl.ds(pl.multiple_of(p * PAIR, PAIR), PAIR)
                    numer, total = attend_parts(
                        q_two[rows, cols],
                        lambda step: keys[which, step, pl.ds(first, size), cols],
                        lambda step: values[which, step, pl.ds(first, size), cols],
                        allowed,
                        members,
                    )
                    if not begin:
                        numer, total = numer + exact_two[rows, cols], total + scale_two[rows, cols]
                    if end:
                        scale = 1.0 / total
                        exact = numer * scale
                        mixed_two[rows, cols] = exact.astype(BF16)
                        exact_two[rows, cols] = exact
                        scale_two[rows, cols] = scale
                    else:
                        exact_two[rows, cols] = numer
                        scale_two[rows, cols] = total
                    return 0

                lax.fori_loop(low, high, pair, 0)

            return job

        for unit in range(2):
            at(unit + done_lag, fetch_cross(unit).start)
        for unit in range(2, 7):
            at(unit + done_lag, fetch_weight(unit, unit % 2).start)
        at(1 + done_lag + 1, fetch_cross(0).wait)
        at(1 + done_lag + 1, fetch_cross(1).wait)
        start = 2 + done_lag + 1
        at(start, project(0, 2, q_one, 0, 0.125))
        at(start + 1, project(1, 3, k_one, None, None))
        at(start + 2, project(0, 4, v_one, 1, None))
        at(start + 2, self_attend(0))
        at(start + 3, self_attend(1))
        at(start + 3, first_norm(1, 5))
        at(start + 4, cross_query(0, 6))
        at(start + 5, *[copy.start for copy in early_copies])
        previous = 1 + done_lag
        per_item = len(due) // items_here
        for which in range(items_here):
            for chunk in range(4):
                ready = due[which * per_item + (chunk + 1) * per_item // 4 - 1] + 2
                begin = max(ready, previous)
                at(begin, fetch_rows(which, chunk).start)
                late = begin if which == items_here - 1 and chunk == 3 else begin + 1
                at(late, project_rows(which, chunk))
                previous = begin + 1
            begin = max(previous, start + 5)
            if which < items_here - 1:
                for quarter in range(4):
                    at(begin + quarter, cross_attend(which, 2 * quarter, 2 * quarter + 2, 0, self.mem_local, True, True))
            else:
                at(late - 1, cross_attend(which, 0, PAIRS, 0, 3 * part, True, False))
                at(late, cross_attend(which, 0, PAIRS, 3 * part, part, False, True))
        self.pending = early_copies + [store(which, value) for which in range(items_here) for value in range(2)]
        return schedule

    def finish(self):
        for copy in self.pending:
            copy.wait()


def gather_by_kernel(shards, memory, vector, tokens, limits, items_count, members):
    items_here = memory.shape[0] // members
    units = []
    for weight, shard in enumerate(shards):
        height, width = shard.shape
        depth = height * 256 // max(height * width // 128, 256)
        for start in range(0, height, depth):
            units.append((weight, start, depth, height))
    forward = Forward(tokens.shape[0], items_here, members, memory.shape[1])
    pieces = memory.shape[1] // 32 * items_here
    hops = members - 1
    kinds = 2 * hops + 8
    out_shape = [jax.ShapeDtypeStruct((s.shape[0] * items_count, s.shape[1] * members), s.dtype) for s in shards]
    out_shape.append(
        jax.ShapeDtypeStruct((items_here, members, memory.shape[1], memory.shape[2]), memory.dtype)
    )
    out_shape.append(jax.ShapeDtypeStruct((vector.shape[0], vector.shape[1] * items_count), vector.dtype))
    gathered = len(out_shape)
    out_shape += forward.out_shapes()
    outs = pl.pallas_call(
        functools.partial(gather_kernel, members, items_here, tuple(units), forward),
        out_shape=out_shape,
        in_specs=[VMEM] * len(shards) + [ANY, VMEM, VMEM, VMEM],
        out_specs=[ANY] * (gathered - 1) + [VMEM] + forward.out_specs(),
        scratch_shapes=[
            pltpu.SemaphoreType.DMA((len(units), kinds)),
            pltpu.SemaphoreType.DMA((len(units), kinds)),
            pltpu.SemaphoreType.DMA((len(units),)),
            pltpu.SemaphoreType.DMA((pieces, members)),
            pltpu.SemaphoreType.DMA((pieces, members)),
            pltpu.SemaphoreType.DMA((2,)),
            pltpu.SemaphoreType.DMA((items_count,)),
            pltpu.SemaphoreType.DMA((items_count,)),
            pltpu.VMEM((items_here,) + memory.shape[1:], memory.dtype),
        ]
        + forward.scratch(),
        compiler_params=pltpu.CompilerParams(
            collective_id=0, has_side_effects=True, vmem_limit_bytes=60 * 1024 * 1024
        ),
        name="gather_all",
    )(*shards, memory, vector, tokens, limits)
    return outs[: gathered - 2], outs[gathered - 2], outs[gathered - 1], outs[gathered:]


def gather_by_collectives(shards, memory, vector, items_count, members):
    whole = []
    for shard in shards:
        cols = lax.all_gather(shard, "mem", axis=1, tiled=True)
        whole.append(lax.all_gather(cols, "items", axis=0, tiled=True))
    items_here = memory.shape[0] // members
    member = lax.axis_index("mem")
    parts = []
    for step in range(members):
        target = lax.rem(member + step, members)
        part = lax.dynamic_slice_in_dim(memory, target * items_here, items_here)
        if step:
            part = lax.ppermute(part, "mem", [(a, (a + step) % members) for a in range(members)])
        parts.append(part)
    return whole, jnp.stack(parts, 1), lax.all_gather(vector, "items", axis=1, tiled=True)


def stack_pair(values, lane_low):
    zero = jnp.zeros_like(values)
    return jnp.concatenate([jnp.where(lane_low, values, zero), jnp.where(lane_low, zero, values)], 0)


def low_lanes(rows):
    return lax.broadcasted_iota(jnp.int32, (rows, PAIR), 1) < HEAD_DIM


def allowed_slots(causal, chunk, lens_ref, bases_ref, which, step, key_dim):
    shape = (2 * DEC, chunk) if key_dim == 1 else (chunk, 2 * DEC)
    slot = lax.broadcasted_iota(jnp.int32, shape, key_dim)
    if causal:
        query = lax.broadcasted_iota(jnp.int32, shape, 1 - key_dim) % DEC
        return (slot <= query) & (slot < lens_ref[which])
    return slot < lens_ref[which] - bases_ref[step]


def attend_forward_kernel(causal, chunk, lens_ref, bases_ref, q_ref, k_ref, v_ref, mixed_ref, exact_ref, scale_ref):
    which = pl.program_id(0)
    lane_low = low_lanes(DEC)
    q2 = stack_pair(q_ref[...], lane_low)
    numer = jnp.zeros((2 * DEC, PAIR), F32)
    total = jnp.zeros((2 * DEC, 1), F32)
    for step in range(k_ref.shape[0] // chunk):
        rows = pl.ds(step * chunk, chunk)
        scores = right_product(q2, k_ref[rows, :])
        allowed = allowed_slots(causal, chunk, lens_ref, bases_ref, which, step, 1)
        exp_scores = jnp.where(allowed, jnp.exp(scores), 0.0)
        total += jnp.sum(exp_scores, -1, keepdims=True)
        numer += product(exp_scores.astype(BF16), v_ref[rows, :])
    numer = jnp.where(lane_low, numer[:DEC], numer[DEC:])
    scale = 1.0 / jnp.where(lane_low, total[:DEC], total[DEC:])
    exact = numer * scale
    mixed_ref[...] = exact.astype(BF16)
    exact_ref[...] = exact
    scale_ref[...] = scale


def attend_backward_kernel(
    causal, chunk, lens_ref, bases_ref, q_ref, k_ref, v_ref, grad_ref, exact_ref, scale_ref, gq_ref, gk_ref, gv_ref
):
    which = pl.program_id(0)
    lane_low = low_lanes(DEC)
    q2 = stack_pair(q_ref[...], lane_low)
    grad_numer = grad_ref[...] * scale_ref[...]
    gn2 = stack_pair(grad_numer.astype(BF16), lane_low)
    weighted = jnp.transpose(grad_numer * exact_ref[...])
    grad_total = -jnp.concatenate(
        [
            jnp.sum(weighted[:HEAD_DIM], 0, keepdims=True),
            jnp.sum(weighted[HEAD_DIM:], 0, keepdims=True),
        ],
        1,
    )
    gq2 = jnp.zeros((2 * DEC, PAIR), F32)
    for step in range(k_ref.shape[0] // chunk):
        rows = pl.ds(step * chunk, chunk)
        keys = k_ref[rows, :]
        scores = right_product(keys, q2)
        allowed = allowed_slots(causal, chunk, lens_ref, bases_ref, which, step, 0)
        exp_scores = jnp.where(allowed, jnp.exp(scores), 0.0)
        grad_exp = right_product(v_ref[rows, :], gn2) + grad_total
        grad_scores = (exp_scores * grad_exp).astype(BF16)
        gk_ref[rows, :] = product(grad_scores, q2).astype(BF16)
        gv_ref[rows, :] = product(exp_scores.astype(BF16), gn2).astype(BF16)
        gq2 += left_product(grad_scores, keys)
    gq_ref[...] = jnp.where(lane_low, gq2[:DEC], gq2[DEC:]).astype(BF16)


def attention_call(kernel, causal, chunk, lens, bases, queries, keys, values, more, outs):
    item_count = lens.shape[0]
    slots = keys.shape[0] // item_count
    q_spec = pl.BlockSpec((DEC, PAIR), lambda a, p, *_: (a, p))
    k_spec = pl.BlockSpec((slots, PAIR), lambda a, p, *_: (a, p))
    spec = {"q": q_spec, "k": k_spec}
    rows = {"q": queries.shape[0], "k": keys.shape[0]}
    return pl.pallas_call(
        functools.partial(kernel, causal, chunk),
        grid_spec=pltpu.PrefetchScalarGridSpec(
            num_scalar_prefetch=2,
            grid=(item_count, PAIRS),
            in_specs=[q_spec, k_spec, k_spec] + [q_spec] * len(more),
            out_specs=[spec[kind] for kind, _ in outs],
        ),
        out_shape=[jax.ShapeDtypeStruct((rows[kind], D), dtype) for kind, dtype in outs],
        cost_estimate=pl.CostEstimate(
            flops=4 * item_count * HEADS * DEC * slots * 256, bytes_accessed=16 * D * slots, transcendentals=0
        ),
        name="self_attention" if causal else "cross_attention",
    )(lens, bases, queries, keys, values, *more)


def attend_forward(causal, chunk, lens, bases, queries, keys, values):
    return attention_call(
        attend_forward_kernel, causal, chunk, lens, bases, queries, keys, values, (),
        (("q", BF16), ("q", F32), ("q", F32)),
    )


def attend_backward(causal, chunk, lens, bases, queries, keys, values, grad_mixed, exact, scale):
    return attention_call(
        attend_backward_kernel, causal, chunk, lens, bases, queries, keys, values, (grad_mixed, exact, scale),
        (("q", BF16), ("k", BF16), ("k", BF16)),
    )


def halving_order(items_count, flipped):
    bits = [1 << b for b in range(1, items_count.bit_length() - 1)]
    return [1] + (bits if flipped else bits[::-1])


def block_order(items_count, flipped):
    bits = halving_order(items_count, flipped)
    order = []
    for spot in range(items_count):
        distance = 0
        for place, bit in enumerate(bits):
            if spot >> (len(bits) - 1 - place) & 1:
                distance |= bit
        order.append(distance)
    return order


def order_columns(values, row, items_count, flipped):
    width = values.shape[1] // items_count
    return jnp.concatenate(
        [
            lax.dynamic_slice_in_dim(values, (row ^ distance) * width, width, 1)
            for distance in block_order(items_count, flipped)
        ],
        1,
    )


def reduce_rows(partial, items_count, flipped):
    for bit in halving_order(items_count, flipped):
        half = partial.shape[0] // 2
        arrived = lax.ppermute(partial[half:], "items", [(a, a ^ bit) for a in range(items_count)])
        partial = (partial[:half].astype(F32) + arrived.astype(F32)).astype(BF16)
    return partial


def reduce_columns(partial, member, members):
    bit = members // 2
    while bit:
        half = partial.shape[1] // 2
        high = (member & bit) != 0
        left, right = partial[:, :half], partial[:, half:]
        arrived = lax.ppermute(
            jnp.where(high, left, right), "mem", [(a, a ^ bit) for a in range(members)]
        )
        partial = jnp.where(high, right, left).astype(F32) + arrived.astype(F32)
        if bit > 1:
            partial = partial.astype(BF16)
        bit //= 2
    return partial


def weight_gradients(left_ordered, grads, items_count, member, members, flipped):
    width = grads[0].shape[1]
    joined = grads[0] if len(grads) == 1 else jnp.concatenate(grads, 1)
    partial = left_product(left_ordered, joined).astype(BF16)
    partial = reduce_rows(partial, items_count, flipped)
    return [
        reduce_columns(partial[:, k * width : (k + 1) * width], member, members) for k in range(len(grads))
    ]

RING, KEPT, ROUND, CORES = 4, 6, 10, 3
BACK_PIECES, BACK_EARLY, BACK_LATE, DIRECT = 8, 6, 4, 0
S_LAG = 2


def total_grads(weighted):
    weighted = jnp.transpose(weighted)
    return -jnp.concatenate(
        [jnp.sum(weighted[:HEAD_DIM], 0, keepdims=True), jnp.sum(weighted[HEAD_DIM:], 0, keepdims=True)], 1
    )


def attend_back_chunk(q2, gn2, grad_total, keys, values, allowed):
    exp_scores = jnp.where(allowed, jnp.exp(right_product(keys, q2)), 0.0)
    grad_exp = right_product(values, gn2) + grad_total
    grad_scores = (exp_scores * grad_exp).astype(BF16)
    return product(grad_scores, q2), product(exp_scores.astype(BF16), gn2), left_product(grad_scores, keys)


class Given:
    (
        active, grad_down, hidden_two, slope, feed_down, feed_up, grad_three, normed_two, mixed_two, q_two, exact_two,
        scale_two, tokens, mixed_one, hidden_one, normed_one, q_one, k_one, v_one, keys, values, memory, exact_one,
        scale_one, output_cross, key_cross, value_cross, query_cross, output_self, query_self, key_self, value_self,
    ) = range(32)
    count = 32


class Small:
    inverse_one, inverse_two, gains, limits, vectors = range(5)
    count = 5


class Block:
    fo, fi, co, ck, cv, cq, so, sq, sk, sv = range(10)
    count = 10


def scatter_kernel(members, items_here, mem_local, *refs):
    big, refs = refs[: Given.count], refs[Given.count :]
    small, refs = refs[: Small.count], refs[Small.count :]
    out_refs, refs = refs[: Block.count], refs[Block.count :]
    tokens_grad, vector_out, part_ref, back_ref = refs[:4]
    (
        wide, grad_down, hidden_two, mixed_two, grad_cross, q_two, tokens, mixed_one, hidden_one, normed_one,
        grad_mixed, exact, scale, grad_numer_low, grad_total, key_buf, value_buf, gk_two, gv_two,
        gq_two, weight_buf,
        grad_self, stage, vector_sum, vector_in, vector_far,
        core_out, core_in, near_out, near_in, near_kept, far_out, far_in, own, hop_out, hop_in,
        send_sem, recv_sem, back_send, back_recv, credit, load_sem, kv_sem, stage_sem, vec_send, vec_recv,
    ) = refs[4:]
    gq_one, q_one, k_one, v_one = key_buf.at[0], key_buf.at[1], value_buf.at[0], value_buf.at[1]
    gk_one, gv_one = stage.at[0], stage.at[1]
    row = lax.axis_index("items")
    member = lax.axis_index("mem")
    hops = members - 1
    core_peer = row ^ 1
    slots = members * mem_local

    loads = {}

    def load(name, source, target):
        loads[name] = pltpu.make_async_copy(source, target, load_sem.at[len(loads)])
        loads[name].start()

    def loaded(*names):
        for name in names:
            loads[name].wait()

    def whole(name, target):
        load(name, big[name], target)

    def down_load(k):
        load((Given.feed_down, k), big[Given.feed_down].at[pl.ds(k * D, D)], weight_buf.at[0])

    def up_load(k):
        load((Given.feed_up, k), big[Given.feed_up].at[:, pl.ds(k * D, D)], weight_buf.at[1])

    def slope_load(k):
        load((Given.slope, k), big[Given.slope].at[:, pl.ds(k * D, D)], (exact, scale)[k % 2])

    whole(Given.grad_down, grad_down)
    for k in range(4):
        load((Given.active, k), big[Given.active].at[:, pl.ds(k * D, D)], wide.at[pl.ds(k * 256, 256)])
    down_load(0)
    slope_load(0)
    up_load(0)
    slope_load(1)
    whole(Given.grad_three, tokens_grad)
    whole(Given.normed_two, normed_one)
    whole(Given.q_two, q_two)
    whole(Given.hidden_two, hidden_two)
    whole(Given.mixed_two, mixed_two)
    whole(Given.hidden_one, hidden_one)
    whole(Given.mixed_one, mixed_one)
    whole(Given.tokens, tokens)

    barrier = pltpu.get_barrier_semaphore()
    partners = [(row ^ distance, member) for distance in range(1, 8)]
    partners += [(row, lax.rem(member + step, members)) for step in range(1, members)]
    for partner in partners:
        pl.semaphore_signal(barrier, inc=1, device_id=partner, device_id_type=MESH)
    pl.semaphore_wait(barrier, len(partners))

    units = [(Block.fo, k) for k in range(4)] + [(Block.fi, k) for k in range(4)]
    units += [(name, 0) for name in range(Block.co, Block.count)]
    count = len(units)
    factors = {
        Block.co: (mixed_two, grad_cross),
        Block.ck: (wide, gk_two),
        Block.cv: (wide, gv_two),
        Block.cq: (hidden_one, gq_two),
        Block.so: (mixed_one, grad_self),
        Block.sq: (tokens, gq_one),
        Block.sk: (tokens, gk_one),
        Block.sv: (tokens, gv_one),
    }
    needs = {
        0: (Given.grad_down,) + tuple((Given.active, k) for k in range(4)),
        4: (Given.hidden_two,),
        8: (Given.mixed_two,),
        9: (Given.memory,),
        11: (Given.hidden_one,),
        12: (Given.mixed_one,),
        13: (Given.tokens,),
    }

    def bits(unit):
        return (2, 4) if unit % 2 == 0 else (4, 2)

    def owners(unit, who):
        near, far = bits(unit)
        return (who ^ near, who ^ near ^ far, who ^ far, who)

    def lanes(start, size):
        return pl.ds(pl.multiple_of(start, 128), size)

    def partial(unit, owner):
        name, k = units[unit]
        if name == Block.fo:
            left = wide[pl.ds(pl.multiple_of(owner // 2 * 256, 256), 256), lanes(owner % 2 * 512 + k * 128, 128)]
            return left_product(left, grad_down[...])
        if name == Block.fi:
            right = jnp.concatenate(
                [wide[pl.ds(D + part * 256, 256), pl.ds(k * 256, 256)] for part in range(members)], 1
            )
            return left_product(hidden_two[:, lanes(owner * 128, 128)], right)
        left_ref, right_ref = factors[name]
        depth = right_ref.shape[0]
        if depth <= 512:
            return left_product(left_ref[:, lanes(owner * 128, 128)], right_ref[...])

        def term(spot, sums):
            rows = pl.ds(pl.multiple_of(spot * 512, 512), 512)
            return sums + left_product(left_ref[rows, lanes(owner * 128, 128)], right_ref[rows, :])

        return lax.fori_loop(0, depth // 512, term, jnp.zeros((128, D), F32))

    def remote(unit, kind, src, dst, device):
        return pltpu.make_async_remote_copy(
            src_ref=src,
            dst_ref=dst,
            send_sem=send_sem.at[unit, kind],
            recv_sem=recv_sem.at[unit, kind],
            device_id=device,
            device_id_type=MESH,
        )

    def core_copy(unit):
        return remote(unit, 0, core_out.at[unit % 2], core_in.at[unit % CORES], (core_peer, member))

    def near_copy(unit):
        return remote(
            unit, 1, near_out.at[unit % RING], near_in.at[unit % ROUND], (row ^ bits(unit)[0], member)
        )

    def far_copy(unit):
        return remote(unit, 2, far_out.at[unit % RING], far_in.at[unit % ROUND], (row ^ bits(unit)[1], member))

    direct = range(count - DIRECT, count)

    def hop_copy(unit, hop, upward):
        reach = members - 1 - hop if unit in direct else 1
        target = jnp.clip(member + reach if upward else member - reach, 0, members - 1)
        place = hop if upward else hops + hop
        return remote(
            unit, 3 + place, hop_out.at[unit % RING, place], hop_in.at[unit % ROUND, place], (row, target)
        )

    def hop_sends(hop, upward):
        distance = members - 1 - hop
        return (member + distance <= members - 1) if upward else (member - distance >= 0)

    def hop_gets(unit, hop, upward):
        distance = members - 1 - hop
        if unit in direct:
            return (member >= distance) if upward else (member <= members - 1 - distance)
        return (
            ((member >= 1) & (member - 1 + distance <= members - 1))
            if upward
            else ((member <= members - 2) & (member + 1 - distance >= 0))
        )

    def core_stage(unit):
        loaded(*needs.get(unit, ()))
        if unit >= 2:
            core_copy(unit - 2).wait_send()
        targets = owners(unit, core_peer)

        def fill(spot, _):
            owner = targets[3]
            for k in range(3):
                owner = jnp.where(spot == k, targets[k], owner)
            core_out[unit % 2, spot] = partial(unit, owner).astype(BF16)
            return 0

        lax.fori_loop(0, 4, fill, 0)
        if unit >= CORES:
            pl.semaphore_wait(credit, 1)
        core_copy(unit).start()

    def near_stage(unit):
        core_copy(unit).wait_recv()
        if unit >= RING:
            near_copy(unit - RING).wait_send()
        mine = owners(unit, row)

        def give(spot, _):
            total = partial(unit, jnp.where(spot == 0, mine[0], mine[1])) + core_in[unit % CORES, spot].astype(F32)
            near_out[unit % RING, spot] = total.astype(BF16)
            return 0

        lax.fori_loop(0, 2, give, 0)
        near_copy(unit).start()

        def keep(spot, _):
            total = partial(unit, jnp.where(spot == 0, mine[2], mine[3])) + core_in[unit % CORES, 2 + spot].astype(F32)
            near_kept[unit % KEPT, spot] = total.astype(BF16)
            return 0

        lax.fori_loop(0, 2, keep, 0)
        if unit + CORES < count:
            pl.semaphore_signal(credit, inc=1, device_id=(core_peer, member), device_id_type=MESH)

    def far_stage(unit):
        near_copy(unit).wait_recv()
        if unit >= RING:
            far_copy(unit - RING).wait_send()
        far_out[unit % RING] = (
            near_kept[unit % KEPT, 0].astype(F32) + near_in[unit % ROUND, 1].astype(F32)
        ).astype(BF16)
        far_copy(unit).start()

    def hop_stage(unit, hop):
        if hop == 0:
            far_copy(unit).wait_recv()
            own[unit % RING] = (
                near_kept[unit % KEPT, 1].astype(F32)
                + near_in[unit % ROUND, 0].astype(F32)
                + far_in[unit % ROUND].astype(F32)
            )
        for upward in (True, False):
            distance = members - 1 - hop
            owner = jnp.clip(member + distance if upward else member - distance, 0, members - 1)
            place = hop if upward else hops + hop
            block = lanes(owner * 256, 256)
            if unit >= RING:
                @pl.when(hop_sends(hop, upward))
                def _():
                    hop_copy(unit - RING, hop, upward).wait_send()

            if hop > 0 and unit not in direct:
                arrived = hop_gets(unit, hop - 1, upward)

                @pl.when(arrived)
                def _():
                    hop_copy(unit, hop - 1, upward).wait_recv()
                    hop_out[unit % RING, place] = (
                        own[unit % RING, :, block] + hop_in[unit % ROUND, place - 1].astype(F32)
                    ).astype(BF16)

                @pl.when(hop_sends(hop, upward) & jnp.logical_not(arrived))
                def _():
                    hop_out[unit % RING, place] = own[unit % RING, :, block].astype(BF16)

            else:
                @pl.when(hop_sends(hop, upward))
                def _():
                    hop_out[unit % RING, place] = own[unit % RING, :, block].astype(BF16)

            @pl.when(hop_sends(hop, upward))
            def _():
                hop_copy(unit, hop, upward).start()

    def last_stage(unit):
        name, k = units[unit]
        rows = pl.ds(k * 128 if name == Block.fo else 0, 128)
        cols = pl.ds(k * 256 if name == Block.fi else 0, 256)
        out_refs[name][rows, cols] = own[unit % RING, :, lanes(member * 256, 256)]
        for upward in (True, False):
            for hop in range(hops) if unit in direct else (hops - 1,):
                place = hop if upward else hops + hop

                @pl.when(hop_gets(unit, hop, upward))
                def _():
                    hop_copy(unit, hop, upward).wait_recv()
                    out_refs[name][rows, cols] += hop_in[unit % ROUND, place].astype(F32)

    vector_sum[...] = small[Small.vectors][...]

    def add_vector(index, cols, values):
        vector_sum[index : index + 1, cols] += jnp.sum(values, 0, keepdims=True)

    chunks = [(which, step % members) for which in range(items_here) for step in range(1, members + 1)]

    def key_load(order):
        which, step = chunks[order]
        rows, slot = pl.ds(which * slots + step * mem_local, mem_local), order % 2
        return (
            pltpu.make_async_copy(big[Given.keys].at[rows], key_buf.at[slot], kv_sem.at[0, slot]),
            pltpu.make_async_copy(big[Given.values].at[rows], value_buf.at[slot], kv_sem.at[1, slot]),
        )

    for copy in key_load(0):
        copy.start()

    def feed_back(k):
        def job():
            loaded((Given.feed_down, k), (Given.slope, k))
            grad_active = right_product(grad_down[...], weight_buf[0])
            if k < 3:
                down_load(k + 1)
            else:
                whole(Given.output_cross, weight_buf.at[0])
            grad = (grad_active * (exact, scale)[k % 2][...]).astype(BF16)
            if k < 2:
                slope_load(k + 2)
            wide[pl.ds(D + k * 256, 256), :] = grad
            sums = jnp.sum(grad.astype(F32), 0, keepdims=True)
            for part in range(8):
                target, place = 2 * k + part // 4, part % 4
                vector_sum[13 + place : 14 + place, target * 128 : target * 128 + 128] = sums[
                    :, part * 128 : part * 128 + 128
                ]
            loaded((Given.feed_up, k))
            if k == 0:
                loaded(Given.grad_three)
            tokens_grad[...] += right_product(grad, weight_buf[1])
            if k < 3:
                up_load(k + 1)
            else:
                whole(Given.key_cross, weight_buf.at[1])

        return job

    def middle_norm_back():
        loaded(Given.normed_two)
        grad_in, gain_grad, shift_grad = norm_backward(
            tokens_grad[...], normed_one[...], small[Small.inverse_two][...], small[Small.gains][1:2]
        )
        whole(Given.normed_one, normed_one)
        whole(Given.exact_two, exact)
        whole(Given.scale_two, scale)
        vector_sum[11:12, :] = gain_grad.reshape(1, D)
        vector_sum[8:9, :] = shift_grad.reshape(1, D)
        tokens_grad[...] = grad_in
        grad_cross[...] = grad_in.astype(BF16)
        add_vector(5, pl.ds(0, D), grad_in)
        loaded(Given.output_cross)
        grad_mixed[...] = right_product(grad_cross[...], weight_buf[0])
        whole(Given.value_cross, weight_buf.at[0])
        loaded(Given.q_two, Given.exact_two, Given.scale_two)

    def cross_prepare():
        def pair(p, _):
            cols = lanes(p * PAIR, PAIR)
            for which in range(items_here):
                rows = pl.ds(which * DEC, DEC)
                grad_numer = grad_mixed[rows, cols] * scale[rows, cols]
                grad_numer_low[rows, cols] = grad_numer.astype(BF16)
                grad_total[which, pl.ds(p, 1), :] = total_grads(grad_numer * exact[rows, cols])
            return 0

        lax.fori_loop(0, PAIRS, pair, 0)

    def cross_chunk(order):
        which, step = chunks[order]

        def job():
            for copy in key_load(order):
                copy.wait()
            if order + 1 < len(chunks):
                for copy in key_load(order + 1):
                    copy.start()
            rows, slot = pl.ds(which * DEC, DEC), order % 2
            limit = small[Small.limits][1:2, which : which + 1] - lax.rem(member - step + members, members) * mem_local
            allowed = lax.broadcasted_iota(jnp.int32, (mem_local, 2 * DEC), 0) < limit
            lane_low = low_lanes(DEC)
            at_rows = pl.ds(which * slots + step * mem_local, mem_local)

            def pair(p, _):
                cols = lanes(p * PAIR, PAIR)
                q2 = stack_pair(q_two[rows, cols], lane_low)
                gn2 = stack_pair(grad_numer_low[rows, cols], lane_low)
                gk, gv, gq2 = attend_back_chunk(
                    q2, gn2, grad_total[which, pl.ds(p, 1), :], key_buf[slot, :, cols], value_buf[slot, :, cols], allowed
                )
                gk_two[at_rows, cols] = gk.astype(BF16)
                gv_two[at_rows, cols] = gv.astype(BF16)
                add_vector(4, cols, gv)
                grad = jnp.where(lane_low, gq2[:DEC], gq2[DEC:]) * 0.125
                if step == 1:
                    grad_mixed[rows, cols] = grad
                else:
                    grad_mixed[rows, cols] += grad
                return 0

            lax.fori_loop(0, PAIRS, pair, 0)
            if step == 0:
                gq_two[rows, :] = grad_mixed[rows, :].astype(BF16)
                add_vector(3, pl.ds(0, D), grad_mixed[rows, :])

        return job

    def stage_copy(order):
        which, step = chunks[order]
        own_place = back_ref.at[member * items_here + which]
        target = own_place if step == 0 else part_ref.at[which, step]
        return pltpu.make_async_copy(stage.at[order % 2], target, stage_sem.at[order % 2])

    def memory_part(order):
        which, step = chunks[order]

        def job():
            if order == 0:
                loaded(Given.key_cross, Given.value_cross)
            rows = pl.ds(which * slots + step * mem_local, mem_local)
            total = right_product(gk_two[rows, :], weight_buf[1]) + right_product(gv_two[rows, :], weight_buf[0])
            stage[order % 2] = total.astype(BF16)
            stage_copy(order).start()
            if order == len(chunks) - 1:
                whole(Given.query_cross, weight_buf.at[1])
                whole(Given.output_self, weight_buf.at[0])
                whole(Given.exact_one, exact)
                whole(Given.scale_one, scale)
                whole(Given.q_one, q_one)
                whole(Given.k_one, k_one)
                whole(Given.v_one, v_one)

        return job

    def norm_back():
        loaded(Given.query_cross, Given.normed_one)
        grad = tokens_grad[...] + right_product(gq_two[...], weight_buf[1])
        whole(Given.query_self, weight_buf.at[1])
        grad_in, gain_grad, shift_grad = norm_backward(
            grad, normed_one[...], small[Small.inverse_one][...], small[Small.gains][0:1]
        )
        vector_sum[10:11, :] = gain_grad.reshape(1, D)
        vector_sum[7:8, :] = shift_grad.reshape(1, D)
        tokens_grad[...] = grad_in
        grad_self[...] = grad_in.astype(BF16)
        add_vector(2, pl.ds(0, D), grad_in)
        loaded(Given.output_self)
        grad_mixed[...] = right_product(grad_self[...], weight_buf[0])
        whole(Given.key_self, weight_buf.at[0])
        loaded(Given.exact_one, Given.scale_one, Given.q_one, Given.k_one, Given.v_one)

    def self_back(which, low, high):
        def job():
            rows = pl.ds(which * DEC, DEC)
            limit = small[Small.limits][0:1, which : which + 1]
            slot = lax.broadcasted_iota(jnp.int32, (DEC, 2 * DEC), 0)
            query = lax.broadcasted_iota(jnp.int32, (DEC, 2 * DEC), 1) % DEC
            allowed = (slot <= query) & (slot < limit)

            def pair(p, _):
                cols = lanes(p * PAIR, PAIR)

                lane_low = low_lanes(DEC)
                grad_numer = grad_mixed[rows, cols] * scale[rows, cols]
                gk, gv, gq2 = attend_back_chunk(
                    stack_pair(q_one[rows, cols], lane_low),
                    stack_pair(grad_numer.astype(BF16), lane_low),
                    total_grads(grad_numer * exact[rows, cols]),
                    k_one[rows, cols],
                    v_one[rows, cols],
                    allowed,
                )
                gk_one[rows, cols] = gk.astype(BF16)
                gv_one[rows, cols] = gv.astype(BF16)
                add_vector(1, cols, gv)
                grad = jnp.where(lane_low, gq2[:DEC], gq2[DEC:]) * 0.125
                gq_one[rows, cols] = grad.astype(BF16)
                add_vector(0, cols, grad)
                return 0

            lax.fori_loop(low, high, pair, 0)

        return job

    def token_term(name, slot, grads, following=None):
        def job():
            loaded(name)
            tokens_grad[...] += right_product(grads[...], weight_buf[slot])
            if following:
                whole(following, weight_buf.at[slot])

        return job

    def plane_vector(distance):
        return pltpu.make_async_remote_copy(
            src_ref=vector_sum.at[:, lanes((row ^ distance) * 128, 128)],
            dst_ref=vector_in.at[distance],
            send_sem=vec_send.at[0, distance],
            recv_sem=vec_recv.at[0, distance],
            device_id=(row ^ distance, member),
            device_id_type=MESH,
        )

    def line_vector(step):
        return pltpu.make_async_remote_copy(
            src_ref=vector_in.at[0],
            dst_ref=vector_far.at[step],
            send_sem=vec_send.at[1, step],
            recv_sem=vec_recv.at[1, step],
            device_id=(row, lax.rem(member + step, members)),
            device_id_type=MESH,
        )

    def vectors_start():
        for distance in range(1, 8):
            plane_vector(distance).start()

    def vectors_pass():
        total = vector_sum[:, lanes(row * 128, 128)]
        for distance in range(1, 8):
            plane_vector(distance).wait()
            total = total + vector_in[distance]
        vector_in[0] = total
        for step in range(1, members):
            line_vector(step).start()

    def vectors_end():
        total = vector_in[0]
        for step in range(1, members):
            line_vector(step).wait()
            total = total + vector_far[step]
        vector_out[...] = total

    back_rows = mem_local // BACK_PIECES

    def back_copy(which, step, piece):
        target = lax.rem(member - step + members, members)
        rows = pl.ds(piece * back_rows, back_rows)
        place = (which * members + step) * BACK_PIECES + piece
        return pltpu.make_async_remote_copy(
            src_ref=part_ref.at[which, step, rows],
            dst_ref=back_ref.at[member * items_here + which, rows],
            send_sem=back_send.at[place],
            recv_sem=back_recv.at[place],
            device_id=(row, target),
            device_id_type=MESH,
        )

    schedule = {}

    def at(tick, *jobs):
        schedule.setdefault(tick, []).extend(jobs)

    steps = {}
    for tick, orders in enumerate(((0,), (1,), (2, 3), (4,), (5,), (6,), (7,)), 2):
        for order in orders:
            steps[order] = tick
    at(0, feed_back(0), feed_back(1))
    at(1, feed_back(2), feed_back(3), middle_norm_back)
    at(2, cross_prepare)
    for order in range(len(chunks)):
        at(steps[order], cross_chunk(order))
        if order:
            at(steps[order], stage_copy(order - 1).wait)
        at(steps[order], memory_part(order))
    at(steps[len(chunks) - 1], stage_copy(len(chunks) - 1).wait)
    at(9, norm_back)
    at(10, self_back(0, 0, 8))
    at(11, self_back(1, 0, 4))
    at(12, self_back(1, 4, 8), vectors_start)
    at(14, token_term(Given.query_self, 1, gq_one, Given.value_self), vectors_pass)
    at(15, token_term(Given.key_self, 0, gk_one))
    at(16, token_term(Given.value_self, 1, gv_one), vectors_end)
    far_tick, hop_tick = 1 + S_LAG, 1 + 2 * S_LAG
    moves, tick, weight = [], 0, 0
    for order, (which, step) in enumerate(chunks):
        if step == 0:
            continue
        for piece in range(BACK_PIECES):
            ready = steps[min(order + 1, len(chunks) - 1)]
            if ready > tick:
                tick, weight = ready, 0
            elif weight >= (BACK_EARLY if tick < hop_tick else BACK_LATE):
                tick, weight = tick + 1, 0
            weight += 2 if step == members // 2 else 1
            moves.append((which, step, piece))
            at(tick, back_copy(which, step, piece).start)
    last_tick = hop_tick + hops
    end = count + last_tick

    for tick in range(end):
        if 0 <= tick - far_tick < count:
            far_stage(tick - far_tick)
        if 0 <= tick - 1 < count:
            near_stage(tick - 1)
        if tick == 8:
            whole(Given.memory, wide)
        if 0 <= tick < count:
            core_stage(tick)
        for hop in range(hops):
            if 0 <= tick - hop_tick - hop < count and tick - hop_tick - hop not in direct:
                hop_stage(tick - hop_tick - hop, hop)
        if tick - hop_tick in direct:
            for hop in range(hops):
                hop_stage(tick - hop_tick, hop)
        if 0 <= tick - last_tick < count and tick - last_tick not in direct:
            last_stage(tick - last_tick)
        if tick - hop_tick - 1 in direct:
            last_stage(tick - hop_tick - 1)
        for job in schedule.get(tick, ()):
            job()
    for unit in range(count - 2, count):
        core_copy(unit).wait_send()
    for unit in range(count - RING, count):
        near_copy(unit).wait_send()
        far_copy(unit).wait_send()
        for hop in range(hops):
            for upward in (True, False):
                @pl.when(hop_sends(hop, upward))
                def _():
                    hop_copy(unit, hop, upward).wait_send()
    for move in moves:
        back_copy(*move).wait()


def scatter_by_kernel(big, small, blocks, members, items_here, mem_local):
    count, hops = 16, members - 1
    rows = big[Given.tokens].shape[0]
    low = pltpu.VMEM((rows, D), BF16)
    high = pltpu.VMEM((rows, D), F32)
    slots = items_here * members * mem_local
    out_shape = [jax.ShapeDtypeStruct(block, F32) for block in blocks]
    out_shape += [
        jax.ShapeDtypeStruct((rows, D), F32),
        jax.ShapeDtypeStruct((small[Small.vectors].shape[0], 128), F32),
        jax.ShapeDtypeStruct((items_here, members, mem_local, D), BF16),
        jax.ShapeDtypeStruct((items_here * members, mem_local, D), BF16),
    ]
    outs = pl.pallas_call(
        functools.partial(scatter_kernel, members, items_here, mem_local),
        out_shape=out_shape,
        in_specs=[ANY] * Given.count + [VMEM] * Small.count,
        out_specs=[VMEM] * (len(blocks) + 2) + [ANY, ANY],
        scratch_shapes=[
            pltpu.VMEM((2 * D, D), BF16),
            low, low, low, low, low, low, low, low,
            high,
            high, high, high,
            low,
            pltpu.VMEM((items_here, PAIRS, 2 * DEC), F32),
            pltpu.VMEM((2, mem_local, D), BF16),
            pltpu.VMEM((2, mem_local, D), BF16),
            pltpu.VMEM((slots, D), BF16),
            pltpu.VMEM((slots, D), BF16),
            low,
            pltpu.VMEM((2, D, D), BF16),
            low,
            pltpu.VMEM((2, mem_local, D), BF16),
            pltpu.VMEM(small[Small.vectors].shape, F32),
            pltpu.VMEM((8, small[Small.vectors].shape[0], 128), F32),
            pltpu.VMEM((members, small[Small.vectors].shape[0], 128), F32),
            pltpu.VMEM((2, 4, 128, D), BF16),
            pltpu.VMEM((CORES, 4, 128, D), BF16),
            pltpu.VMEM((RING, 2, 128, D), BF16),
            pltpu.VMEM((ROUND, 2, 128, D), BF16),
            pltpu.VMEM((KEPT, 2, 128, D), BF16),
            pltpu.VMEM((RING, 128, D), BF16),
            pltpu.VMEM((ROUND, 128, D), BF16),
            pltpu.VMEM((RING, 128, D), F32),
            pltpu.VMEM((RING, 2 * hops, 128, 256), BF16),
            pltpu.VMEM((ROUND, 2 * hops, 128, 256), BF16),
            pltpu.SemaphoreType.DMA((count, 3 + 2 * hops)),
            pltpu.SemaphoreType.DMA((count, 3 + 2 * hops)),
            pltpu.SemaphoreType.DMA((items_here * members * BACK_PIECES,)),
            pltpu.SemaphoreType.DMA((items_here * members * BACK_PIECES,)),
            pltpu.SemaphoreType.REGULAR,
            pltpu.SemaphoreType.DMA((48,)),
            pltpu.SemaphoreType.DMA((2, 2)),
            pltpu.SemaphoreType.DMA((2,)),
            pltpu.SemaphoreType.DMA((2, 8)),
            pltpu.SemaphoreType.DMA((2, 8)),
        ],
        compiler_params=pltpu.CompilerParams(
            collective_id=1, has_side_effects=True, vmem_limit_bytes=62 * 1024 * 1024
        ),
        name="scatter_all",
    )(*big, *small)
    return outs[: len(blocks)], outs[len(blocks)], outs[len(blocks) + 1], outs[len(blocks) + 3]


def scatter_by_collectives(pairs, blocks, memory_part, row, member, items_count, members):
    grads = []
    for place, (left, right) in enumerate(pairs):
        ordered = order_columns(left, row, items_count, place % 2 == 1)
        grads += weight_gradients(ordered, [right], items_count, member, members, place % 2 == 1)
    items_here = memory_part.shape[0]
    back = jnp.zeros((items_here * members,) + memory_part.shape[2:], BF16)
    for step in range(1, members):
        part = lax.ppermute(memory_part[:, step], "mem", [(a, (a - step) % members) for a in range(members)])
        owner = lax.rem(member + step, members)
        back = lax.dynamic_update_slice_in_dim(back, part, owner * items_here, 0)
    return grads, back


def body(
    items_count,
    members,
    tokens,
    memory,
    cotangent,
    mem_len,
    dec_len,
    self_query,
    self_key,
    self_value,
    self_out,
    cross_query,
    cross_key,
    cross_value,
    cross_out,
    feed_in,
    feed_out,
    shifts,
    gains,
    inner_bias,
):
    row = lax.axis_index("items")
    member = lax.axis_index("mem")
    rows_here = tokens.shape[0]
    item_count = rows_here // DEC
    group_items = memory.shape[0]
    mem_local = memory.shape[1]
    shards = (
        cross_key, cross_value, self_query, self_key, self_value, self_out, cross_query, cross_out, feed_in, feed_out,
    )
    by_kernel = (items_count, members) == (8, 4)
    shift_width, bias_rows = shifts.shape[1], inner_bias.shape[0] // shifts.shape[1]
    vector = jnp.concatenate([shifts, gains, inner_bias.reshape(bias_rows, shift_width)], 0)
    own_dec = lax.dynamic_slice_in_dim(dec_len, member * item_count, item_count)
    own_mem = lax.dynamic_slice_in_dim(mem_len, member * item_count, item_count)
    if by_kernel:
        whole, item_memory, vectors, forward = gather_by_kernel(
            shards, memory, vector, tokens, jnp.stack([own_dec, own_mem]), items_count, members
        )
    else:
        whole, item_memory, vectors = gather_by_collectives(shards, memory, vector, items_count, members)
    (
        key_cross, value_cross, query_self, key_self, value_self, output_self, query_cross, output_cross,
        feed_up, feed_down,
    ) = whole
    memory_flat = item_memory.reshape(-1, D)
    vectors = vectors.astype(F32)
    bias_start = shifts.shape[0] + gains.shape[0]
    shift_rows = vectors[: shifts.shape[0]]
    gain_rows = vectors[shifts.shape[0] : bias_start]
    inner_shift = (
        vectors[bias_start:].reshape(bias_rows, items_count, shift_width).transpose(1, 0, 2).reshape(-1)
    )

    bases = lax.rem(member - jnp.arange(members, dtype=jnp.int32) + members, members) * mem_local

    if by_kernel:
        (
            queries_one, keys_one, values_one, mixed_one, exact_one, scale_one, hidden_one, hidden_one_low, normed_one,
            queries_two, inverse_one, mixed_two, exact_two, scale_two, keys_two, values_two,
        ) = forward
        keys_two, values_two = keys_two.reshape(-1, D), values_two.reshape(-1, D)
    else:
        tokens_float = tokens.astype(F32)
        queries_one = ((product(tokens, query_self) + shift_rows[0]) * 0.125).astype(BF16)
        keys_one = product(tokens, key_self).astype(BF16)
        values_one = (product(tokens, value_self) + shift_rows[1]).astype(BF16)
        mixed_one, exact_one, scale_one = attend_forward(
            True, DEC, own_dec, bases, queries_one, keys_one, values_one
        )
        resid_one = tokens_float + product(mixed_one, output_self) + shift_rows[2]
        hidden_one, normed_one, inverse_one = norm_forward(resid_one, gain_rows[0], shift_rows[7])
        hidden_one_low = hidden_one.astype(BF16)
        queries_two = ((product(hidden_one_low, query_cross) + shift_rows[3]) * 0.125).astype(BF16)
        keys_two = product(memory_flat, key_cross).astype(BF16)
        values_two = (product(memory_flat, value_cross) + shift_rows[4]).astype(BF16)
        mixed_two, exact_two, scale_two = attend_forward(
            False, mem_local, own_mem, bases, queries_two, keys_two, values_two
        )
    resid_two = hidden_one + product(mixed_two, output_cross) + shift_rows[5]
    hidden_two, normed_two, inverse_two = norm_forward(resid_two, gain_rows[1], shift_rows[8])
    hidden_two_low = hidden_two.astype(BF16)
    inner_pre = product(hidden_two_low, feed_up) + inner_shift
    cdf_part = 0.5 * (1.0 + jax.scipy.special.erf(inner_pre * half_root))
    active_low = (inner_pre * cdf_part).astype(BF16)
    resid_three = hidden_two + product(active_low, feed_down) + shift_rows[6]
    layer_out, normed_three, inverse_three = norm_forward(resid_three, gain_rows[2], shift_rows[9])

    grad_three, gain_grad_three, shift_grad_three = norm_backward(
        cotangent.astype(F32), normed_three, inverse_three, gain_rows[2]
    )
    grad_down = grad_three.astype(BF16)

    out_bias_grad = column_sums(grad_down)
    slope = cdf_part + inner_pre * jnp.exp(-0.5 * inner_pre * inner_pre) * normal_peak
    blocks = tuple(
        weight.shape
        for weight in (
            feed_out, feed_in, cross_out, cross_key, cross_value, cross_query, self_out, self_query, self_key, self_value,
        )
    )
    if by_kernel:
        vector_rows = (
            jnp.zeros((24, D), F32).at[6].set(out_bias_grad).at[9].set(shift_grad_three).at[12].set(gain_grad_three)
        )
        big = (
            active_low, grad_down, hidden_two_low, slope, feed_down, feed_up, grad_three, normed_two, mixed_two,
            queries_two, exact_two, scale_two, tokens, mixed_one, hidden_one_low, normed_one, queries_one, keys_one,
            values_one, keys_two, values_two, memory_flat, exact_one, scale_one, output_cross, key_cross, value_cross,
            query_cross, output_self, query_self, key_self, value_self,
        )
        small = (inverse_one, inverse_two, gain_rows, jnp.stack([own_dec, own_mem]), vector_rows)
        grads, tokens_grad, sums, memory_back = scatter_by_kernel(
            big, small, blocks, members, item_count, mem_local
        )
        memory_grad = memory_back.astype(F32)
        (
            feed_down_grad, feed_up_grad, output_cross_grad, key_cross_grad, value_cross_grad, query_cross_grad,
            output_self_grad, query_self_grad, key_self_grad, value_self_grad,
        ) = grads
        shifts_grad = sums[: shifts.shape[0]]
        gains_grad = sums[shifts.shape[0] : bias_start]
        bias_grad = sums[bias_start : bias_start + bias_rows].reshape(-1)
    else:
        grad_active = right_product(grad_down, feed_down)
        grad_inner = (grad_active * slope).astype(BF16)
        inner_bias_grad = column_sums(grad_inner)
        grad_hidden_two = grad_three + right_product(grad_inner, feed_up)
        grad_two, gain_grad_two, shift_grad_two = norm_backward(
            grad_hidden_two, normed_two, inverse_two, gain_rows[1]
        )
        grad_cross_branch = grad_two.astype(BF16)
        cross_out_bias_grad = column_sums(grad_cross_branch)
        grad_mixed_two = right_product(grad_cross_branch, output_cross)
        query_grad_two, key_grad_two, value_grad_two = attend_backward(
            False, mem_local, own_mem, bases, queries_two, keys_two, values_two, grad_mixed_two, exact_two, scale_two
        )
        query_grad_two = query_grad_two * jnp.asarray(0.125, BF16)

        memory_part = (
            right_product(key_grad_two, key_cross) + right_product(value_grad_two, value_cross)
        ).astype(BF16).reshape(item_count, members, mem_local, D)
        cross_value_bias_grad = column_sums(value_grad_two)
        cross_query_bias_grad = column_sums(query_grad_two)
        grad_hidden_one = grad_two + right_product(query_grad_two, query_cross)
        grad_one, gain_grad_one, shift_grad_one = norm_backward(
            grad_hidden_one, normed_one, inverse_one, gain_rows[0]
        )
        grad_self_branch = grad_one.astype(BF16)
        self_out_bias_grad = column_sums(grad_self_branch)
        grad_mixed_one = right_product(grad_self_branch, output_self)
        query_grad_one, key_grad_one, value_grad_one = attend_backward(
            True, DEC, own_dec, bases, queries_one, keys_one, values_one, grad_mixed_one, exact_one, scale_one
        )
        query_grad_one = query_grad_one * jnp.asarray(0.125, BF16)
        pairs = (
            (active_low, grad_down),
            (hidden_two_low, grad_inner),
            (mixed_two, grad_cross_branch),
            (memory_flat, key_grad_two),
            (memory_flat, value_grad_two),
            (hidden_one_low, query_grad_two),
            (mixed_one, grad_self_branch),
            (tokens, query_grad_one),
            (tokens, key_grad_one),
            (tokens, value_grad_one),
        )
        grads, memory_back = scatter_by_collectives(pairs, blocks, memory_part, row, member, items_count, members)
        (
            feed_down_grad, feed_up_grad, output_cross_grad, key_cross_grad, value_cross_grad, query_cross_grad,
            output_self_grad, query_self_grad, key_self_grad, value_self_grad,
        ) = grads
        memory_grad = lax.dynamic_update_slice_in_dim(
            memory_back.astype(F32), memory_part[:, 0].astype(F32), member * item_count, 0
        )
        tokens_grad = (
            grad_one
            + right_product(query_grad_one, query_self)
            + right_product(key_grad_one, key_self)
            + right_product(value_grad_one, value_self)
        )
        vectors = jnp.concatenate(
            [
                column_sums(query_grad_one),
                column_sums(value_grad_one),
                self_out_bias_grad,
                cross_query_bias_grad,
                cross_value_bias_grad,
                cross_out_bias_grad,
                out_bias_grad,
                shift_grad_one,
                shift_grad_two,
                shift_grad_three,
                gain_grad_one,
                gain_grad_two,
                gain_grad_three,
                inner_bias_grad,
            ]
        )
        vectors = lax.psum(vectors.reshape(-1, 128), ("items", "mem")).reshape(-1)
        shift_count = shifts.shape[0] * D
        gain_count = gains.shape[0] * D
        shift_width, gain_width, bias_width = shifts.shape[1], gains.shape[1], inner_bias.shape[0]
        shifts_grad = lax.dynamic_slice_in_dim(
            vectors[:shift_count].reshape(-1, D), row * shift_width, shift_width, 1
        )
        gains_grad = lax.dynamic_slice_in_dim(
            vectors[shift_count : shift_count + gain_count].reshape(-1, D), row * gain_width, gain_width, 1
        )
        bias_grad = lax.dynamic_slice_in_dim(vectors[shift_count + gain_count :], row * bias_width, bias_width)
    return (
        layer_out,
        tokens_grad,
        memory_grad,
        query_self_grad,
        key_self_grad,
        value_self_grad,
        output_self_grad,
        query_cross_grad,
        key_cross_grad,
        value_cross_grad,
        output_cross_grad,
        feed_up_grad,
        feed_down_grad,
        shifts_grad,
        gains_grad,
        bias_grad,
    )


def solution(mesh):
    tiles = P("items", "mem")
    rows = P(("items", "mem"), None)
    blocks = P("items", "mem", None)
    return jax.shard_map(
        functools.partial(body, mesh.shape["items"], mesh.shape["mem"]),
        mesh=mesh,
        in_specs=(rows, blocks, rows, P("items"), P("items"))
        + (tiles,) * 10
        + (P(None, "items"), P(None, "items"), P("items")),
        out_specs=(rows, rows, blocks) + (tiles,) * 10 + (P(None, "items"), P(None, "items"), P("items")),
        check_vma=False,
    )
```
